32 devices in a mesh: group: 2 (over y), context: 4 (over z), head: 4 (over x, core).
Axes of the slice: x: 2, y: 2, z: 4, core: 2. Of those that a mesh axis runs over, the one named last changes fastest.
Arguments:
- dn_query: bfloat16 [1024, 2048], P(('group', 'context'), 'head'), parts along dimension 0, may hold values from -6 to 6
- dn_key: bfloat16 [1024, 2048], P(('group', 'context'), 'head'), parts along dimension 0, may hold values from -6 to 6
- dn_value: bfloat16 [1024, 4096], P(('group', 'context'), 'head'), parts along dimension 0, may hold values from -6 to 6
- dn_gate: bfloat16 [1024, 4096], P(('group', 'context'), 'head'), parts along dimension 0, may hold values from -6 to 6
- dn_beta_logit: float32 [1024, 32], P(('group', 'context'), 'head'), parts along dimension 0, may hold values from -6 to 6
- dn_decay: float32 [1024, 32], P(('group', 'context'), 'head'), parts along dimension 0, may hold values from -1 to 0
- dn_norm_gain: float32 [128], replicated, may hold values from 0.1 to 1.9
- prefix_state: bfloat16 [4, 32, 128, 128], P('group', 'head', 'context'), parts along dimension 0, may hold values from -6 to 6
- at_query: bfloat16 [1024, 4096], P(('group', 'context'), 'head'), parts along dimension 0, may hold values from -6 to 6
- at_gate: bfloat16 [1024, 4096], P(('group', 'context'), 'head'), parts along dimension 0, may hold values from -6 to 6
- at_key: bfloat16 [1024, 512], P(('group', 'context')), parts along dimension 0, may hold values from -6 to 6
- at_value: bfloat16 [1024, 512], P(('group', 'context')), parts along dimension 0, may hold values from -6 to 6
- prefix_key: bfloat16 [16, 64, 512], P(('group', 'context')), parts along dimension 0, may hold values from -6 to 6
- prefix_value: bfloat16 [16, 64, 512], P(('group', 'context')), parts along dimension 0, may hold values from -6 to 6
- req_len: int32 [8], P('group'), parts along dimension 0, may hold values from 1 to 256, 512 in all
- req_prefix: int32 [8], P('group'), parts along dimension 0, may hold values from 0 to 1, as said below
- req_offset: int32 [8], P('group'), parts along dimension 0, may hold values from 64 to 256, as said below
- block_table: int32 [16], P('group'), parts along dimension 0, may hold values from 0 to 7, each once
Outputs:
- dn_out: bfloat16 [1024, 4096], P(('group', 'context'), 'head'), parts along dimension 0
- at_out: bfloat16 [1024, 4096], P(('group', 'context'), 'head'), parts along dimension 0
The draws below stay inside these ranges and needn't reach their ends.
There are 2 independent parts, one for each index of `group`. The reference program is written for one: setup_inputs(seed, part) draws one part's arguments, and reference() takes and returns one part's arrays. A program takes and returns all parts, laid end to end along the dimension named above; an argument that names none is the same for every part. Nothing has to cross between parts.
Inputs may be any that keep to these rules, and one draw needn't show every extreme that they name: `req_len`: requests lie one after another in row order; the longest has exactly 256 new tokens. `req_prefix`: every prefix is extended by one or more requests. `req_offset`: equal for the requests of one prefix: the number of its cached positions; one prefix holds 256, another from a quarter to a half of 256. `block_table`: entry p * 4 + j is the slot of block j of prefix p; every slot once.
All inputs are finite; a program needn't handle non-finite values.
Results may differ from the reference program's by a relative error of at most 0.011.
Values may be sent and summed in bfloat16 or wider, within the bound.
A program may use at most 128 MiB of HBM per device.

```python
import math
import jax
import jax.numpy as jnp
import numpy as np
from jax import lax

VH = 32
KH = 16
DK = 128
DV = 128
HQ = 16
KVH = 2
HD = 256
ROT = 64
TOK_DEV = 128
REQS = 4
PREF = 2
BLK = 64
NEW_ITEM_COUNT = 512
BLOCKS = 8
PBLK = 4
PLEN = 256
MOST = 256


def request_layout(key, part):
    base = jax.random.fold_in(key, 7101)
    order = jax.random.permutation(jax.random.fold_in(base, 1), REQS)
    spare = jax.random.randint(jax.random.fold_in(base, 2), (REQS,), 0, PREF)
    listed = jnp.where(jnp.arange(REQS) < PREF, jnp.arange(REQS) % PREF, spare)
    prefix = listed[order].astype(jnp.int32)
    sizes = jax.random.randint(jax.random.fold_in(base, 3), (PREF,), PLEN // 4, PLEN + 1)
    longest = prefix[0]
    shortest = (longest + 1 + jax.random.randint(jax.random.fold_in(base, 4), (), 0, PREF - 1)) % PREF
    half_span = max(PLEN // 4 // 2, 1)
    short_size = PLEN // 4 + 2 * jax.random.randint(jax.random.fold_in(base, 5), (), 0, half_span) + jnp.asarray(part, jnp.int32) % 2
    sizes = jnp.where(jnp.arange(PREF) == longest, PLEN, sizes)
    sizes = jnp.where(jnp.arange(PREF) == shortest, short_size, sizes)
    return (prefix, sizes[prefix].astype(jnp.int32))


def draw_req_prefix(key, part):
    return request_layout(key, part)[0]


def draw_req_offset(key, part):
    return request_layout(key, part)[1]


def draw_dn_decay(key, part):
    search_handles = jax.random.split(jax.random.fold_in(key, 3301), 7)
    fast_share = 0.5
    fast = jax.random.uniform(search_handles[0], (VH,)) < fast_share
    fast_rate = jnp.exp(jax.random.uniform(search_handles[1], (VH,), minval=math.log(1.0 / 50.0), maxval=math.log(1.0 / 30.0)))
    slow_rate = jnp.exp(jax.random.uniform(search_handles[2], (VH,), minval=math.log(0.1), maxval=0.0)) * math.log(10.0) / (4.0 * MOST)
    incoming_speed = jnp.where(fast, fast_rate, slow_rate)
    approximate_guess = jnp.exp(jax.random.uniform(search_handles[3], (NEW_ITEM_COUNT, VH), minval=math.log(0.7), maxval=math.log(1.4)))
    accelerator_scaling = jnp.exp(jax.random.uniform(search_handles[4], (NEW_ITEM_COUNT // TOK_DEV, 1, VH), minval=math.log(0.5), maxval=math.log(2.0)))
    accelerator_scaling = jnp.broadcast_to(accelerator_scaling, (NEW_ITEM_COUNT // TOK_DEV, TOK_DEV, VH)).reshape(NEW_ITEM_COUNT, VH)
    piece_waves = max(2, NEW_ITEM_COUNT // 1024)
    vacant_places = jax.random.randint(search_handles[5], (piece_waves,), 0, NEW_ITEM_COUNT)
    leading_absent = jnp.log(1.0 - jax.random.uniform(search_handles[6], (piece_waves,), minval=0.2, maxval=0.5))
    leading_found = (jnp.arange(NEW_ITEM_COUNT)[:, None] == vacant_places[None, :]).astype(jnp.float32)
    piece_wave = jnp.sum(leading_found * leading_absent[None, :], axis=1)
    return (-incoming_speed[None, :] * approximate_guess * accelerator_scaling + piece_wave[:, None]).astype(jnp.float32)


def drawn_values(key, heads):
    return jnp.clip(jax.random.normal(key, (NEW_ITEM_COUNT, heads, HD)), -6.0, 6.0)


def draw_at_query(key, part):
    drawn = drawn_values(jax.random.fold_in(key, 11), HQ)
    return drawn.reshape(NEW_ITEM_COUNT, HQ * HD).astype(jnp.bfloat16)


def draw_at_key(key, part):
    drawn = drawn_values(jax.random.fold_in(key, 12), KVH)
    return drawn.reshape(NEW_ITEM_COUNT, KVH * HD).astype(jnp.bfloat16)


def steps_of(own_key, dims, cuts, low, largest):
    def one(dim, blocks):
        draws = jax.random.uniform(jax.random.fold_in(jax.random.fold_in(own_key, 6), dim), (blocks,), jnp.float32, low / len(cuts), largest / len(cuts))
        return jnp.repeat(jnp.exp(draws), dims[dim] // blocks).reshape((-1,) + (1,) * (len(dims) - dim - 1))

    level = one(*cuts[0])
    for cut in cuts[1:]:
        level = level * one(*cut)
    return level


def split_up(amount, total, most, skew):
    loads = [(1 << 20) // math.isqrt(rank ** skew) + 1 for rank in range(2, amount + 1)]
    spare, given = total - most - (amount - 1), [1] * (amount - 1)
    while spare > 0:
        movable = [i for i in range(amount - 1) if given[i] < most]
        whole, remaining = sum([loads[i] for i in movable]), spare
        for i in movable:
            extra = min(most - given[i], max(1, remaining * loads[i] // whole), spare)
            given[i] = given[i] + extra
            spare = spare - extra
    return np.array([most] + given)


def ragged_sizes(rng, amount, total, most, slope):
    if amount == 2:
        one = jax.random.randint(rng, (), max(1, total - most), min(most, total - 1) + 1)
        return jnp.stack([one, total - one])
    tallies = jnp.asarray(split_up(amount, total, most, slope), jnp.int32)
    twos = (amount - 1) // 2
    source_of, receiver = tallies[1:1 + 2 * twos:2], tallies[2:2 + 2 * twos:2]
    slack = jnp.minimum(source_of - 1, most - receiver)
    moved = jax.random.randint(jax.random.fold_in(rng, 1), (twos,), 0, 1 << 20) % (slack + 1)
    tallies = tallies.at[1:1 + 2 * twos:2].set(source_of - moved).at[2:2 + 2 * twos:2].set(receiver + moved)
    return tallies[jax.random.permutation(jax.random.fold_in(rng, 2), amount)]


def gaussian(stream_key, dims, deviation, limit, pieces=(), held_as=jnp.bfloat16):
    factor_of = steps_of(stream_key, dims, pieces, -0.22, 0.18) if pieces else 1.0
    entries = jax.random.normal(stream_key, dims, jnp.float32) * deviation * factor_of
    return jnp.minimum(jnp.maximum(entries, -limit), limit).astype(held_as)


def setup_inputs(seed: int = 0, part: int = 0) -> dict:
    streams_of = jax.random.split(jax.random.key(seed), 19)
    own_keys = jax.random.split(jax.random.fold_in(streams_of[18], part), 19)
    dn_query = gaussian(own_keys[0], (NEW_ITEM_COUNT, KH * DK), 1.0, 6.0, ((0, 4), (1, 4)))
    dn_key = gaussian(own_keys[1], (NEW_ITEM_COUNT, KH * DK), 1.0, 6.0, ((0, 4), (1, 4)))
    dn_value = gaussian(own_keys[2], (NEW_ITEM_COUNT, VH * DV), 1.0, 6.0, ((0, 4), (1, 4)))
    dn_gate = gaussian(own_keys[3], (NEW_ITEM_COUNT, VH * DV), 1.0, 6.0, ((0, 4), (1, 4)))
    dn_beta_logit = gaussian(own_keys[4], (NEW_ITEM_COUNT, VH), 1.5, 6.0, ((0, 4), (1, 4)), jnp.float32)
    dn_decay = draw_dn_decay(jax.random.fold_in(jax.random.fold_in(streams_of[18], part), 71), part)
    dn_norm_gain = jnp.clip(1.0 + 0.18 * jax.random.normal(streams_of[6], (DV,), jnp.float32), 0.1, 1.9)
    prefix_state = gaussian(own_keys[7], (PREF, VH, DV, DK), 1.0, 6.0, ((1, 4), (2, 4)))
    at_query = draw_at_query(jax.random.fold_in(jax.random.fold_in(streams_of[18], part), 71), part)
    at_gate = gaussian(own_keys[9], (NEW_ITEM_COUNT, HQ * HD), 1.0, 6.0, ((0, 4), (1, 4)))
    at_key = draw_at_key(jax.random.fold_in(jax.random.fold_in(streams_of[18], part), 71), part)
    at_value = gaussian(own_keys[11], (NEW_ITEM_COUNT, KVH * HD), 1.0, 6.0, ((0, 4),))
    prefix_key = gaussian(own_keys[12], (BLOCKS, BLK, KVH * HD), 1.0, 6.0, ((0, 4),))
    prefix_value = gaussian(own_keys[13], (BLOCKS, BLK, KVH * HD), 1.0, 6.0, ((0, 4),))
    req_len = ragged_sizes(own_keys[14], REQS, NEW_ITEM_COUNT, MOST, 2).astype(jnp.int32)
    req_prefix = draw_req_prefix(jax.random.fold_in(jax.random.fold_in(streams_of[18], part), 71), part)
    req_offset = draw_req_offset(jax.random.fold_in(jax.random.fold_in(streams_of[18], part), 71), part)
    block_table = jax.random.permutation(own_keys[17], BLOCKS).astype(jnp.int32)
    return {"dn_query": dn_query, "dn_key": dn_key, "dn_value": dn_value, "dn_gate": dn_gate, "dn_beta_logit": dn_beta_logit, "dn_decay": dn_decay, "dn_norm_gain": dn_norm_gain, "prefix_state": prefix_state, "at_query": at_query, "at_gate": at_gate, "at_key": at_key, "at_value": at_value, "prefix_key": prefix_key, "prefix_value": prefix_value, "req_len": req_len, "req_prefix": req_prefix, "req_offset": req_offset, "block_table": block_table}


ROPE_THETA = 10000000.0
YARN_FACTOR = 4.0
YARN_ANCHOR = 262144.0
NEG_LARGE = -1e+30
HIGH = lax.Precision.HIGHEST

def yarn_tables(positions, rotary):
    half = rotary // 2
    log_theta = math.log(ROPE_THETA)
    lower = max(math.floor(rotary * math.log(YARN_ANCHOR / (64.0 * math.pi)) / (2.0 * log_theta)), 0)
    upper = min(math.ceil(rotary * math.log(YARN_ANCHOR / (2.0 * math.pi)) / (2.0 * log_theta)), rotary - 1)
    spread = float(upper - lower) if upper > lower else 0.001
    index = jnp.arange(half, dtype=jnp.float32)
    plain_frequency = jnp.exp(index * (-2.0 * log_theta / rotary))
    keep = 1.0 - jnp.clip((index - lower) / spread, 0.0, 1.0)
    frequency = plain_frequency * keep + plain_frequency / YARN_FACTOR * (1.0 - keep)
    angles = positions.astype(jnp.float32)[:, None] * frequency[None, :]
    attention_factor = 0.1 * math.log(YARN_FACTOR) + 1.0
    return (jnp.cos(angles) * attention_factor, jnp.sin(angles) * attention_factor)

def rotate(values, cosines, sines, rotary):
    half = rotary // 2
    first = values[..., :half]
    second = values[..., half:rotary]
    cosines = cosines[:, None, :]
    sines = sines[:, None, :]
    return jnp.concatenate([first * cosines - second * sines, second * cosines + first * sines, values[..., rotary:]], axis=-1)

def unit_rows(values):
    return values * lax.rsqrt(lax.optimization_barrier(jnp.sum(values * values, axis=-1, keepdims=True)) + 1e-06)

def row_layout(rows, req_len, req_prefix, req_offset):
    starts = (jnp.cumsum(req_len) - req_len).astype(jnp.int32)
    leading_found = (starts[None, :] <= rows[:, None]).astype(jnp.int32)
    segment = (lax.optimization_barrier(jnp.sum(leading_found, axis=1)) - 1).astype(jnp.int32)
    choose = (segment[:, None] == jnp.arange(req_len.shape[0], dtype=jnp.int32)[None, :]).astype(jnp.int32)
    first = lax.optimization_barrier(jnp.sum(choose * starts[None, :], axis=1)).astype(jnp.int32)
    prefix = lax.optimization_barrier(jnp.sum(choose * req_prefix[None, :], axis=1)).astype(jnp.int32)
    offset = lax.optimization_barrier(jnp.sum(choose * req_offset[None, :], axis=1)).astype(jnp.int32)
    return (segment, first, prefix, offset, (offset + rows - first).astype(jnp.int32))

def reference(dn_query, dn_key, dn_value, dn_gate, dn_beta_logit, dn_decay, dn_norm_gain, prefix_state, at_query, at_gate, at_key, at_value, prefix_key, prefix_value, req_len, req_prefix, req_offset, block_table):
    rows = jnp.arange(NEW_ITEM_COUNT, dtype=jnp.int32)
    segment, first, prefix, offset, position = row_layout(rows, req_len, req_prefix, req_offset)
    query = jnp.repeat(unit_rows(dn_query.reshape(NEW_ITEM_COUNT, KH, DK).astype(jnp.float32)) * DK ** (-0.5), VH // KH, axis=1)
    key = jnp.repeat(unit_rows(dn_key.reshape(NEW_ITEM_COUNT, KH, DK).astype(jnp.float32)), VH // KH, axis=1)
    value = dn_value.reshape(NEW_ITEM_COUNT, VH, DV).astype(jnp.float32)
    beta = jax.nn.sigmoid(dn_beta_logit)
    begins = rows == first
    identity = jnp.broadcast_to(jnp.eye(DK, dtype=jnp.float32), (VH, DK, DK))

    def advance(carry, inputs):
        state, transfer = carry
        query_row, key_row, value_row, beta_row, decay_row, begin_row = inputs
        state = jnp.where(begin_row, jnp.zeros_like(state), state)
        transfer = jnp.where(begin_row, identity, transfer)
        factor = jnp.exp(decay_row)[:, None, None]
        strength = beta_row[:, None, None]
        state_key = jnp.einsum('hvk,hk->hv', state, key_row, precision=HIGH)
        state = factor * (state - strength * state_key[:, :, None] * key_row[:, None, :]) + strength * value_row[:, :, None] * key_row[:, None, :]
        transfer_key = jnp.einsum('hjk,hk->hj', transfer, key_row, precision=HIGH)
        transfer = factor * (transfer - strength * transfer_key[:, :, None] * key_row[:, None, :])
        local_row = jnp.einsum('hvk,hk->hv', state, query_row, precision=HIGH)
        reach_row = jnp.einsum('hjk,hk->hj', transfer, query_row, precision=HIGH)
        return ((state, transfer), (local_row, reach_row))
    initial = (jnp.zeros((VH, DV, DK), jnp.float32), identity)
    unused, (local_out, reach) = lax.scan(advance, initial, (query, key, value, beta, dn_decay, begins))
    weights = reach.astype(jnp.bfloat16)

    def state_term(block):
        owners = lax.dynamic_slice_in_dim(prefix, block * 8, 8)
        vectors = lax.dynamic_slice_in_dim(weights, block * 8, 8, 0)
        states = jnp.take(prefix_state, owners, axis=0).astype(jnp.float32)
        return jnp.einsum('thvk,thk->thv', states, vectors.astype(jnp.float32), precision=HIGH)
    carried = lax.map(state_term, jnp.arange(NEW_ITEM_COUNT // 8, dtype=jnp.int32)).reshape(NEW_ITEM_COUNT, VH, DV)
    core = local_out + carried
    normed = core * lax.rsqrt(lax.optimization_barrier(jnp.mean(core * core, axis=-1, keepdims=True)) + 1e-06)
    gate = dn_gate.reshape(NEW_ITEM_COUNT, VH, DV).astype(jnp.float32)
    dn_out = (normed * dn_norm_gain * jax.nn.silu(gate)).reshape(NEW_ITEM_COUNT, VH * DV).astype(jnp.bfloat16)
    cosines, sines = yarn_tables(position, ROT)
    group = HQ // KVH
    query_rot = rotate(at_query.reshape(NEW_ITEM_COUNT, HQ, HD).astype(jnp.float32), cosines, sines, ROT).astype(jnp.bfloat16)
    query_rot = query_rot.reshape(NEW_ITEM_COUNT, KVH, group, HD)
    key_rot = rotate(at_key.reshape(NEW_ITEM_COUNT, KVH, HD).astype(jnp.float32), cosines, sines, ROT).astype(jnp.bfloat16)
    value_new = at_value.reshape(NEW_ITEM_COUNT, KVH, HD)
    order = block_table.reshape(PREF * PBLK)
    cached_keys = jnp.take(prefix_key, order, axis=0).reshape(PREF * PLEN, KVH, HD).astype(jnp.float32)
    cached_values = jnp.take(prefix_value, order, axis=0).reshape(PREF * PLEN, KVH, HD).astype(jnp.float32)
    flat_index = jnp.arange(PREF * PLEN, dtype=jnp.int32)
    flat_owner = flat_index // PLEN
    flat_place = flat_index % PLEN
    padded_keys = jnp.concatenate([jnp.zeros((MOST, KVH, HD), jnp.bfloat16), key_rot], axis=0)
    padded_values = jnp.concatenate([jnp.zeros((MOST, KVH, HD), jnp.bfloat16), value_new], axis=0)
    padded_segment = jnp.concatenate([jnp.full((MOST,), -1, jnp.int32), segment])
    window = MOST + TOK_DEV - 1
    scale = HD ** (-0.5)

    def attend(block):
        begin = block * TOK_DEV
        queries = lax.dynamic_slice_in_dim(query_rot, begin, TOK_DEV, 0).astype(jnp.float32)
        owners = lax.dynamic_slice_in_dim(prefix, begin, TOK_DEV)
        limits = lax.dynamic_slice_in_dim(offset, begin, TOK_DEV)
        own_segment = lax.dynamic_slice_in_dim(segment, begin, TOK_DEV)
        own_rows = begin + jnp.arange(TOK_DEV, dtype=jnp.int32)
        near_keys = lax.dynamic_slice_in_dim(padded_keys, begin + 1, window, 0).astype(jnp.float32)
        near_values = lax.dynamic_slice_in_dim(padded_values, begin + 1, window, 0).astype(jnp.float32)
        near_segment = lax.dynamic_slice_in_dim(padded_segment, begin + 1, window)
        near_rows = begin + 1 - MOST + jnp.arange(window, dtype=jnp.int32)
        old_scores = jnp.einsum('tkgd,nkd->tkgn', queries, cached_keys, precision=HIGH) * scale
        new_scores = jnp.einsum('tkgd,nkd->tkgn', queries, near_keys, precision=HIGH) * scale
        old_mask = (flat_owner[None, :] == owners[:, None]) & (flat_place[None, :] < limits[:, None])
        old_seen = jnp.broadcast_to(old_mask[:, None, None, :], old_scores.shape)
        new_mask = (near_segment[None, :] == own_segment[:, None]) & (near_rows[None, :] <= own_rows[:, None])
        new_seen = jnp.broadcast_to(new_mask[:, None, None, :], new_scores.shape)
        peak = jnp.maximum(lax.optimization_barrier(jnp.max(jnp.where(old_seen, old_scores, NEG_LARGE), axis=-1)), lax.optimization_barrier(jnp.max(jnp.where(new_seen, new_scores, NEG_LARGE), axis=-1)))[..., None]
        old_numer = jnp.where(old_seen, jnp.exp(old_scores - peak), 0.0)
        new_numer = jnp.where(new_seen, jnp.exp(new_scores - peak), 0.0)
        total = lax.optimization_barrier(jnp.sum(old_numer, axis=-1)) + lax.optimization_barrier(jnp.sum(new_numer, axis=-1))
        old_round = lax.optimization_barrier(old_numer.astype(jnp.bfloat16)).astype(jnp.float32)
        new_round = lax.optimization_barrier(new_numer.astype(jnp.bfloat16)).astype(jnp.float32)
        summed = jnp.einsum('tkgn,nkd->tkgd', old_round, cached_values, precision=HIGH)
        summed = summed + jnp.einsum('tkgn,nkd->tkgd', new_round, near_values, precision=HIGH)
        return summed / total[..., None]
    attention = lax.map(attend, jnp.arange(NEW_ITEM_COUNT // TOK_DEV, dtype=jnp.int32)).reshape(NEW_ITEM_COUNT, HQ, HD)
    gate_att = at_gate.reshape(NEW_ITEM_COUNT, HQ, HD).astype(jnp.float32)
    at_out = (attention * jax.nn.sigmoid(gate_att)).reshape(NEW_ITEM_COUNT, HQ * HD).astype(jnp.bfloat16)
    return (dn_out, at_out)
```

```python
import math

import jax
import jax.numpy as jnp
from jax import lax
from jax.experimental import pallas as pl
from jax.experimental.pallas import tpu as pltpu
from jax.sharding import PartitionSpec as P

VH = 32
KH = 16
DK = 128
DV = 128
HQ = 16
KVH = 2
HD = 256
ROT = 64


ROPE_THETA = 10000000.0
YARN_FACTOR = 4.0
YARN_ANCHOR = 262144.0
NEG_LARGE = -1e30
HIGH = lax.Precision.HIGHEST


def chain_kernel(size, map_ref, add_ref, into_ref, held, leaving, send_sem, recv_sem):
    me = lax.axis_index("context")
    heads = map_ref.shape[0]
    barrier = pltpu.get_barrier_semaphore()
    after, before = lax.rem(me + 1, size), lax.rem(me + size - 1, size)
    for neighbour in (before, after):
        pl.semaphore_signal(barrier, inc=1, device_id={"context": neighbour})
    pl.semaphore_wait(barrier, 2)

    def sent(h):
        return pltpu.make_async_remote_copy(
            src_ref=leaving.at[h],
            dst_ref=held.at[h],
            send_sem=send_sem.at[h],
            recv_sem=recv_sem.at[h],
            device_id={"context": after},
        )

    @pl.when(me == 0)
    def _():
        held[...] = jnp.zeros_like(held)

    for h in range(heads):

        @pl.when(me > 0)
        def _(h=h):
            sent(h).wait_recv()

        leaving[h] = (
            jnp.dot(held[h], map_ref[h], preferred_element_type=jnp.float32) + add_ref[h]
        ).astype(jnp.bfloat16)

        @pl.when(me < size - 1)
        def _(h=h):
            sent(h).start()

    into_ref[...] = held[...]

    @pl.when(me < size - 1)
    def _():
        for h in range(heads):
            sent(h).wait_send()


def chain(carry_map, carry_add, size):
    heads = carry_map.shape[0]
    return pl.pallas_call(
        lambda *refs: chain_kernel(size, *refs),
        out_shape=jax.ShapeDtypeStruct(carry_add.shape, jnp.bfloat16),
        in_specs=[pl.BlockSpec(memory_space=pltpu.VMEM)] * 2,
        out_specs=pl.BlockSpec(memory_space=pltpu.VMEM),
        scratch_shapes=[
            pltpu.VMEM(carry_add.shape, jnp.bfloat16),
            pltpu.VMEM(carry_add.shape, jnp.bfloat16),
            pltpu.SemaphoreType.DMA((heads,)),
            pltpu.SemaphoreType.DMA((heads,)),
        ],
        compiler_params=pltpu.CompilerParams(collective_id=1, has_side_effects=True),
    )(carry_map, carry_add)


def from_others(x, axis, size, span):
    return [
        lax.ppermute(
            x, axis, [(i, i // span * span + (i + step) % span) for i in range(size)]
        )
        for step in range(1, span)
    ]


def halves(x):
    high = x.astype(jnp.bfloat16)
    return high, (x - high.astype(jnp.float32)).astype(jnp.bfloat16)


def dot1(a, b, contract=((1,), (0,))):
    return lax.dot_general(a, b, (contract, ((), ())), preferred_element_type=jnp.float32)


def dot2(a, exact):
    high, low = halves(a)
    return dot1(high, exact) + dot1(low, exact)


def dot3(a, b):
    a_high, a_low = halves(a)
    b_high, b_low = halves(b)
    return dot1(a_high, b_high) + (dot1(a_high, b_low) + dot1(a_low, b_high))


def local_kernel(
    query_ref, key_ref, value_ref, logit_ref, logit_row_ref, decay_ref, decay_row_ref,
    seg_ref, seg_row_ref, local_ref, reach_ref, map_ref, add_ref,
):
    tokens = query_ref.shape[0]
    heads = local_ref.shape[0]
    share = VH // KH
    seg, seg_row = seg_ref[...], seg_row_ref[...]
    row = lax.broadcasted_iota(jnp.int32, (tokens, tokens), 0)
    col = lax.broadcasted_iota(jnp.int32, (tokens, tokens), 1)
    same = seg == seg_row
    causal = same & (row >= col)
    strict = same & (row > col)
    eye = row == col
    causal_f = causal.astype(jnp.float32)
    run = lax.dot_general(
        causal_f, decay_ref[...], (((1,), (0,)), ((), ())),
        precision=HIGH, preferred_element_type=jnp.float32,
    )
    run_row = lax.dot_general(
        decay_row_ref[...], causal_f, (((1,), (1,)), ((), ())),
        precision=HIGH, preferred_element_type=jnp.float32,
    )
    beta, beta_row = jax.nn.sigmoid(logit_ref[...]), jax.nn.sigmoid(logit_row_ref[...])
    start, start_row = jnp.exp(run), jnp.exp(run_row)
    tail = seg_row == seg_row[:, tokens - 1 : tokens]
    end_row = jnp.where(
        tail, jnp.exp(jnp.where(tail, run_row[:, tokens - 1 : tokens] - run_row, 0.0)), 0.0
    )
    keys, grams, mixes, scaled, inv_rows = [], [], [], [], []
    for g in range(heads // share):
        k = key_ref[:, g * DK : (g + 1) * DK]
        q = query_ref[:, g * DK : (g + 1) * DK]
        gram = dot1(k, k, ((1,), (1,)))
        cross = dot1(q, k, ((1,), (1,)))
        squares = jnp.where(eye, gram, 0.0)
        inv = lax.rsqrt(jnp.sum(squares, axis=1, keepdims=True) + 1e-06)
        inv_row = lax.rsqrt(jnp.sum(squares, axis=0, keepdims=True) + 1e-06)
        q_f = q.astype(jnp.float32)
        inv_q = lax.rsqrt(jnp.sum(q_f * q_f, axis=1, keepdims=True) + 1e-06) * DK ** (-0.5)
        keys.append(k)
        inv_rows.append(inv_row)
        grams.append(gram * inv * inv_row)
        mixes.append(cross * inv_q * inv_row)
        scaled.append(q_f * inv_q)
    lowers, inverses, mixing = [], [], []
    for h in range(heads):
        gaps = run[:, h : h + 1] - run_row[h : h + 1, :]
        decay_mat = jnp.where(causal, jnp.exp(jnp.where(causal, gaps, 0.0)), 0.0)
        mixing.append(decay_mat * mixes[h // share])
        lower = jnp.where(strict, beta[:, h : h + 1] * grams[h // share] * decay_mat, 0.0)
        lowers.append(lower)
        inverses.append(
            jnp.where(eye, 1.0, 0.0) - jnp.where(row // 2 == col // 2, lower, 0.0)
        )
    width = 2
    while width < tokens:
        pair = (row // (2 * width) == col // (2 * width)) & (row // width > col // width)
        half = [dot3(jnp.where(pair, lowers[h], 0.0), inverses[h]) for h in range(heads)]
        inverses = [inverses[h] - dot3(inverses[h], half[h]) for h in range(heads)]
        width *= 2
    for h in range(heads):
        g = h // share
        weighted = inverses[h] * beta_row[h : h + 1, :]
        update = dot2(weighted, value_ref[:, h * DV : (h + 1) * DV])
        wy = dot2(weighted * (start_row[h : h + 1, :] * inv_rows[g]), keys[g])
        solved = jnp.concatenate([update, wy], axis=1)
        mixed = dot3(mixing[h], solved)
        local_ref[h] = mixed[:, :DV]
        reach_ref[h] = (start[:, h : h + 1] * scaled[g] - mixed[:, DV:]).astype(jnp.bfloat16)
        turned = solved.T * (end_row[h : h + 1, :] * inv_rows[g])
        carry = dot2(turned, keys[g])
        add_ref[h] = carry[:DV]
        map_ref[h] = (
            jnp.where(eye, start[tokens - 1 : tokens, h : h + 1], 0.0) - carry[DV:]
        ).astype(jnp.bfloat16)


def finish_kernel(local_ref, reach_ref, states_ref, into_ref, select_ref, gate_ref, gain_ref, out_ref):
    owners = states_ref.shape[0]
    select = select_ref[...] > 0.5
    for h in range(local_ref.shape[0]):
        core = local_ref[h]
        reach = reach_ref[h]
        for owner in range(owners + 1):
            state = states_ref[owner, h] if owner < owners else into_ref[h]
            part = dot1(reach, state, ((1,), (1,)))
            core = core + jnp.where(select[:, owner : owner + 1], part, 0.0)
        normed = core * lax.rsqrt(jnp.mean(core * core, axis=1, keepdims=True) + 1e-06)
        gate = gate_ref[:, h * DV : (h + 1) * DV].astype(jnp.float32)
        out_ref[:, h * DV : (h + 1) * DV] = (
            normed * gain_ref[...] * (gate * jax.nn.sigmoid(gate))
        ).astype(jnp.bfloat16)


def attend_kernel(
    query_ref, cos_ref, sin_ref, gate_ref, row_ref, code_ref, place_ref, own_ref, *rest
):
    pieces, out_ref = [own_ref] + list(rest[:-1]), rest[-1]
    tokens = query_ref.shape[0]
    cosines, sines = cos_ref[...], sin_ref[...]
    lane = lax.broadcasted_iota(jnp.int32, (tokens, 128), 1)
    old_code, limit = row_ref[:, 0:1], row_ref[:, 1:2]
    new_code, own_row = row_ref[:, 2:3], row_ref[:, 3:4]
    keys, values, seen, at = [], [], [], 0
    for ref in pieces:
        if len(ref.shape) == 3:
            keys.append(ref[0])
            values.append(ref[1])
        else:
            keys.append(ref[:, 0].reshape(-1, HD))
            values.append(ref[:, 1].reshape(-1, HD))
        count = keys[-1].shape[0]
        code, place = code_ref[:, at : at + count], place_ref[:, at : at + count]
        at += count
        seen.append(
            ((code == old_code) & (place < limit)) | ((code == new_code) & (place <= own_row))
        )
    for h in range(query_ref.shape[1] // HD):
        front = query_ref[:, h * HD : h * HD + 128].astype(jnp.float32)
        swapped = jnp.where(
            lane < ROT // 2, pltpu.roll(front, 128 - ROT // 2, 1), pltpu.roll(front, ROT // 2, 1)
        )
        query = jnp.concatenate(
            [
                (front * cosines + swapped * sines).astype(jnp.bfloat16),
                query_ref[:, h * HD + 128 : (h + 1) * HD],
            ],
            axis=1,
        )
        scores = [
            jnp.where(see, dot1(query, key, ((1,), (1,))) * HD ** (-0.5), NEG_LARGE)
            for see, key in zip(seen, keys)
        ]
        peak = jnp.max(scores[0], axis=1, keepdims=True)
        for score in scores[1:]:
            peak = jnp.maximum(peak, jnp.max(score, axis=1, keepdims=True))
        total, summed = 0.0, 0.0
        for score, see, value in zip(scores, seen, values):
            weight = jnp.where(see, jnp.exp(score - peak), 0.0)
            total = total + jnp.sum(weight, axis=1, keepdims=True)
            summed = summed + dot1(weight.astype(jnp.bfloat16), value)
        gate = gate_ref[:, h * HD : (h + 1) * HD].astype(jnp.float32)
        out_ref[:, h * HD : (h + 1) * HD] = (
            summed / total * jax.nn.sigmoid(gate)
        ).astype(jnp.bfloat16)


def whole_call(kernel, shapes, *arrays):
    space = pl.BlockSpec(memory_space=pltpu.VMEM)
    return pl.pallas_call(
        kernel,
        out_shape=shapes,
        in_specs=[space] * len(arrays),
        out_specs=jax.tree.map(lambda _: space, shapes),
        compiler_params=pltpu.CompilerParams(vmem_limit_bytes=48 * 2**20),
    )(*arrays)


def yarn_tables(positions, rotary):
    half = rotary // 2
    log_theta = math.log(ROPE_THETA)
    lower = max(
        math.floor(rotary * math.log(YARN_ANCHOR / (64.0 * math.pi)) / (2.0 * log_theta)), 0
    )
    upper = min(
        math.ceil(rotary * math.log(YARN_ANCHOR / (2.0 * math.pi)) / (2.0 * log_theta)), rotary - 1
    )
    spread = float(upper - lower)
    index = jnp.arange(half, dtype=jnp.float32)
    plain_frequency = jnp.exp(index * (-2.0 * log_theta / rotary))
    keep = 1.0 - jnp.clip((index - lower) / spread, 0.0, 1.0)
    frequency = plain_frequency * keep + plain_frequency / YARN_FACTOR * (1.0 - keep)
    angles = positions.astype(jnp.float32)[:, None] * frequency[None, :]
    attention_factor = 0.1 * math.log(YARN_FACTOR) + 1.0
    return (jnp.cos(angles) * attention_factor, jnp.sin(angles) * attention_factor)


def rotate(values, cosines, sines, rotary):
    half = rotary // 2
    first = values[..., :half]
    second = values[..., half:rotary]
    cosines = cosines[:, None, :]
    sines = sines[:, None, :]
    return jnp.concatenate(
        [first * cosines - second * sines, second * cosines + first * sines, values[..., rotary:]],
        axis=-1,
    )


def request_starts(req_len):
    order = jnp.arange(req_len.shape[0], dtype=jnp.int32)
    return jnp.sum(jnp.where(order[:, None] < order[None, :], req_len[:, None], 0), axis=0)


def row_layout(rows, req_len, req_prefix, req_offset):
    starts = request_starts(req_len)
    leading_found = (starts[None, :] <= rows[:, None]).astype(jnp.int32)
    segment = jnp.sum(leading_found, axis=1) - 1
    choose = (segment[:, None] == jnp.arange(req_len.shape[0], dtype=jnp.int32)[None, :]).astype(
        jnp.int32
    )
    first = jnp.sum(choose * starts[None, :], axis=1)
    prefix = jnp.sum(choose * req_prefix[None, :], axis=1)
    offset = jnp.sum(choose * req_offset[None, :], axis=1)
    return (segment, first, prefix, offset, offset + rows - first)


def turn(angle):
    quarter = jnp.floor(angle * (2.0 / math.pi) + 0.5)
    rest = angle - quarter * 1.5703125
    rest = rest - quarter * 4.837512969970703125e-4
    rest = rest - quarter * 7.54978995489188216e-8
    square = rest * rest
    sine = rest + rest * square * (
        (-1.9515295891e-4 * square + 8.3321608736e-3) * square - 1.6666654611e-1
    )
    cosine = (
        1.0
        - 0.5 * square
        + square
        * square
        * ((2.443315711809948e-5 * square - 1.388731625493765e-3) * square + 4.166664568298827e-2)
    )
    which = quarter.astype(jnp.int32) & 3
    odd = (which & 1) == 1
    cos_part = jnp.where(odd, sine, cosine)
    sin_part = jnp.where(odd, cosine, sine)
    cos_part = jnp.where((which == 1) | (which == 2), -cos_part, cos_part)
    sin_part = jnp.where(which >= 2, -sin_part, sin_part)
    return cos_part, sin_part


def lane_tables(position):
    half = ROT // 2
    log_theta = math.log(ROPE_THETA)
    lower = max(math.floor(ROT * math.log(YARN_ANCHOR / (64.0 * math.pi)) / (2.0 * log_theta)), 0)
    upper = min(
        math.ceil(ROT * math.log(YARN_ANCHOR / (2.0 * math.pi)) / (2.0 * log_theta)), ROT - 1
    )
    lane = lax.broadcasted_iota(jnp.int32, (1, 128), 1)
    index = (lane % half).astype(jnp.float32)
    plain = jnp.exp(index * (-2.0 * log_theta / ROT))
    keep = 1.0 - jnp.clip((index - lower) / float(upper - lower), 0.0, 1.0)
    frequency = plain * keep + plain / YARN_FACTOR * (1.0 - keep)
    cosine, sine = turn(position.astype(jnp.float32) * frequency)
    factor = 0.1 * math.log(YARN_FACTOR) + 1.0
    cosine = jnp.where(lane < ROT, cosine * factor, 1.0)
    sine = jnp.where(lane < half, -sine * factor, jnp.where(lane < ROT, sine * factor, 0.0))
    return cosine, sine


def roped(front, cosines, sines):
    lane = lax.broadcasted_iota(jnp.int32, front.shape, 1)
    swapped = jnp.where(
        lane < ROT // 2, pltpu.roll(front, 128 - ROT // 2, 1), pltpu.roll(front, ROT // 2, 1)
    )
    return front * cosines + swapped * sines


def fused_kernel(
    size, span,
    query_hbm, key_hbm, value_hbm, gate_hbm, logit_hbm, decay_hbm, gain_hbm, state_hbm,
    atq_hbm, atg_hbm, atk_hbm, atv_hbm, pk_hbm, pv_hbm,
    len_ref, prefix_ref, offset_ref, table_ref,
    dn_out_ref, at_out_ref,
    query_ref, key_ref, value_ref, gate_ref, logit_ref, decay_ref, gain_ref, atq_ref, atg_ref, raw_ref,
    states, cached, fresh,
    local_ref, reach_ref, map_ref, add_ref, held, leaving, bias_ref,
    load_sem, st_send, st_recv, ck_send, ck_recv, nk_send, nk_recv, sib_send, sib_recv,
    chain_send, chain_recv,
):
    me = lax.axis_index("context")
    head_at = lax.axis_index("head")
    tokens = query_ref.shape[0]
    heads = local_ref.shape[0]
    share = VH // KH
    prefixes = states.shape[1]
    width = cached.shape[3]
    part = tokens // 2
    lane_half = lax.rem(head_at, 2)
    sibling = head_at + 1 - 2 * lane_half
    kv_head = lax.div(head_at, 2)

    barrier = pltpu.get_barrier_semaphore()
    for step in range(1, size):
        pl.semaphore_signal(
            barrier, inc=1, device_id={"context": lax.rem(me + step, size)}
        )
    pl.semaphore_signal(barrier, inc=1, device_id={"head": sibling})

    columns = pl.ds(pl.multiple_of(kv_head * HD, HD), HD)
    loads = [
        (state_hbm, states.at[me]),
        (atk_hbm.at[:, columns], raw_ref),
        (atv_hbm.at[pl.ds(0, part), columns], fresh.at[1, 0, 0]),
        (atv_hbm.at[pl.ds(part, part), columns], fresh.at[1, 0, 1]),
        (pk_hbm.at[0, :, columns], cached.at[0, me, 0]),
        (pk_hbm.at[1, :, columns], cached.at[0, me, 1]),
        (pv_hbm.at[0, :, columns], cached.at[1, me, 0]),
        (pv_hbm.at[1, :, columns], cached.at[1, me, 1]),
        (decay_hbm, decay_ref),
        (logit_hbm, logit_ref),
        (key_hbm, key_ref),
        (query_hbm, query_ref),
        (value_hbm, value_ref),
        (atq_hbm, atq_ref),
        (atg_hbm, atg_ref),
        (gate_hbm, gate_ref),
        (gain_hbm, gain_ref),
    ]
    loads = [
        pltpu.make_async_copy(source, target, load_sem.at[i])
        for i, (source, target) in enumerate(loads)
    ]
    for load in loads:
        load.start()

    row_start = me * tokens
    last_row = row_start + tokens - 1
    requests = len_ref.shape[0]
    starts, total = [], jnp.int32(0)
    for r in range(requests):
        starts.append(total)
        total = total + len_ref[r]

    def layout(rows):
        seg = jnp.zeros_like(rows)
        for r in range(1, requests):
            seg = seg + (rows >= starts[r]).astype(jnp.int32)
        return seg

    rows = row_start + lax.broadcasted_iota(jnp.int32, (tokens, 1), 0)
    seg = layout(rows)
    first, prefix, offset = [jnp.zeros_like(rows)] * 3
    tail_first, tail_prefix, head_seg = jnp.int32(0), prefix_ref[0], jnp.int32(0)
    head_first = jnp.int32(0)
    for r in range(requests):
        first = jnp.where(seg == r, starts[r], first)
        prefix = jnp.where(seg == r, prefix_ref[r], prefix)
        offset = jnp.where(seg == r, offset_ref[r], offset)
        tail_first = jnp.where(starts[r] <= last_row, starts[r], tail_first)
        tail_prefix = jnp.where(starts[r] <= last_row, prefix_ref[r], tail_prefix)
        head_first = jnp.where(starts[r] <= row_start, starts[r], head_first)
        head_seg = jnp.where(starts[r] <= row_start, r, head_seg)
    restarts = tail_first >= row_start
    carried = (seg == head_seg) & (first < row_start)
    row_lane = lax.broadcasted_iota(jnp.int32, (1, tokens), 1)
    seg_row = layout(row_start + row_lane)
    cosines, sines = lane_tables(offset + rows - first)

    for load in loads[1:2]:
        load.wait()
    for j in range(2):
        piece = pl.ds(j * part, part)
        cut = slice(j * part, (j + 1) * part)
        fresh[0, 0, j, :, 0:128] = roped(
            raw_ref[piece, 0:128].astype(jnp.float32), cosines[cut], sines[cut]
        ).astype(jnp.bfloat16)
        fresh[0, 0, j, :, 128:HD] = raw_ref[piece, 128:HD]

    groups = st_send.shape[2]
    group_heads = heads // groups

    def right_ok(s):
        return (me >= s) & (me < size - 1), me >= s + 1

    def left_ok(s):
        return (me + s < size) & (me > 0), me + s + 1 < size

    def st_copy(way, s, g, arriving):
        step = 1 if way == 0 else -1
        owner = lax.rem(me - step * (s + (1 if arriving else 0)) + 2 * size, size)
        ref = states.at[owner, :, pl.ds(g * group_heads, group_heads)]
        return pltpu.make_async_remote_copy(
            src_ref=ref, dst_ref=ref,
            send_sem=st_send.at[way, s, g], recv_sem=st_recv.at[way, s, g],
            device_id={"context": lax.rem(me + step + size, size)},
        )

    def state_start(s, g):
        for way, ok in ((0, right_ok), (1, left_ok)):

            @pl.when(ok(s)[0])
            def _(way=way):
                st_copy(way, s, g, False).start()

    def state_arrive(s, g):
        for way, ok in ((0, right_ok), (1, left_ok)):

            @pl.when(ok(s)[1])
            def _(way=way):
                st_copy(way, s, g, True).wait_recv()

    def ck_copy(step, arriving):
        owner = lax.rem(me - step + size, size) if arriving else me
        ref = cached.at[:, owner, lane_half]
        return pltpu.make_async_remote_copy(
            src_ref=ref, dst_ref=ref,
            send_sem=ck_send.at[step - 1], recv_sem=ck_recv.at[step - 1],
            device_id={"context": lax.rem(me + step, size)},
        )

    def nk_copy(step):
        return pltpu.make_async_remote_copy(
            src_ref=fresh.at[:, 0, lane_half], dst_ref=fresh.at[:, step, lane_half],
            send_sem=nk_send.at[step - 1], recv_sem=nk_recv.at[step - 1],
            device_id={"context": lax.rem(me + step, size)},
        )

    def sib_ck(step, arriving):
        owner = lax.rem(me - step + size, size)
        ref = cached.at[:, owner, 1 - lane_half if arriving else lane_half]
        return pltpu.make_async_remote_copy(
            src_ref=ref, dst_ref=ref,
            send_sem=sib_send.at[0, step - 1], recv_sem=sib_recv.at[0, step - 1],
            device_id={"head": sibling},
        )

    def sib_nk(step, arriving):
        ref = fresh.at[:, step, 1 - lane_half if arriving else lane_half]
        return pltpu.make_async_remote_copy(
            src_ref=ref, dst_ref=ref,
            send_sem=sib_send.at[1, step - 1], recv_sem=sib_recv.at[1, step - 1],
            device_id={"head": sibling},
        )

    def chain_copy(h):
        return pltpu.make_async_remote_copy(
            src_ref=leaving.at[h], dst_ref=held.at[h],
            send_sem=chain_send.at[h], recv_sem=chain_recv.at[h],
            device_id={"context": lax.rem(me + 1, size)},
        )

    loads[0].wait()
    pl.semaphore_wait(barrier, size)
    for g in range(groups):
        state_start(0, g)
    for load in loads[2:8]:
        load.wait()

    def kv_start():
        for step in range(1, size):
            ck_copy(step, False).start()
            if step <= span:

                @pl.when(me + step < size)
                def _(step=step):
                    nk_copy(step).start()

    def kv_share():
        for step in range(1, size):
            ck_copy(step, True).wait_recv()
            sib_ck(step, False).start()
            if step <= span:

                @pl.when(me >= step)
                def _(step=step):
                    nk_copy(step).wait_recv()
                    sib_nk(step, False).start()

    def kv_arrive():
        for step in range(1, size):
            sib_ck(step, True).wait_recv()
            if step <= span:

                @pl.when(me >= step)
                def _(step=step):
                    sib_nk(step, True).wait_recv()

    def forward(s):
        for g in range(groups):
            state_arrive(s - 1, g)
            if s < size - 1:
                state_start(s, g)

    kv_start()

    for step in range(1, span + 1):

        @pl.when(me < step)
        def _(step=step):
            fresh[:, step] = jnp.zeros_like(fresh[:, step])

    @pl.when(me == 0)
    def _():
        held[...] = jnp.zeros_like(held)

    slots = size * 2
    lanes = lax.broadcasted_iota(jnp.int32, (1, slots * width), 1)
    slot, inside = lanes // width, lanes % width
    per_prefix = table_ref.shape[0] // prefixes
    code, place = jnp.zeros_like(lanes), jnp.zeros_like(lanes)
    for e in range(table_ref.shape[0]):
        here = slot == table_ref[e]
        code = jnp.where(here, e // per_prefix, code)
        place = jnp.where(here, e % per_prefix * width + inside, place)
    bias_ref[:, : slots * width] = jnp.where(
        (code == prefix) & (place < offset), 0.0, NEG_LARGE
    )
    for step in range(span + 1):
        key_row = row_start - step * tokens + row_lane
        seen = (layout(key_row) == seg) & (key_row <= rows) & (key_row >= 0)
        at = slots * width + step * tokens
        bias_ref[:, at : at + tokens] = jnp.where(seen, 0.0, NEG_LARGE)

    row = lax.broadcasted_iota(jnp.int32, (tokens, tokens), 0)
    col = lax.broadcasted_iota(jnp.int32, (tokens, tokens), 1)
    same = seg == seg_row
    causal = same & (row >= col)
    strict = same & (row > col)
    eye = row == col
    causal_f = causal.astype(jnp.float32)
    for load in loads[8:13]:
        load.wait()
    run = lax.dot_general(
        causal_f, decay_ref[...], (((1,), (0,)), ((), ())),
        precision=HIGH, preferred_element_type=jnp.float32,
    )
    beta = jax.nn.sigmoid(logit_ref[...])
    turned = jnp.concatenate(
        [run, beta, jnp.zeros((tokens, 128 - 2 * heads), jnp.float32)], axis=1
    ).T
    run_row, beta_row = turned[:heads], turned[heads : 2 * heads]
    start, start_row = jnp.exp(run), jnp.exp(run_row)
    tail = seg_row == seg_row[:, tokens - 1 : tokens]
    end_row = jnp.where(
        tail, jnp.exp(jnp.where(tail, run_row[:, tokens - 1 : tokens] - run_row, 0.0)), 0.0
    )
    keys, grams, mixes, scaled, inv_rows = [], [], [], [], []
    for g in range(heads // share):
        k = key_ref[:, g * DK : (g + 1) * DK]
        q = query_ref[:, g * DK : (g + 1) * DK]
        gram = dot1(k, k, ((1,), (1,)))
        cross = dot1(q, k, ((1,), (1,)))
        squares = jnp.where(eye, gram, 0.0)
        inv = lax.rsqrt(jnp.sum(squares, axis=1, keepdims=True) + 1e-06)
        inv_row = lax.rsqrt(jnp.sum(squares, axis=0, keepdims=True) + 1e-06)
        q_f = q.astype(jnp.float32)
        inv_q = lax.rsqrt(jnp.sum(q_f * q_f, axis=1, keepdims=True) + 1e-06) * DK ** (-0.5)
        keys.append(k)
        inv_rows.append(inv_row)
        grams.append(gram * inv * inv_row)
        mixes.append(cross * inv_q * inv_row)
        scaled.append(q_f * inv_q)
    lowers, inverses, mixing = [], [], []
    for h in range(heads):
        gaps = run[:, h : h + 1] - run_row[h : h + 1, :]
        decay_mat = jnp.where(causal, jnp.exp(jnp.where(causal, gaps, 0.0)), 0.0)
        mixing.append(decay_mat * mixes[h // share])
        lower = jnp.where(strict, beta[:, h : h + 1] * grams[h // share] * decay_mat, 0.0)
        lowers.append(lower)
        inverses.append(
            jnp.where(eye, 1.0, 0.0) - jnp.where(row // 2 == col // 2, lower, 0.0)
        )
    depth = 2
    while depth < tokens:
        pair = (row // (2 * depth) == col // (2 * depth)) & (row // depth > col // depth)
        half = [dot3(jnp.where(pair, lowers[h], 0.0), inverses[h]) for h in range(heads)]
        inverses = [inverses[h] - dot3(inverses[h], half[h]) for h in range(heads)]
        depth *= 2
        if depth == 32:
            forward(1)
    for h in range(heads):
        g = h // share
        weighted = inverses[h] * beta_row[h : h + 1, :]
        update = dot2(weighted, value_ref[:, h * DV : (h + 1) * DV])
        wy = dot2(weighted * (start_row[h : h + 1, :] * inv_rows[g]), keys[g])
        solved = jnp.concatenate([update, wy], axis=1)
        mixed = dot3(mixing[h], solved)
        local_ref[h] = mixed[:, :DV]
        reach_ref[h] = (start[:, h : h + 1] * scaled[g] - mixed[:, DV:]).astype(jnp.bfloat16)
        carry = dot2(solved.T * (end_row[h : h + 1, :] * inv_rows[g]), keys[g])
        add_ref[h] = carry[:DV]
        map_ref[h] = (
            jnp.where(eye, start[tokens - 1 : tokens, h : h + 1], 0.0) - carry[DV:]
        ).astype(jnp.bfloat16)
    for s in range(2, size):
        forward(s)

    for load in loads[13:]:
        load.wait()

    def attend():
        kv_arrive()
        old_keys = cached[0].reshape(-1, HD)
        old_values = cached[1].reshape(-1, HD)
        new_keys = fresh[0].reshape(-1, HD)
        new_values = fresh[1].reshape(-1, HD)
        old_bias, new_bias = bias_ref[:, : slots * width], bias_ref[:, slots * width :]
        for h in range(atq_ref.shape[1] // HD):
            front = atq_ref[:, h * HD : h * HD + 128].astype(jnp.float32)
            rear = atq_ref[:, h * HD + 128 : (h + 1) * HD].astype(jnp.float32)
            turned_front = roped(front, cosines, sines).astype(jnp.bfloat16).astype(jnp.float32)
            query = (
                jnp.concatenate([turned_front, rear], axis=1) * HD ** (-0.5)
            ).astype(jnp.bfloat16)
            old = dot1(query, old_keys, ((1,), (1,))) + old_bias
            new = dot1(query, new_keys, ((1,), (1,))) + new_bias
            peak = jnp.maximum(
                jnp.max(old, axis=1, keepdims=True), jnp.max(new, axis=1, keepdims=True)
            )
            old, new = jnp.exp(old - peak), jnp.exp(new - peak)
            whole = jnp.sum(old, axis=1, keepdims=True) + jnp.sum(new, axis=1, keepdims=True)
            summed = dot1(old.astype(jnp.bfloat16), old_values) + dot1(
                new.astype(jnp.bfloat16), new_values
            )
            gate = atg_ref[:, h * HD : (h + 1) * HD].astype(jnp.float32)
            at_out_ref[:, h * HD : (h + 1) * HD] = (
                summed / whole * jax.nn.sigmoid(gate)
            ).astype(jnp.bfloat16)

    def state_of(p, h):
        return jnp.concatenate([states[o, p, h] for o in range(size)], axis=0)

    @pl.when(me == size - 1)
    def _():
        kv_share()
        attend()

    for h in range(heads):
        whole_states = [state_of(p, h) for p in range(prefixes)]
        base = whole_states[0]
        for p in range(1, prefixes):
            base = jnp.where(tail_prefix == p, whole_states[p], base)
        reach = reach_ref[h]
        core = local_ref[h]
        for p in range(prefixes):
            core = core + jnp.where(
                (prefix == p) & ~carried, dot1(reach, whole_states[p], ((1,), (1,))), 0.0
            )

        @pl.when(me > 0)
        def _(h=h):
            chain_copy(h).wait_recv()

        into = held[h]

        @pl.when(me < size - 1)
        def _(h=h, base=base, into=into):
            leaving[h] = (
                dot1(jnp.where(restarts, base, into), map_ref[h]) + add_ref[h]
            ).astype(jnp.bfloat16)
            chain_copy(h).start()

        core = core + jnp.where(carried, dot1(reach, into, ((1,), (1,))), 0.0)
        normed = core * lax.rsqrt(jnp.mean(core * core, axis=1, keepdims=True) + 1e-06)
        gate = gate_ref[:, h * DV : (h + 1) * DV].astype(jnp.float32)
        dn_out_ref[:, h * DV : (h + 1) * DV] = (
            normed * gain_ref[...] * (gate * jax.nn.sigmoid(gate))
        ).astype(jnp.bfloat16)

    @pl.when(me < size - 1)
    def _():
        kv_share()
        attend()

    for s in range(size - 1):
        for g in range(groups):
            for way, ok in ((0, right_ok), (1, left_ok)):

                @pl.when(ok(s)[0])
                def _(way=way, s=s, g=g):
                    st_copy(way, s, g, False).wait_send()

    for step in range(1, size):
        ck_copy(step, False).wait_send()
        sib_ck(step, False).wait_send()
        if step <= span:

            @pl.when(me + step < size)
            def _(step=step):
                nk_copy(step).wait_send()

            @pl.when(me >= step)
            def _(step=step):
                sib_nk(step, False).wait_send()

    @pl.when(me < size - 1)
    def _():
        for h in range(heads):
            chain_copy(h).wait_send()


def fits_fused(tokens, query_heads, prefix_state, prefix_key):
    size = lax.axis_size("context")
    return (
        tokens == 128
        and size <= 4
        and prefix_state.shape[2] % 16 == 0
        and prefix_key.shape[0] == 2
        and prefix_key.shape[1] % 16 == 0
        and HQ // KVH == 2 * query_heads
    )


def fused(
    dn_query, dn_key, dn_value, dn_gate, dn_beta_logit, dn_decay, dn_norm_gain,
    prefix_state, at_query, at_gate, at_key, at_value, prefix_key, prefix_value,
    req_len, req_prefix, req_offset, block_table,
):
    size = lax.axis_size("context")
    tokens = dn_query.shape[0]
    heads = dn_value.shape[1] // DV
    prefixes, _, state_rows, _ = prefix_state.shape
    width = prefix_key.shape[1]
    longest = size * tokens // 2
    span = min(size - 1, (longest - 1 + tokens - 1) // tokens)
    groups = 2
    bf16, f32 = jnp.bfloat16, jnp.float32
    far = pl.BlockSpec(memory_space=pl.ANY)
    near = pl.BlockSpec(memory_space=pltpu.VMEM)
    small = pl.BlockSpec(memory_space=pltpu.SMEM)
    keys_seen = size * 2 * width + (span + 1) * tokens
    dma = pltpu.SemaphoreType.DMA
    return pl.pallas_call(
        lambda *refs: fused_kernel(size, span, *refs),
        out_shape=[
            jax.ShapeDtypeStruct(dn_gate.shape, bf16),
            jax.ShapeDtypeStruct(at_query.shape, bf16),
        ],
        in_specs=[far] * 14 + [small] * 4,
        out_specs=[near, near],
        scratch_shapes=[
            pltpu.VMEM(dn_query.shape, bf16),
            pltpu.VMEM(dn_key.shape, bf16),
            pltpu.VMEM(dn_value.shape, bf16),
            pltpu.VMEM(dn_gate.shape, bf16),
            pltpu.VMEM(dn_beta_logit.shape, f32),
            pltpu.VMEM(dn_decay.shape, f32),
            pltpu.VMEM((1, DV), f32),
            pltpu.VMEM(at_query.shape, bf16),
            pltpu.VMEM(at_gate.shape, bf16),
            pltpu.VMEM((tokens, HD), bf16),
            pltpu.VMEM((size, prefixes, heads, state_rows, DK), bf16),
            pltpu.VMEM((2, size, 2, width, HD), bf16),
            pltpu.VMEM((2, span + 1, 2, tokens // 2, HD), bf16),
            pltpu.VMEM((heads, tokens, DV), f32),
            pltpu.VMEM((heads, tokens, DK), bf16),
            pltpu.VMEM((heads, DK, DK), bf16),
            pltpu.VMEM((heads, DV, DK), f32),
            pltpu.VMEM((heads, DV, DK), bf16),
            pltpu.VMEM((heads, DV, DK), bf16),
            pltpu.VMEM((tokens, keys_seen), f32),
            dma((17,)),
            dma((2, size - 1, groups)),
            dma((2, size - 1, groups)),
            dma((size - 1,)),
            dma((size - 1,)),
            dma((span,)),
            dma((span,)),
            dma((2, size - 1)),
            dma((2, size - 1)),
            dma((heads,)),
            dma((heads,)),
        ],
        compiler_params=pltpu.CompilerParams(
            collective_id=2, has_side_effects=True, vmem_limit_bytes=60 * 2**20
        ),
    )(
        dn_query, dn_key, dn_value, dn_gate, dn_beta_logit, dn_decay, dn_norm_gain[None, :],
        prefix_state, at_query, at_gate, at_key, at_value, prefix_key, prefix_value,
        req_len, req_prefix, req_offset, block_table,
    )


def shards(
    dn_query,
    dn_key,
    dn_value,
    dn_gate,
    dn_beta_logit,
    dn_decay,
    dn_norm_gain,
    prefix_state,
    at_query,
    at_gate,
    at_key,
    at_value,
    prefix_key,
    prefix_value,
    req_len,
    req_prefix,
    req_offset,
    block_table,
):
    tokens_here = dn_query.shape[0]
    value_heads = dn_value.shape[1] // DV
    query_heads = at_query.shape[1] // HD
    if fits_fused(tokens_here, query_heads, prefix_state, prefix_key):
        return fused(
            dn_query, dn_key, dn_value, dn_gate, dn_beta_logit, dn_decay, dn_norm_gain,
            prefix_state, at_query, at_gate, at_key, at_value, prefix_key, prefix_value,
            req_len, req_prefix, req_offset, block_table,
        )
    device = lax.axis_index("context")
    row_start = device * tokens_here
    rows = row_start + jnp.arange(tokens_here, dtype=jnp.int32)
    segment, first, prefix, offset, position = row_layout(rows, req_len, req_prefix, req_offset)
    size = lax.axis_size("context")
    query_heads_here = query_heads
    kv_head = lax.axis_index("head") * query_heads_here // (HQ // KVH)
    cosines, sines = yarn_tables(position, ROT)
    new_key = lax.dynamic_slice_in_dim(at_key, kv_head * HD, HD, 1).reshape(tokens_here, 1, HD)
    new_key = (
        rotate(new_key.astype(jnp.float32), cosines, sines, ROT)
        .reshape(tokens_here, HD)
        .astype(jnp.bfloat16)
    )
    new_value = lax.dynamic_slice_in_dim(at_value, kv_head * HD, HD, 1)
    cached_key = lax.dynamic_slice_in_dim(prefix_key, kv_head * HD, HD, 2)
    cached_value = lax.dynamic_slice_in_dim(prefix_value, kv_head * HD, HD, 2)
    states = jnp.stack([prefix_state] + from_others(prefix_state, "context", size, size))
    states = jnp.concatenate([states[::-1]] * 2)
    states = lax.dynamic_slice_in_dim(states, size - 1 - device, size, 0)
    states = jnp.moveaxis(states, 0, 2)
    states = states.reshape(states.shape[:2] + (-1, DK))
    slots_here = cached_key.shape[0]
    own_block = jnp.concatenate(
        [cached_key.reshape(-1, HD), new_key, cached_value.reshape(-1, HD), new_value]
    ).reshape(2, -1, HD)
    block_rows = own_block.shape[1]
    sharers = HQ // KVH // query_heads
    share = block_rows // sharers
    share_index = lax.axis_index("head") % sharers
    mine = lax.dynamic_slice_in_dim(own_block, share_index * share, share, 1)
    received = jnp.stack(from_others(mine, "context", size, size))
    siblings = from_others(received, "head", lax.axis_size("head"), sharers)
    cached_rows = cached_key.shape[0] * cached_key.shape[1]
    square = (value_heads, DK, DK)
    local_out, reach, map_half, carry_add = whole_call(
        local_kernel,
        [
            jax.ShapeDtypeStruct((value_heads, tokens_here, DV), jnp.float32),
            jax.ShapeDtypeStruct((value_heads, tokens_here, DK), jnp.bfloat16),
            jax.ShapeDtypeStruct(square, jnp.bfloat16),
            jax.ShapeDtypeStruct(square, jnp.float32),
        ],
        dn_query,
        dn_key,
        dn_value,
        dn_beta_logit,
        dn_beta_logit.T,
        dn_decay,
        dn_decay.T,
        segment[:, None],
        segment[None, :],
    )
    restarts = first[tokens_here - 1] >= row_start
    tail_prefix = prefix[tokens_here - 1]
    base = jnp.zeros(states.shape[1:], states.dtype)
    for owner in range(states.shape[0]):
        base = jnp.where(tail_prefix == owner, states[owner], base)
    fresh = jnp.einsum("hvj,hjk->hvk", base, map_half, preferred_element_type=jnp.float32)
    into_state = chain(
        jnp.where(restarts, 0, map_half).astype(jnp.bfloat16),
        carry_add + jnp.where(restarts, fresh, 0.0),
        size,
    )
    carried = (segment == segment[0]) & (first[0] < row_start)
    owner_ids = jnp.arange(states.shape[0], dtype=jnp.int32)
    select = (prefix[None, :] == owner_ids[:, None]) & ~carried[None, :]
    select = jnp.concatenate([select, carried[None, :]], axis=0)
    dn_out = whole_call(
        finish_kernel,
        jax.ShapeDtypeStruct((tokens_here, value_heads * DV), jnp.bfloat16),
        local_out,
        reach,
        states,
        into_state,
        select.astype(jnp.float32).T,
        dn_gate,
        dn_norm_gain[None, :],
    )
    blocks_per_prefix = block_table.shape[0] // prefix_state.shape[0]
    width = cached_key.shape[1]
    others = (device - 1 - jnp.arange(size - 1, dtype=jnp.int32)) % size
    origins = [jnp.full((block_rows,), device, jnp.int32)]
    parts = [jnp.arange(block_rows, dtype=jnp.int32)]
    for step in range(sharers):
        origins.append(jnp.repeat(others, share))
        parts.append(
            (share_index - step) % sharers * share
            + jnp.tile(jnp.arange(share, dtype=jnp.int32), size - 1)
        )
    origin, part = jnp.concatenate(origins), jnp.concatenate(parts)
    slot = origin * slots_here + part // width
    entry = jnp.sum(
        jnp.where(
            block_table[:, None] == slot[None, :],
            jnp.arange(block_table.shape[0], dtype=jnp.int32)[:, None],
            0,
        ),
        axis=0,
    )
    key_row = origin * tokens_here + part - cached_rows
    starts = request_starts(req_len)
    key_segment = jnp.sum((starts[:, None] <= key_row[None, :]).astype(jnp.int32), axis=0) - 1
    old = part < cached_rows
    prefixes = prefix_state.shape[0]
    code = jnp.where(old, entry // blocks_per_prefix, prefixes + key_segment)
    place = jnp.where(old, entry % blocks_per_prefix * width + part % width, key_row)
    ones = jnp.ones((tokens_here, 128 - ROT), jnp.float32)
    at_out = whole_call(
        attend_kernel,
        jax.ShapeDtypeStruct((tokens_here, query_heads * HD), jnp.bfloat16),
        at_query,
        jnp.concatenate([cosines, cosines, ones], axis=1),
        jnp.concatenate([-sines, sines, 0.0 * ones], axis=1),
        at_gate,
        jnp.stack([prefix, offset, prefixes + segment, rows], axis=1),
        code[None, :],
        place[None, :],
        own_block,
        received,
        *siblings,
    )
    return (dn_out, at_out)


def solution(mesh):
    placed = (
        P(("group", "context"), "head"),
        P(("group", "context"), "head"),
        P(("group", "context"), "head"),
        P(("group", "context"), "head"),
        P(("group", "context"), "head"),
        P(("group", "context"), "head"),
        P(),
        P("group", "head", "context", None),
        P(("group", "context"), "head"),
        P(("group", "context"), "head"),
        P(("group", "context"), None),
        P(("group", "context"), None),
        P(("group", "context"), None, None),
        P(("group", "context"), None, None),
        P("group"),
        P("group"),
        P("group"),
        P("group"),
    )
    return jax.shard_map(
        shards,
        mesh=mesh,
        in_specs=placed,
        out_specs=(P(("group", "context"), "head"), P(("group", "context"), "head")),
        check_vma=False,
    )
```

```python
import math

import jax
import jax.numpy as jnp
from jax import lax
from jax.experimental import pallas as pl
from jax.experimental.pallas import tpu as pltpu
from jax.sharding import PartitionSpec as P

VH = 32
KH = 16
DK = 128
DV = 128
HQ = 16
KVH = 2
HD = 256
ROT = 64


ROPE_THETA = 10000000.0
YARN_FACTOR = 4.0
YARN_ANCHOR = 262144.0
NEG_LARGE = -1e30
HIGH = lax.Precision.HIGHEST


def chain_kernel(size, map_ref, add_ref, into_ref, held, leaving, send_sem, recv_sem):
    me = lax.axis_index("context")
    heads = map_ref.shape[0]
    barrier = pltpu.get_barrier_semaphore()
    after, before = lax.rem(me + 1, size), lax.rem(me + size - 1, size)
    for neighbour in (before, after):
        pl.semaphore_signal(barrier, inc=1, device_id={"context": neighbour})
    pl.semaphore_wait(barrier, 2)

    def sent(h):
        return pltpu.make_async_remote_copy(
            src_ref=leaving.at[h],
            dst_ref=held.at[h],
            send_sem=send_sem.at[h],
            recv_sem=recv_sem.at[h],
            device_id={"context": after},
        )

    @pl.when(me == 0)
    def _():
        held[...] = jnp.zeros_like(held)

    for h in range(heads):

        @pl.when(me > 0)
        def _(h=h):
            sent(h).wait_recv()

        leaving[h] = (
            jnp.dot(held[h], map_ref[h], preferred_element_type=jnp.float32) + add_ref[h]
        ).astype(jnp.bfloat16)

        @pl.when(me < size - 1)
        def _(h=h):
            sent(h).start()

    into_ref[...] = held[...]

    @pl.when(me < size - 1)
    def _():
        for h in range(heads):
            sent(h).wait_send()


def chain(carry_map, carry_add, size):
    heads = carry_map.shape[0]
    return pl.pallas_call(
        lambda *refs: chain_kernel(size, *refs),
        out_shape=jax.ShapeDtypeStruct(carry_add.shape, jnp.bfloat16),
        in_specs=[pl.BlockSpec(memory_space=pltpu.VMEM)] * 2,
        out_specs=pl.BlockSpec(memory_space=pltpu.VMEM),
        scratch_shapes=[
            pltpu.VMEM(carry_add.shape, jnp.bfloat16),
            pltpu.VMEM(carry_add.shape, jnp.bfloat16),
            pltpu.SemaphoreType.DMA((heads,)),
            pltpu.SemaphoreType.DMA((heads,)),
        ],
        compiler_params=pltpu.CompilerParams(collective_id=1, has_side_effects=True),
    )(carry_map, carry_add)


def from_others(x, axis, size, span):
    return [
        lax.ppermute(
            x, axis, [(i, i // span * span + (i + step) % span) for i in range(size)]
        )
        for step in range(1, span)
    ]


def halves(x):
    high = x.astype(jnp.bfloat16)
    return high, (x - high.astype(jnp.float32)).astype(jnp.bfloat16)


def dot1(a, b, contract=((1,), (0,))):
    return lax.dot_general(a, b, (contract, ((), ())), preferred_element_type=jnp.float32)


def dot2(a, exact):
    high, low = halves(a)
    return dot1(high, exact) + dot1(low, exact)


def dot3(a, b):
    a_high, a_low = halves(a)
    b_high, b_low = halves(b)
    return dot1(a_high, b_high) + (dot1(a_high, b_low) + dot1(a_low, b_high))


def local_kernel(
    query_ref, key_ref, value_ref, logit_ref, logit_row_ref, decay_ref, decay_row_ref,
    seg_ref, seg_row_ref, local_ref, reach_ref, map_ref, add_ref,
):
    tokens = query_ref.shape[0]
    heads = local_ref.shape[0]
    share = VH // KH
    seg, seg_row = seg_ref[...], seg_row_ref[...]
    row = lax.broadcasted_iota(jnp.int32, (tokens, tokens), 0)
    col = lax.broadcasted_iota(jnp.int32, (tokens, tokens), 1)
    same = seg == seg_row
    causal = same & (row >= col)
    strict = same & (row > col)
    eye = row == col
    causal_f = causal.astype(jnp.float32)
    run = lax.dot_general(
        causal_f, decay_ref[...], (((1,), (0,)), ((), ())),
        precision=HIGH, preferred_element_type=jnp.float32,
    )
    run_row = lax.dot_general(
        decay_row_ref[...], causal_f, (((1,), (1,)), ((), ())),
        precision=HIGH, preferred_element_type=jnp.float32,
    )
    beta, beta_row = jax.nn.sigmoid(logit_ref[...]), jax.nn.sigmoid(logit_row_ref[...])
    start, start_row = jnp.exp(run), jnp.exp(run_row)
    tail = seg_row == seg_row[:, tokens - 1 : tokens]
    end_row = jnp.where(
        tail, jnp.exp(jnp.where(tail, run_row[:, tokens - 1 : tokens] - run_row, 0.0)), 0.0
    )
    keys, grams, mixes, scaled, inv_rows = [], [], [], [], []
    for g in range(heads // share):
        k = key_ref[:, g * DK : (g + 1) * DK]
        q = query_ref[:, g * DK : (g + 1) * DK]
        gram = dot1(k, k, ((1,), (1,)))
        cross = dot1(q, k, ((1,), (1,)))
        squares = jnp.where(eye, gram, 0.0)
        inv = lax.rsqrt(jnp.sum(squares, axis=1, keepdims=True) + 1e-06)
        inv_row = lax.rsqrt(jnp.sum(squares, axis=0, keepdims=True) + 1e-06)
        q_f = q.astype(jnp.float32)
        inv_q = lax.rsqrt(jnp.sum(q_f * q_f, axis=1, keepdims=True) + 1e-06) * DK ** (-0.5)
        keys.append(k)
        inv_rows.append(inv_row)
        grams.append(gram * inv * inv_row)
        mixes.append(cross * inv_q * inv_row)
        scaled.append(q_f * inv_q)
    lowers, inverses, mixing = [], [], []
    for h in range(heads):
        gaps = run[:, h : h + 1] - run_row[h : h + 1, :]
        decay_mat = jnp.where(causal, jnp.exp(jnp.where(causal, gaps, 0.0)), 0.0)
        mixing.append(decay_mat * mixes[h // share])
        lower = jnp.where(strict, beta[:, h : h + 1] * grams[h // share] * decay_mat, 0.0)
        lowers.append(lower)
        inverses.append(
            jnp.where(eye, 1.0, 0.0) - jnp.where(row // 2 == col // 2, lower, 0.0)
        )
    width = 2
    while width < tokens:
        pair = (row // (2 * width) == col // (2 * width)) & (row // width > col // width)
        half = [dot3(jnp.where(pair, lowers[h], 0.0), inverses[h]) for h in range(heads)]
        inverses = [inverses[h] - dot3(inverses[h], half[h]) for h in range(heads)]
        width *= 2
    for h in range(heads):
        g = h // share
        weighted = inverses[h] * beta_row[h : h + 1, :]
        update = dot2(weighted, value_ref[:, h * DV : (h + 1) * DV])
        wy = dot2(weighted * (start_row[h : h + 1, :] * inv_rows[g]), keys[g])
        solved = jnp.concatenate([update, wy], axis=1)
        mixed = dot3(mixing[h], solved)
        local_ref[h] = mixed[:, :DV]
        reach_ref[h] = (start[:, h : h + 1] * scaled[g] - mixed[:, DV:]).astype(jnp.bfloat16)
        turned = solved.T * (end_row[h : h + 1, :] * inv_rows[g])
        carry = dot2(turned, keys[g])
        add_ref[h] = carry[:DV]
        map_ref[h] = (
            jnp.where(eye, start[tokens - 1 : tokens, h : h + 1], 0.0) - carry[DV:]
        ).astype(jnp.bfloat16)


def finish_kernel(local_ref, reach_ref, states_ref, into_ref, select_ref, gate_ref, gain_ref, out_ref):
    owners = states_ref.shape[0]
    select = select_ref[...] > 0.5
    for h in range(local_ref.shape[0]):
        core = local_ref[h]
        reach = reach_ref[h]
        for owner in range(owners + 1):
            state = states_ref[owner, h] if owner < owners else into_ref[h]
            part = dot1(reach, state, ((1,), (1,)))
            core = core + jnp.where(select[:, owner : owner + 1], part, 0.0)
        normed = core * lax.rsqrt(jnp.mean(core * core, axis=1, keepdims=True) + 1e-06)
        gate = gate_ref[:, h * DV : (h + 1) * DV].astype(jnp.float32)
        out_ref[:, h * DV : (h + 1) * DV] = (
            normed * gain_ref[...] * (gate * jax.nn.sigmoid(gate))
        ).astype(jnp.bfloat16)


def attend_kernel(
    query_ref, cos_ref, sin_ref, gate_ref, row_ref, code_ref, place_ref, own_ref, *rest
):
    pieces, out_ref = [own_ref] + list(rest[:-1]), rest[-1]
    tokens = query_ref.shape[0]
    cosines, sines = cos_ref[...], sin_ref[...]
    lane = lax.broadcasted_iota(jnp.int32, (tokens, 128), 1)
    old_code, limit = row_ref[:, 0:1], row_ref[:, 1:2]
    new_code, own_row = row_ref[:, 2:3], row_ref[:, 3:4]
    keys, values, seen, at = [], [], [], 0
    for ref in pieces:
        if len(ref.shape) == 3:
            keys.append(ref[0])
            values.append(ref[1])
        else:
            keys.append(ref[:, 0].reshape(-1, HD))
            values.append(ref[:, 1].reshape(-1, HD))
        count = keys[-1].shape[0]
        code, place = code_ref[:, at : at + count], place_ref[:, at : at + count]
        at += count
        seen.append(
            ((code == old_code) & (place < limit)) | ((code == new_code) & (place <= own_row))
        )
    for h in range(query_ref.shape[1] // HD):
        front = query_ref[:, h * HD : h * HD + 128].astype(jnp.float32)
        swapped = jnp.where(
            lane < ROT // 2, pltpu.roll(front, 128 - ROT // 2, 1), pltpu.roll(front, ROT // 2, 1)
        )
        query = jnp.concatenate(
            [
                (front * cosines + swapped * sines).astype(jnp.bfloat16),
                query_ref[:, h * HD + 128 : (h + 1) * HD],
            ],
            axis=1,
        )
        scores = [
            jnp.where(see, dot1(query, key, ((1,), (1,))) * HD ** (-0.5), NEG_LARGE)
            for see, key in zip(seen, keys)
        ]
        peak = jnp.max(scores[0], axis=1, keepdims=True)
        for score in scores[1:]:
            peak = jnp.maximum(peak, jnp.max(score, axis=1, keepdims=True))
        total, summed = 0.0, 0.0
        for score, see, value in zip(scores, seen, values):
            weight = jnp.where(see, jnp.exp(score - peak), 0.0)
            total = total + jnp.sum(weight, axis=1, keepdims=True)
            summed = summed + dot1(weight.astype(jnp.bfloat16), value)
        gate = gate_ref[:, h * HD : (h + 1) * HD].astype(jnp.float32)
        out_ref[:, h * HD : (h + 1) * HD] = (
            summed / total * jax.nn.sigmoid(gate)
        ).astype(jnp.bfloat16)


def whole_call(kernel, shapes, *arrays):
    space = pl.BlockSpec(memory_space=pltpu.VMEM)
    return pl.pallas_call(
        kernel,
        out_shape=shapes,
        in_specs=[space] * len(arrays),
        out_specs=jax.tree.map(lambda _: space, shapes),
        compiler_params=pltpu.CompilerParams(vmem_limit_bytes=48 * 2**20),
    )(*arrays)


def yarn_tables(positions, rotary):
    half = rotary // 2
    log_theta = math.log(ROPE_THETA)
    lower = max(
        math.floor(rotary * math.log(YARN_ANCHOR / (64.0 * math.pi)) / (2.0 * log_theta)), 0
    )
    upper = min(
        math.ceil(rotary * math.log(YARN_ANCHOR / (2.0 * math.pi)) / (2.0 * log_theta)), rotary - 1
    )
    spread = float(upper - lower)
    index = jnp.arange(half, dtype=jnp.float32)
    plain_frequency = jnp.exp(index * (-2.0 * log_theta / rotary))
    keep = 1.0 - jnp.clip((index - lower) / spread, 0.0, 1.0)
    frequency = plain_frequency * keep + plain_frequency / YARN_FACTOR * (1.0 - keep)
    angles = positions.astype(jnp.float32)[:, None] * frequency[None, :]
    attention_factor = 0.1 * math.log(YARN_FACTOR) + 1.0
    return (jnp.cos(angles) * attention_factor, jnp.sin(angles) * attention_factor)


def rotate(values, cosines, sines, rotary):
    half = rotary // 2
    first = values[..., :half]
    second = values[..., half:rotary]
    cosines = cosines[:, None, :]
    sines = sines[:, None, :]
    return jnp.concatenate(
        [first * cosines - second * sines, second * cosines + first * sines, values[..., rotary:]],
        axis=-1,
    )


def request_starts(req_len):
    order = jnp.arange(req_len.shape[0], dtype=jnp.int32)
    return jnp.sum(jnp.where(order[:, None] < order[None, :], req_len[:, None], 0), axis=0)


def row_layout(rows, req_len, req_prefix, req_offset):
    starts = request_starts(req_len)
    leading_found = (starts[None, :] <= rows[:, None]).astype(jnp.int32)
    segment = jnp.sum(leading_found, axis=1) - 1
    choose = (segment[:, None] == jnp.arange(req_len.shape[0], dtype=jnp.int32)[None, :]).astype(
        jnp.int32
    )
    first = jnp.sum(choose * starts[None, :], axis=1)
    prefix = jnp.sum(choose * req_prefix[None, :], axis=1)
    offset = jnp.sum(choose * req_offset[None, :], axis=1)
    return (segment, first, prefix, offset, offset + rows - first)


def packed2(a, exact):
    return dot1(jnp.concatenate(halves(a), axis=1), jnp.concatenate([exact, exact], axis=0))


def packed3(a, b):
    b_high, b_low = halves(b)
    right = jnp.concatenate(
        [
            jnp.concatenate([b_high, b_low], axis=1),
            jnp.concatenate([b_high, jnp.zeros_like(b_low)], axis=1),
        ],
        axis=0,
    )
    both = dot1(jnp.concatenate(halves(a), axis=1), right)
    return both[:, : b.shape[1]] + both[:, b.shape[1] :]


def turn(angle):
    quarter = jnp.floor(angle * (2.0 / math.pi) + 0.5)
    rest = angle - quarter * 1.5703125
    rest = rest - quarter * 4.837512969970703125e-4
    rest = rest - quarter * 7.54978995489188216e-8
    square = rest * rest
    sine = rest + rest * square * (
        (-1.9515295891e-4 * square + 8.3321608736e-3) * square - 1.6666654611e-1
    )
    cosine = (
        1.0
        - 0.5 * square
        + square
        * square
        * ((2.443315711809948e-5 * square - 1.388731625493765e-3) * square + 4.166664568298827e-2)
    )
    which = quarter.astype(jnp.int32) & 3
    odd = (which & 1) == 1
    cos_part = jnp.where(odd, sine, cosine)
    sin_part = jnp.where(odd, cosine, sine)
    cos_part = jnp.where((which == 1) | (which == 2), -cos_part, cos_part)
    sin_part = jnp.where(which >= 2, -sin_part, sin_part)
    return cos_part, sin_part


def lane_tables(position):
    half = ROT // 2
    log_theta = math.log(ROPE_THETA)
    lower = max(math.floor(ROT * math.log(YARN_ANCHOR / (64.0 * math.pi)) / (2.0 * log_theta)), 0)
    upper = min(
        math.ceil(ROT * math.log(YARN_ANCHOR / (2.0 * math.pi)) / (2.0 * log_theta)), ROT - 1
    )
    lane = lax.broadcasted_iota(jnp.int32, (1, 128), 1)
    index = (lane % half).astype(jnp.float32)
    plain = jnp.exp(index * (-2.0 * log_theta / ROT))
    keep = 1.0 - jnp.clip((index - lower) / float(upper - lower), 0.0, 1.0)
    frequency = plain * keep + plain / YARN_FACTOR * (1.0 - keep)
    cosine, sine = turn(position.astype(jnp.float32) * frequency)
    factor = 0.1 * math.log(YARN_FACTOR) + 1.0
    cosine = jnp.where(lane < ROT, cosine * factor, 1.0)
    sine = jnp.where(lane < half, -sine * factor, jnp.where(lane < ROT, sine * factor, 0.0))
    return cosine, sine


def roped(front, cosines, sines):
    lane = lax.broadcasted_iota(jnp.int32, front.shape, 1)
    swapped = jnp.where(
        lane < ROT // 2, pltpu.roll(front, 128 - ROT // 2, 1), pltpu.roll(front, ROT // 2, 1)
    )
    return front * cosines + swapped * sines


def fused_kernel(
    size, span,
    query_hbm, key_hbm, value_hbm, gate_hbm, logit_hbm, decay_hbm, gain_hbm, state_hbm,
    atq_hbm, atg_hbm, atk_hbm, atv_hbm, pk_hbm, pv_hbm,
    len_ref, prefix_ref, offset_ref, table_ref,
    dn_out_ref, at_out_ref,
    query_ref, key_ref, value_ref, gate_ref, logit_ref, decay_ref, gain_ref, atq_ref, atg_ref, raw_ref,
    states, cached, fresh,
    local_ref, reach_ref, map_ref, add_ref, held, leaving, bias_ref,
    load_sem, st_send, st_recv, ck_send, ck_recv, nk_send, nk_recv, sib_send, sib_recv,
    chain_send, chain_recv, fw_send,
):
    me = lax.axis_index("context")
    head_at = lax.axis_index("head")
    tokens = query_ref.shape[0]
    heads = local_ref.shape[0]
    share = VH // KH
    prefixes = states.shape[1]
    width = cached.shape[3]
    part = tokens // 2
    lane_half = lax.rem(head_at, 2)
    sibling = head_at + 1 - 2 * lane_half
    kv_head = lax.div(head_at, 2)

    barrier = pltpu.get_barrier_semaphore()
    for step in range(1, size):
        pl.semaphore_signal(
            barrier, inc=1, device_id={"context": lax.rem(me + step, size)}
        )
    pl.semaphore_signal(barrier, inc=1, device_id={"head": sibling})

    columns = pl.ds(pl.multiple_of(kv_head * HD, HD), HD)
    loads = [
        (state_hbm, states.at[me]),
        (atk_hbm.at[:, columns], raw_ref),
        (atv_hbm.at[pl.ds(0, part), columns], fresh.at[1, 0, 0]),
        (atv_hbm.at[pl.ds(part, part), columns], fresh.at[1, 0, 1]),
        (pk_hbm.at[0, :, columns], cached.at[0, me, 0]),
        (pk_hbm.at[1, :, columns], cached.at[0, me, 1]),
        (pv_hbm.at[0, :, columns], cached.at[1, me, 0]),
        (pv_hbm.at[1, :, columns], cached.at[1, me, 1]),
        (decay_hbm, decay_ref),
        (logit_hbm, logit_ref),
        (key_hbm, key_ref),
        (query_hbm, query_ref),
        (value_hbm, value_ref),
        (atq_hbm, atq_ref),
        (atg_hbm, atg_ref),
        (gate_hbm, gate_ref),
        (gain_hbm, gain_ref),
    ]
    loads = [
        pltpu.make_async_copy(source, target, load_sem.at[i])
        for i, (source, target) in enumerate(loads)
    ]
    for load in loads:
        load.start()

    groups = st_send.shape[2]
    group_heads = heads // groups

    def right_ok(s):
        return (me >= s) & (me < size - 1)

    def left_ok(s):
        return (me + s < size) & (me > 0)

    def st_copy(way, s, g, arriving):
        step = 1 if way == 0 else -1
        owner = lax.rem(me - step * (s + (1 if arriving else 0)) + 2 * size, size)
        ref = states.at[owner, :, pl.ds(g * group_heads, group_heads)]
        return pltpu.make_async_remote_copy(
            src_ref=ref, dst_ref=ref,
            send_sem=st_send.at[way, s, g], recv_sem=st_recv.at[way, s, g],
            device_id={"context": lax.rem(me + step + size, size)},
        )

    def state_start(s, g):
        for way, ok in ((0, right_ok), (1, left_ok)):

            @pl.when(ok(s)[0])
            def _(way=way):
                st_copy(way, s, g, False).start()

    def state_arrive(s, g):
        for way, ok in ((0, right_ok), (1, left_ok)):

            @pl.when(ok(s)[1])
            def _(way=way):
                st_copy(way, s, g, True).wait_recv()

    def ck_copy(step, arriving):
        owner = lax.rem(me - step + size, size) if arriving else me
        ref = cached.at[:, owner, lane_half]
        return pltpu.make_async_remote_copy(
            src_ref=ref, dst_ref=ref,
            send_sem=ck_send.at[step - 1], recv_sem=ck_recv.at[step - 1],
            device_id={"context": lax.rem(me + step, size)},
        )

    def nk_copy(step):
        return pltpu.make_async_remote_copy(
            src_ref=fresh.at[:, 0, lane_half], dst_ref=fresh.at[:, step, lane_half],
            send_sem=nk_send.at[step - 1], recv_sem=nk_recv.at[step - 1],
            device_id={"context": lax.rem(me + step, size)},
        )

    def sib_ck(step, arriving):
        owner = lax.rem(me - step + size, size)
        ref = cached.at[:, owner, 1 - lane_half if arriving else lane_half]
        return pltpu.make_async_remote_copy(
            src_ref=ref, dst_ref=ref,
            send_sem=sib_send.at[0, step - 1], recv_sem=sib_recv.at[0, step - 1],
            device_id={"head": sibling},
        )

    def sib_nk(step, arriving):
        ref = fresh.at[:, step, 1 - lane_half if arriving else lane_half]
        return pltpu.make_async_remote_copy(
            src_ref=ref, dst_ref=ref,
            send_sem=sib_send.at[1, step - 1], recv_sem=sib_recv.at[1, step - 1],
            device_id={"head": sibling},
        )

    def chain_copy(h):
        return pltpu.make_async_remote_copy(
            src_ref=leaving.at[h], dst_ref=held.at[h],
            send_sem=chain_send.at[h], recv_sem=chain_recv.at[h],
            device_id={"context": lax.rem(me + 1, size)},
        )

    def state_own(g):
        for way, ok in ((0, right_ok), (1, left_ok)):

            @pl.when(ok(0))
            def _(way=way):
                st_copy(way, 0, g, False).start()

    def state_forward(s, g):
        for way, ok in ((0, right_ok), (1, left_ok)):

            @pl.when(ok(s))
            def _(way=way):
                st_copy(way, s - 1, g, True).wait_recv()
                st_copy(way, s, g, False).start()

    def state_end(g):
        for way, end in ((0, size - 1), (1, 0)):

            @pl.when(me == end)
            def _(way=way):
                for s in range(size - 1):
                    st_copy(way, s, g, True).wait_recv()

    def kv_start(step):
        ck_copy(step, False).start()
        if step <= span:

            @pl.when(me + step < size)
            def _():
                nk_copy(step).start()

    def relayed(step):
        return (me + step == size - 1) & (step > 1)

    def ck_onward(owner):
        ref = cached.at[:, owner, lane_half]
        return pltpu.make_async_remote_copy(
            src_ref=ref, dst_ref=ref,
            send_sem=fw_send.at[0, owner], recv_sem=ck_recv.at[size - 2 - owner],
            device_id={"context": size - 1},
        )

    def nk_onward(owner):
        far = size - 1 - owner
        return pltpu.make_async_remote_copy(
            src_ref=fresh.at[:, far - 1, lane_half], dst_ref=fresh.at[:, far, lane_half],
            send_sem=fw_send.at[1, owner], recv_sem=nk_recv.at[far - 1],
            device_id={"context": size - 1},
        )

    def kv_onward(owner):
        @pl.when(me == size - 2)
        def _():
            near = size - 2 - owner
            ck_copy(near, True).wait_recv()
            ck_onward(owner).start()
            sib_ck(near, False).start()
            if near <= span:
                nk_copy(near).wait_recv()
                sib_nk(near, False).start()
            if near + 1 <= span:
                nk_onward(owner).start()

    def kv_stage(s):
        for step in (1,2,3):
            right = me + step < size
            first = jnp.where(me == size - 2, 1, me)
            here = (right & (first == s)) | (jnp.logical_not(right) & (size - 1 - me == s))

            @pl.when(here & jnp.logical_not(relayed(step)))
            def _(step=step):
                kv_start(step)

    def kv_share():
        for step in range(1, size):

            @pl.when((me != size - 2) | (step > me))
            def _(step=step):
                ck_copy(step, True).wait_recv()
                sib_ck(step, False).start()
                if step <= span:

                    @pl.when(me >= step)
                    def _():
                        nk_copy(step).wait_recv()
                        sib_nk(step, False).start()

    def kv_arrive():
        for step in range(1, size):
            sib_ck(step, True).wait_recv()
            if step <= span:

                @pl.when(me >= step)
                def _(step=step):
                    sib_nk(step, True).wait_recv()

    loads[0].wait()
    pl.semaphore_wait(barrier, size)
    for g in range(groups):
        state_own(g)

    row_start = me * tokens
    last_row = row_start + tokens - 1
    requests = len_ref.shape[0]
    starts, total = [], jnp.int32(0)
    for r in range(requests):
        starts.append(total)
        total = total + len_ref[r]

    def layout(rows):
        seg = jnp.zeros_like(rows)
        for r in range(1, requests):
            seg = seg + (rows >= starts[r]).astype(jnp.int32)
        return seg

    rows = row_start + lax.broadcasted_iota(jnp.int32, (tokens, 1), 0)
    seg = layout(rows)
    first, prefix, offset = [jnp.zeros_like(rows)] * 3
    tail_first, tail_prefix, head_seg = jnp.int32(0), prefix_ref[0], jnp.int32(0)
    head_first = jnp.int32(0)
    for r in range(requests):
        first = jnp.where(seg == r, starts[r], first)
        prefix = jnp.where(seg == r, prefix_ref[r], prefix)
        offset = jnp.where(seg == r, offset_ref[r], offset)
        tail_first = jnp.where(starts[r] <= last_row, starts[r], tail_first)
        tail_prefix = jnp.where(starts[r] <= last_row, prefix_ref[r], tail_prefix)
        head_first = jnp.where(starts[r] <= row_start, starts[r], head_first)
        head_seg = jnp.where(starts[r] <= row_start, r, head_seg)
    restarts = tail_first >= row_start
    carried = (seg == head_seg) & (first < row_start)
    row_lane = lax.broadcasted_iota(jnp.int32, (1, tokens), 1)
    seg_row = layout(row_start + row_lane)
    cosines, sines = lane_tables(offset + rows - first)

    for load in loads[1:2]:
        load.wait()
    for j in range(2):
        piece = pl.ds(j * part, part)
        cut = slice(j * part, (j + 1) * part)
        fresh[0, 0, j, :, 0:128] = roped(
            raw_ref[piece, 0:128].astype(jnp.float32), cosines[cut], sines[cut]
        ).astype(jnp.bfloat16)
        fresh[0, 0, j, :, 128:HD] = raw_ref[piece, 128:HD]

    for load in loads[2:8]:
        load.wait()
    kv_stage(0)

    for step in range(1, span + 1):

        @pl.when(me < step)
        def _(step=step):
            fresh[:, step] = jnp.zeros_like(fresh[:, step])

    @pl.when(me == 0)
    def _():
        held[...] = jnp.zeros_like(held)

    slots = size * 2
    lanes = lax.broadcasted_iota(jnp.int32, (1, slots * width), 1)
    slot, inside = lanes // width, lanes % width
    per_prefix = table_ref.shape[0] // prefixes
    code, place = jnp.zeros_like(lanes), jnp.zeros_like(lanes)
    for e in range(table_ref.shape[0]):
        here = slot == table_ref[e]
        code = jnp.where(here, e // per_prefix, code)
        place = jnp.where(here, e % per_prefix * width + inside, place)
    bias_ref[:, : slots * width] = jnp.where(
        (code == prefix) & (place < offset), 0.0, NEG_LARGE
    )
    for step in range(span + 1):
        key_row = row_start - step * tokens + row_lane
        seen = (layout(key_row) == seg) & (key_row <= rows) & (key_row >= 0)
        at = slots * width + step * tokens
        bias_ref[:, at : at + tokens] = jnp.where(seen, 0.0, NEG_LARGE)

    row = lax.broadcasted_iota(jnp.int32, (tokens, tokens), 0)
    col = lax.broadcasted_iota(jnp.int32, (tokens, tokens), 1)
    same = seg == seg_row
    causal = same & (row >= col)
    strict = same & (row > col)
    eye = row == col
    causal_f = causal.astype(jnp.float32)
    for load in loads[8:13]:
        load.wait()
    run_row = lax.dot_general(
        decay_ref[...], causal_f, (((1,), (1,)), ((), ())),
        precision=HIGH, preferred_element_type=jnp.float32,
    )
    beta_row = jax.nn.sigmoid(logit_ref[...])
    tail = seg_row == seg_row[:, tokens - 1 : tokens]
    end_row = jnp.where(
        tail, jnp.exp(jnp.where(tail, run_row[:, tokens - 1 : tokens] - run_row, 0.0)), 0.0
    )
    turned = jnp.concatenate(
        [run_row, beta_row, end_row, jnp.zeros((128 - 3 * heads, tokens), jnp.float32)], axis=0
    ).T
    run, beta = turned[:, :heads], turned[:, heads : 2 * heads]
    end = turned[:, 2 * heads : 3 * heads]
    start, start_row = jnp.exp(run), jnp.exp(run_row)
    keys, turned_keys, grams, mixes, scaled, inv_rows, inv_cols = [], [], [], [], [], [], []
    for g in range(heads // share):
        k = key_ref[:, g * DK : (g + 1) * DK]
        q = query_ref[:, g * DK : (g + 1) * DK]
        gram = dot1(k, k, ((1,), (1,)))
        cross = dot1(q, k, ((1,), (1,)))
        squares = jnp.where(eye, gram, 0.0)
        inv = lax.rsqrt(jnp.sum(squares, axis=1, keepdims=True) + 1e-06)
        inv_row = lax.rsqrt(jnp.sum(squares, axis=0, keepdims=True) + 1e-06)
        q_f = q.astype(jnp.float32)
        inv_q = lax.rsqrt(jnp.sum(q_f * q_f, axis=1, keepdims=True) + 1e-06) * DK ** (-0.5)
        keys.append(k)
        turned_keys.append(k.T)
        inv_rows.append(inv_row)
        inv_cols.append(inv)
        grams.append(gram * inv * inv_row)
        mixes.append(cross * inv_q * inv_row)
        scaled.append(q_f * inv_q)
    lowers, inverses, mixing = [], [], []
    for h in range(heads):
        gaps = run[:, h : h + 1] - run_row[h : h + 1, :]
        decay_mat = jnp.where(causal, jnp.exp(jnp.where(causal, gaps, 0.0)), 0.0)
        mixing.append(decay_mat * mixes[h // share])
        lower = jnp.where(strict, beta[:, h : h + 1] * grams[h // share] * decay_mat, 0.0)
        lowers.append(lower)
        inverses.append(
            jnp.where(eye, 1.0, 0.0) - jnp.where((row >> 1) == (col >> 1), lower, 0.0)
        )
    plan = {5: (("state", 1, 0),), 7: (("state", 1, 1),), 9: (("state", 1, 2),), 11: (("state", 1, 3),("kv",1))}
    ticks = [0]

    def tick():
        for what, *which in plan.get(ticks[0], ()):
            if what == "state":
                state_forward(*which)
            else:
                kv_stage(*which)
        ticks[0] += 1

    depth, level = 2, 1
    while depth < tokens:
        pair = ((row >> (level + 1)) == (col >> (level + 1))) & ((row >> level) > (col >> level))
        half = [packed3(jnp.where(pair, lowers[h], 0.0), inverses[h]) for h in range(heads)]
        tick()
        inverses = [inverses[h] - packed3(inverses[h], half[h]) for h in range(heads)]
        tick()
        depth, level = depth * 2, level + 1
    weighted = [inverses[h] * beta_row[h : h + 1, :] for h in range(heads)]
    update = [packed2(weighted[h], value_ref[:, h * DV : (h + 1) * DV]) for h in range(heads)]
    wy = [
        packed2(weighted[h] * (start_row[h : h + 1, :] * inv_rows[h // share]), keys[h // share])
        for h in range(heads)
    ]
    tick()
    solved = [jnp.concatenate([update[h], wy[h]], axis=1) for h in range(heads)]
    carries = []
    for h in range(heads):
        high, low = halves(solved[h] * (end[:, h : h + 1] * inv_cols[h // share]))
        twice = jnp.concatenate([turned_keys[h // share]] * 2, axis=1)
        carries.append(dot1(twice, jnp.concatenate([high, low], axis=0)))
    tick()
    mixed = []
    for h in range(heads):
        high, low = halves(solved[h])
        mix_high, mix_low = halves(mixing[h])
        mixed.append(
            dot1(jnp.concatenate([mix_high, mix_low], axis=1), jnp.concatenate([high, high], axis=0))
            + dot1(mix_high, low)
        )
    tick()
    for h in range(heads):
        add_ref[h] = carries[h][:, :DV]
        map_ref[h] = (
            jnp.where(eye, start[tokens - 1 : tokens, h : h + 1], 0.0) - carries[h][:, DV:]
        ).astype(jnp.bfloat16)
        local_ref[h] = mixed[h][:, :DV]
        reach_ref[h] = (start[:, h : h + 1] * scaled[h // share] - mixed[h][:, DV:]).astype(
            jnp.bfloat16
        )
    for load in loads[13:]:
        load.wait()

    def attend():
        kv_arrive()
        old_keys = cached[0].reshape(-1, HD)
        old_values = cached[1].reshape(-1, HD)
        new_keys = fresh[0].reshape(-1, HD)
        new_values = fresh[1].reshape(-1, HD)
        old_bias, new_bias = bias_ref[:, : slots * width], bias_ref[:, slots * width :]
        for h in range(atq_ref.shape[1] // HD):
            front = atq_ref[:, h * HD : h * HD + 128].astype(jnp.float32)
            rear = atq_ref[:, h * HD + 128 : (h + 1) * HD].astype(jnp.float32)
            turned_front = roped(front, cosines, sines).astype(jnp.bfloat16).astype(jnp.float32)
            query = (
                jnp.concatenate([turned_front, rear], axis=1) * HD ** (-0.5)
            ).astype(jnp.bfloat16)
            old = dot1(query, old_keys, ((1,), (1,))) + old_bias
            new = dot1(query, new_keys, ((1,), (1,))) + new_bias
            peak = jnp.maximum(
                jnp.max(old, axis=1, keepdims=True), jnp.max(new, axis=1, keepdims=True)
            )
            old, new = jnp.exp(old - peak), jnp.exp(new - peak)
            whole = jnp.sum(old, axis=1, keepdims=True) + jnp.sum(new, axis=1, keepdims=True)
            summed = dot1(old.astype(jnp.bfloat16), old_values) + dot1(
                new.astype(jnp.bfloat16), new_values
            )
            gate = atg_ref[:, h * HD : (h + 1) * HD].astype(jnp.float32)
            at_out_ref[:, h * HD : (h + 1) * HD] = (
                summed / whole * jax.nn.sigmoid(gate)
            ).astype(jnp.bfloat16)

    def state_of(p, h):
        return jnp.concatenate([states[o, p, h] for o in range(size)], axis=0)

    def from_prefixes(these):
        own = [(prefix == p) & ~carried for p in range(prefixes)]
        for h in these:
            whole_states = [state_of(p, h) for p in range(prefixes)]
            base = whole_states[0]
            for p in range(1, prefixes):
                base = jnp.where(tail_prefix == p, whole_states[p], base)
            opened = dot1(map_ref[h], base, ((1,), (1,)))
            parts = dot1(reach_ref[h], jnp.concatenate(whole_states, axis=0), ((1,), (1,)))
            core = local_ref[h]
            for p in range(prefixes):
                core = core + jnp.where(own[p], parts[:, p * DV : (p + 1) * DV], 0.0)
            local_ref[h] = core
            add_ref[h] = add_ref[h] + jnp.where(restarts, opened, 0.0)

    for g in range(groups):
        for s in range(2, size - 1):
            state_forward(s, g)
        these = range(g * group_heads, (g + 1) * group_heads)
        state_end(g)
        from_prefixes(these)

        @pl.when(me == 0)
        def _(these=these):
            for h in these:
                leaving[h] = add_ref[h].astype(jnp.bfloat16)
                chain_copy(h).start()

    for s in range(2, size):
        kv_stage(s)
    for owner in range(size - 3, -1, -1):
        kv_onward(owner)

    @pl.when(me == size - 1)
    def _():
        kv_share()
        attend()

    for h in range(heads):

        @pl.when(me > 0)
        def _(h=h):
            chain_copy(h).wait_recv()

        @pl.when((me > 0) & (me < size - 1))
        def _(h=h):
            onward = dot1(map_ref[h], held[h])
            leaving[h] = (add_ref[h] + jnp.where(restarts, 0.0, onward)).astype(jnp.bfloat16)
            chain_copy(h).start()

        core = local_ref[h] + jnp.where(carried, dot1(reach_ref[h], held[h]), 0.0)
        normed = core * lax.rsqrt(jnp.mean(core * core, axis=1, keepdims=True) + 1e-06)
        gate = gate_ref[:, h * DV : (h + 1) * DV].astype(jnp.float32)
        dn_out_ref[:, h * DV : (h + 1) * DV] = (
            normed * gain_ref[...] * (gate * jax.nn.sigmoid(gate))
        ).astype(jnp.bfloat16)
        if h == 4:

            @pl.when(me < size - 1)
            def _():
                kv_share()

    @pl.when(me < size - 1)
    def _():
        attend()

    for s in range(size - 1):
        for g in range(groups):
            for way, ok in ((0, right_ok), (1, left_ok)):

                @pl.when(ok(s))
                def _(way=way, s=s, g=g):
                    st_copy(way, s, g, False).wait_send()

    for step in range(1, size):
        sib_ck(step, False).wait_send()

        @pl.when(jnp.logical_not(relayed(step)))
        def _(step=step):
            ck_copy(step, False).wait_send()
            if step <= span:

                @pl.when(me + step < size)
                def _():
                    nk_copy(step).wait_send()

        if step <= span:

            @pl.when(me >= step)
            def _(step=step):
                sib_nk(step, False).wait_send()

    @pl.when(me == size - 2)
    def _():
        for owner in range(size - 2):
            ck_onward(owner).wait_send()
            if size - 1 - owner <= span:
                nk_onward(owner).wait_send()

    @pl.when(me < size - 1)
    def _():
        for h in range(heads):
            chain_copy(h).wait_send()


def hand_out_kernel(dn_ref, at_ref, dn_out_ref, at_out_ref, held, load_sem, store_sem):
    rows = dn_ref.shape[0] // 2
    loads, stores = [], []
    for i in range(2):
        cut = pl.ds(i * rows, rows)
        for j, (source, target) in enumerate(((dn_ref, dn_out_ref), (at_ref, at_out_ref))):
            loads.append(pltpu.make_async_copy(source.at[cut], held.at[j, cut], load_sem.at[i, j]))
            stores.append(pltpu.make_async_copy(held.at[j, cut], target.at[cut], store_sem.at[i, j]))
    for load in loads:
        load.start()
    for load, store in zip(loads, stores):
        load.wait()
        store.start()
    for store in stores:
        store.wait()


def hand_out(dn_out, at_out):
    far = pl.BlockSpec(memory_space=pl.ANY)
    return pl.pallas_call(
        hand_out_kernel,
        out_shape=[
            jax.ShapeDtypeStruct(dn_out.shape, dn_out.dtype),
            jax.ShapeDtypeStruct(at_out.shape, at_out.dtype),
        ],
        in_specs=[far, far],
        out_specs=[far, far],
        scratch_shapes=[
            pltpu.VMEM((2,) + dn_out.shape, dn_out.dtype),
            pltpu.SemaphoreType.DMA((2, 2)),
            pltpu.SemaphoreType.DMA((2, 2)),
        ],
        compiler_params=pltpu.CompilerParams(vmem_limit_bytes=60 * 2**20),
    )(dn_out, at_out)


def fits_fused(tokens, query_heads, prefix_state, prefix_key):
    size = lax.axis_size("context")
    return (
        tokens == 128
        and size <= 4
        and prefix_state.shape[2] % 16 == 0
        and prefix_key.shape[0] == 2
        and prefix_key.shape[1] % 16 == 0
        and HQ // KVH == 2 * query_heads
    )


def fused(
    dn_query, dn_key, dn_value, dn_gate, dn_beta_logit, dn_decay, dn_norm_gain,
    prefix_state, at_query, at_gate, at_key, at_value, prefix_key, prefix_value,
    req_len, req_prefix, req_offset, block_table,
):
    size = lax.axis_size("context")
    tokens = dn_query.shape[0]
    heads = dn_value.shape[1] // DV
    prefixes, _, state_rows, _ = prefix_state.shape
    width = prefix_key.shape[1]
    longest = size * tokens // 2
    span = min(size - 1, (longest - 1 + tokens - 1) // tokens)
    groups = 4
    bf16, f32 = jnp.bfloat16, jnp.float32
    far = pl.BlockSpec(memory_space=pl.ANY)
    near = pl.BlockSpec(memory_space=pltpu.VMEM)
    small = pl.BlockSpec(memory_space=pltpu.SMEM)
    keys_seen = size * 2 * width + (span + 1) * tokens
    dma = pltpu.SemaphoreType.DMA
    dn_out, at_out = pl.pallas_call(
        lambda *refs: fused_kernel(size, span, *refs),
        out_shape=[
            jax.ShapeDtypeStruct(dn_gate.shape, bf16),
            jax.ShapeDtypeStruct(at_query.shape, bf16),
        ],
        in_specs=[far] * 14 + [small] * 4,
        out_specs=[near, near],
        scratch_shapes=[
            pltpu.VMEM(dn_query.shape, bf16),
            pltpu.VMEM(dn_key.shape, bf16),
            pltpu.VMEM(dn_value.shape, bf16),
            pltpu.VMEM(dn_gate.shape, bf16),
            pltpu.VMEM((heads, tokens), f32),
            pltpu.VMEM((heads, tokens), f32),
            pltpu.VMEM((1, DV), f32),
            pltpu.VMEM(at_query.shape, bf16),
            pltpu.VMEM(at_gate.shape, bf16),
            pltpu.VMEM((tokens, HD), bf16),
            pltpu.VMEM((size, prefixes, heads, state_rows, DK), bf16),
            pltpu.VMEM((2, size, 2, width, HD), bf16),
            pltpu.VMEM((2, span + 1, 2, tokens // 2, HD), bf16),
            pltpu.VMEM((heads, tokens, DV), f32),
            pltpu.VMEM((heads, tokens, DK), bf16),
            pltpu.VMEM((heads, DK, DK), bf16),
            pltpu.VMEM((heads, DV, DK), f32),
            pltpu.VMEM((heads, DV, DK), bf16),
            pltpu.VMEM((heads, DV, DK), bf16),
            pltpu.VMEM((tokens, keys_seen), f32),
            dma((17,)),
            dma((2, size - 1, groups)),
            dma((2, size - 1, groups)),
            dma((size - 1,)),
            dma((size - 1,)),
            dma((span,)),
            dma((span,)),
            dma((2, size - 1)),
            dma((2, size - 1)),
            dma((heads,)),
            dma((heads,)),
            dma((2, size)),
        ],
        compiler_params=pltpu.CompilerParams(
            collective_id=2, has_side_effects=True, vmem_limit_bytes=60 * 2**20
        ),
    )(
        dn_query, dn_key, dn_value, dn_gate, dn_beta_logit.T, dn_decay.T, dn_norm_gain[None, :],
        prefix_state, at_query, at_gate, at_key, at_value, prefix_key, prefix_value,
        req_len, req_prefix, req_offset, block_table,
    )
    return hand_out(dn_out, at_out)


def shards(
    dn_query,
    dn_key,
    dn_value,
    dn_gate,
    dn_beta_logit,
    dn_decay,
    dn_norm_gain,
    prefix_state,
    at_query,
    at_gate,
    at_key,
    at_value,
    prefix_key,
    prefix_value,
    req_len,
    req_prefix,
    req_offset,
    block_table,
):
    tokens_here = dn_query.shape[0]
    value_heads = dn_value.shape[1] // DV
    query_heads = at_query.shape[1] // HD
    if fits_fused(tokens_here, query_heads, prefix_state, prefix_key):
        return fused(
            dn_query, dn_key, dn_value, dn_gate, dn_beta_logit, dn_decay, dn_norm_gain,
            prefix_state, at_query, at_gate, at_key, at_value, prefix_key, prefix_value,
            req_len, req_prefix, req_offset, block_table,
        )
    device = lax.axis_index("context")
    row_start = device * tokens_here
    rows = row_start + jnp.arange(tokens_here, dtype=jnp.int32)
    segment, first, prefix, offset, position = row_layout(rows, req_len, req_prefix, req_offset)
    size = lax.axis_size("context")
    query_heads_here = query_heads
    kv_head = lax.axis_index("head") * query_heads_here // (HQ // KVH)
    cosines, sines = yarn_tables(position, ROT)
    new_key = lax.dynamic_slice_in_dim(at_key, kv_head * HD, HD, 1).reshape(tokens_here, 1, HD)
    new_key = (
        rotate(new_key.astype(jnp.float32), cosines, sines, ROT)
        .reshape(tokens_here, HD)
        .astype(jnp.bfloat16)
    )
    new_value = lax.dynamic_slice_in_dim(at_value, kv_head * HD, HD, 1)
    cached_key = lax.dynamic_slice_in_dim(prefix_key, kv_head * HD, HD, 2)
    cached_value = lax.dynamic_slice_in_dim(prefix_value, kv_head * HD, HD, 2)
    states = jnp.stack([prefix_state] + from_others(prefix_state, "context", size, size))
    states = jnp.concatenate([states[::-1]] * 2)
    states = lax.dynamic_slice_in_dim(states, size - 1 - device, size, 0)
    states = jnp.moveaxis(states, 0, 2)
    states = states.reshape(states.shape[:2] + (-1, DK))
    slots_here = cached_key.shape[0]
    own_block = jnp.concatenate(
        [cached_key.reshape(-1, HD), new_key, cached_value.reshape(-1, HD), new_value]
    ).reshape(2, -1, HD)
    block_rows = own_block.shape[1]
    sharers = HQ // KVH // query_heads
    share = block_rows // sharers
    share_index = lax.axis_index("head") % sharers
    mine = lax.dynamic_slice_in_dim(own_block, share_index * share, share, 1)
    received = jnp.stack(from_others(mine, "context", size, size))
    siblings = from_others(received, "head", lax.axis_size("head"), sharers)
    cached_rows = cached_key.shape[0] * cached_key.shape[1]
    square = (value_heads, DK, DK)
    local_out, reach, map_half, carry_add = whole_call(
        local_kernel,
        [
            jax.ShapeDtypeStruct((value_heads, tokens_here, DV), jnp.float32),
            jax.ShapeDtypeStruct((value_heads, tokens_here, DK), jnp.bfloat16),
            jax.ShapeDtypeStruct(square, jnp.bfloat16),
            jax.ShapeDtypeStruct(square, jnp.float32),
        ],
        dn_query,
        dn_key,
        dn_value,
        dn_beta_logit,
        dn_beta_logit.T,
        dn_decay,
        dn_decay.T,
        segment[:, None],
        segment[None, :],
    )
    restarts = first[tokens_here - 1] >= row_start
    tail_prefix = prefix[tokens_here - 1]
    base = jnp.zeros(states.shape[1:], states.dtype)
    for owner in range(states.shape[0]):
        base = jnp.where(tail_prefix == owner, states[owner], base)
    fresh = jnp.einsum("hvj,hjk->hvk", base, map_half, preferred_element_type=jnp.float32)
    into_state = chain(
        jnp.where(restarts, 0, map_half).astype(jnp.bfloat16),
        carry_add + jnp.where(restarts, fresh, 0.0),
        size,
    )
    carried = (segment == segment[0]) & (first[0] < row_start)
    owner_ids = jnp.arange(states.shape[0], dtype=jnp.int32)
    select = (prefix[None, :] == owner_ids[:, None]) & ~carried[None, :]
    select = jnp.concatenate([select, carried[None, :]], axis=0)
    dn_out = whole_call(
        finish_kernel,
        jax.ShapeDtypeStruct((tokens_here, value_heads * DV), jnp.bfloat16),
        local_out,
        reach,
        states,
        into_state,
        select.astype(jnp.float32).T,
        dn_gate,
        dn_norm_gain[None, :],
    )
    blocks_per_prefix = block_table.shape[0] // prefix_state.shape[0]
    width = cached_key.shape[1]
    others = (device - 1 - jnp.arange(size - 1, dtype=jnp.int32)) % size
    origins = [jnp.full((block_rows,), device, jnp.int32)]
    parts = [jnp.arange(block_rows, dtype=jnp.int32)]
    for step in range(sharers):
        origins.append(jnp.repeat(others, share))
        parts.append(
            (share_index - step) % sharers * share
            + jnp.tile(jnp.arange(share, dtype=jnp.int32), size - 1)
        )
    origin, part = jnp.concatenate(origins), jnp.concatenate(parts)
    slot = origin * slots_here + part // width
    entry = jnp.sum(
        jnp.where(
            block_table[:, None] == slot[None, :],
            jnp.arange(block_table.shape[0], dtype=jnp.int32)[:, None],
            0,
        ),
        axis=0,
    )
    key_row = origin * tokens_here + part - cached_rows
    starts = request_starts(req_len)
    key_segment = jnp.sum((starts[:, None] <= key_row[None, :]).astype(jnp.int32), axis=0) - 1
    old = part < cached_rows
    prefixes = prefix_state.shape[0]
    code = jnp.where(old, entry // blocks_per_prefix, prefixes + key_segment)
    place = jnp.where(old, entry % blocks_per_prefix * width + part % width, key_row)
    ones = jnp.ones((tokens_here, 128 - ROT), jnp.float32)
    at_out = whole_call(
        attend_kernel,
        jax.ShapeDtypeStruct((tokens_here, query_heads * HD), jnp.bfloat16),
        at_query,
        jnp.concatenate([cosines, cosines, ones], axis=1),
        jnp.concatenate([-sines, sines, 0.0 * ones], axis=1),
        at_gate,
        jnp.stack([prefix, offset, prefixes + segment, rows], axis=1),
        code[None, :],
        place[None, :],
        own_block,
        received,
        *siblings,
    )
    return (dn_out, at_out)


def solution(mesh):
    placed = (
        P(("group", "context"), "head"),
        P(("group", "context"), "head"),
        P(("group", "context"), "head"),
        P(("group", "context"), "head"),
        P(("group", "context"), "head"),
        P(("group", "context"), "head"),
        P(),
        P("group", "head", "context", None),
        P(("group", "context"), "head"),
        P(("group", "context"), "head"),
        P(("group", "context"), None),
        P(("group", "context"), None),
        P(("group", "context"), None, None),
        P(("group", "context"), None, None),
        P("group"),
        P("group"),
        P("group"),
        P("group"),
    )
    return jax.shard_map(
        shards,
        mesh=mesh,
        in_specs=placed,
        out_specs=(P(("group", "context"), "head"), P(("group", "context"), "head")),
        check_vma=False,
    )
```

```python
import math

import jax
import jax.numpy as jnp
from jax import lax
from jax.experimental import pallas as pl
from jax.experimental.pallas import tpu as pltpu
from jax.sharding import PartitionSpec as P

VH = 32
KH = 16
DK = 128
DV = 128
HQ = 16
KVH = 2
HD = 256
ROT = 64


ROPE_THETA = 10000000.0
YARN_FACTOR = 4.0
YARN_ANCHOR = 262144.0
NEG_LARGE = -1e30
HIGH = lax.Precision.HIGHEST


def chain_kernel(size, map_ref, add_ref, into_ref, held, leaving, send_sem, recv_sem):
    me = lax.axis_index("context")
    heads = map_ref.shape[0]
    barrier = pltpu.get_barrier_semaphore()
    after, before = lax.rem(me + 1, size), lax.rem(me + size - 1, size)
    for neighbour in (before, after):
        pl.semaphore_signal(barrier, inc=1, device_id={"context": neighbour})
    pl.semaphore_wait(barrier, 2)

    def sent(h):
        return pltpu.make_async_remote_copy(
            src_ref=leaving.at[h],
            dst_ref=held.at[h],
            send_sem=send_sem.at[h],
            recv_sem=recv_sem.at[h],
            device_id={"context": after},
        )

    @pl.when(me == 0)
    def _():
        held[...] = jnp.zeros_like(held)

    for h in range(heads):

        @pl.when(me > 0)
        def _(h=h):
            sent(h).wait_recv()

        leaving[h] = (
            jnp.dot(held[h], map_ref[h], preferred_element_type=jnp.float32) + add_ref[h]
        ).astype(jnp.bfloat16)

        @pl.when(me < size - 1)
        def _(h=h):
            sent(h).start()

    into_ref[...] = held[...]

    @pl.when(me < size - 1)
    def _():
        for h in range(heads):
            sent(h).wait_send()


def chain(carry_map, carry_add, size):
    heads = carry_map.shape[0]
    return pl.pallas_call(
        lambda *refs: chain_kernel(size, *refs),
        out_shape=jax.ShapeDtypeStruct(carry_add.shape, jnp.bfloat16),
        in_specs=[pl.BlockSpec(memory_space=pltpu.VMEM)] * 2,
        out_specs=pl.BlockSpec(memory_space=pltpu.VMEM),
        scratch_shapes=[
            pltpu.VMEM(carry_add.shape, jnp.bfloat16),
            pltpu.VMEM(carry_add.shape, jnp.bfloat16),
            pltpu.SemaphoreType.DMA((heads,)),
            pltpu.SemaphoreType.DMA((heads,)),
        ],
        compiler_params=pltpu.CompilerParams(collective_id=1, has_side_effects=True),
    )(carry_map, carry_add)


def from_others(x, axis, size, span):
    return [
        lax.ppermute(
            x, axis, [(i, i // span * span + (i + step) % span) for i in range(size)]
        )
        for step in range(1, span)
    ]


def halves(x):
    high = x.astype(jnp.bfloat16)
    return high, (x - high.astype(jnp.float32)).astype(jnp.bfloat16)


def dot1(a, b, contract=((1,), (0,))):
    return lax.dot_general(a, b, (contract, ((), ())), preferred_element_type=jnp.float32)


def dot2(a, exact):
    high, low = halves(a)
    return dot1(high, exact) + dot1(low, exact)


def dot3(a, b):
    a_high, a_low = halves(a)
    b_high, b_low = halves(b)
    return dot1(a_high, b_high) + (dot1(a_high, b_low) + dot1(a_low, b_high))


def local_kernel(
    query_ref, key_ref, value_ref, logit_ref, logit_row_ref, decay_ref, decay_row_ref,
    seg_ref, seg_row_ref, local_ref, reach_ref, map_ref, add_ref,
):
    tokens = query_ref.shape[0]
    heads = local_ref.shape[0]
    share = VH // KH
    seg, seg_row = seg_ref[...], seg_row_ref[...]
    row = lax.broadcasted_iota(jnp.int32, (tokens, tokens), 0)
    col = lax.broadcasted_iota(jnp.int32, (tokens, tokens), 1)
    same = seg == seg_row
    causal = same & (row >= col)
    strict = same & (row > col)
    eye = row == col
    causal_f = causal.astype(jnp.float32)
    run = lax.dot_general(
        causal_f, decay_ref[...], (((1,), (0,)), ((), ())),
        precision=HIGH, preferred_element_type=jnp.float32,
    )
    run_row = lax.dot_general(
        decay_row_ref[...], causal_f, (((1,), (1,)), ((), ())),
        precision=HIGH, preferred_element_type=jnp.float32,
    )
    beta, beta_row = jax.nn.sigmoid(logit_ref[...]), jax.nn.sigmoid(logit_row_ref[...])
    start, start_row = jnp.exp(run), jnp.exp(run_row)
    tail = seg_row == seg_row[:, tokens - 1 : tokens]
    end_row = jnp.where(
        tail, jnp.exp(jnp.where(tail, run_row[:, tokens - 1 : tokens] - run_row, 0.0)), 0.0
    )
    keys, grams, mixes, scaled, inv_rows = [], [], [], [], []
    for g in range(heads // share):
        k = key_ref[:, g * DK : (g + 1) * DK]
        q = query_ref[:, g * DK : (g + 1) * DK]
        gram = dot1(k, k, ((1,), (1,)))
        cross = dot1(q, k, ((1,), (1,)))
        squares = jnp.where(eye, gram, 0.0)
        inv = lax.rsqrt(jnp.sum(squares, axis=1, keepdims=True) + 1e-06)
        inv_row = lax.rsqrt(jnp.sum(squares, axis=0, keepdims=True) + 1e-06)
        q_f = q.astype(jnp.float32)
        inv_q = lax.rsqrt(jnp.sum(q_f * q_f, axis=1, keepdims=True) + 1e-06) * DK ** (-0.5)
        keys.append(k)
        inv_rows.append(inv_row)
        grams.append(gram * inv * inv_row)
        mixes.append(cross * inv_q * inv_row)
        scaled.append(q_f * inv_q)
    lowers, inverses, mixing = [], [], []
    for h in range(heads):
        gaps = run[:, h : h + 1] - run_row[h : h + 1, :]
        decay_mat = jnp.where(causal, jnp.exp(jnp.where(causal, gaps, 0.0)), 0.0)
        mixing.append(decay_mat * mixes[h // share])
        lower = jnp.where(strict, beta[:, h : h + 1] * grams[h // share] * decay_mat, 0.0)
        lowers.append(lower)
        inverses.append(
            jnp.where(eye, 1.0, 0.0) - jnp.where(row // 2 == col // 2, lower, 0.0)
        )
    width = 2
    while width < tokens:
        pair = (row // (2 * width) == col // (2 * width)) & (row // width > col // width)
        half = [dot3(jnp.where(pair, lowers[h], 0.0), inverses[h]) for h in range(heads)]
        inverses = [inverses[h] - dot3(inverses[h], half[h]) for h in range(heads)]
        width *= 2
    for h in range(heads):
        g = h // share
        weighted = inverses[h] * beta_row[h : h + 1, :]
        update = dot2(weighted, value_ref[:, h * DV : (h + 1) * DV])
        wy = dot2(weighted * (start_row[h : h + 1, :] * inv_rows[g]), keys[g])
        solved = jnp.concatenate([update, wy], axis=1)
        mixed = dot3(mixing[h], solved)
        local_ref[h] = mixed[:, :DV]
        reach_ref[h] = (start[:, h : h + 1] * scaled[g] - mixed[:, DV:]).astype(jnp.bfloat16)
        turned = solved.T * (end_row[h : h + 1, :] * inv_rows[g])
        carry = dot2(turned, keys[g])
        add_ref[h] = carry[:DV]
        map_ref[h] = (
            jnp.where(eye, start[tokens - 1 : tokens, h : h + 1], 0.0) - carry[DV:]
        ).astype(jnp.bfloat16)


def finish_kernel(local_ref, reach_ref, states_ref, into_ref, select_ref, gate_ref, gain_ref, out_ref):
    owners = states_ref.shape[0]
    select = select_ref[...] > 0.5
    for h in range(local_ref.shape[0]):
        core = local_ref[h]
        reach = reach_ref[h]
        for owner in range(owners + 1):
            state = states_ref[owner, h] if owner < owners else into_ref[h]
            part = dot1(reach, state, ((1,), (1,)))
            core = core + jnp.where(select[:, owner : owner + 1], part, 0.0)
        normed = core * lax.rsqrt(jnp.mean(core * core, axis=1, keepdims=True) + 1e-06)
        gate = gate_ref[:, h * DV : (h + 1) * DV].astype(jnp.float32)
        out_ref[:, h * DV : (h + 1) * DV] = (
            normed * gain_ref[...] * (gate * jax.nn.sigmoid(gate))
        ).astype(jnp.bfloat16)


def attend_kernel(
    query_ref, cos_ref, sin_ref, gate_ref, row_ref, code_ref, place_ref, own_ref, *rest
):
    pieces, out_ref = [own_ref] + list(rest[:-1]), rest[-1]
    tokens = query_ref.shape[0]
    cosines, sines = cos_ref[...], sin_ref[...]
    lane = lax.broadcasted_iota(jnp.int32, (tokens, 128), 1)
    old_code, limit = row_ref[:, 0:1], row_ref[:, 1:2]
    new_code, own_row = row_ref[:, 2:3], row_ref[:, 3:4]
    keys, values, seen, at = [], [], [], 0
    for ref in pieces:
        if len(ref.shape) == 3:
            keys.append(ref[0])
            values.append(ref[1])
        else:
            keys.append(ref[:, 0].reshape(-1, HD))
            values.append(ref[:, 1].reshape(-1, HD))
        count = keys[-1].shape[0]
        code, place = code_ref[:, at : at + count], place_ref[:, at : at + count]
        at += count
        seen.append(
            ((code == old_code) & (place < limit)) | ((code == new_code) & (place <= own_row))
        )
    for h in range(query_ref.shape[1] // HD):
        front = query_ref[:, h * HD : h * HD + 128].astype(jnp.float32)
        swapped = jnp.where(
            lane < ROT // 2, pltpu.roll(front, 128 - ROT // 2, 1), pltpu.roll(front, ROT // 2, 1)
        )
        query = jnp.concatenate(
            [
                (front * cosines + swapped * sines).astype(jnp.bfloat16),
                query_ref[:, h * HD + 128 : (h + 1) * HD],
            ],
            axis=1,
        )
        scores = [
            jnp.where(see, dot1(query, key, ((1,), (1,))) * HD ** (-0.5), NEG_LARGE)
            for see, key in zip(seen, keys)
        ]
        peak = jnp.max(scores[0], axis=1, keepdims=True)
        for score in scores[1:]:
            peak = jnp.maximum(peak, jnp.max(score, axis=1, keepdims=True))
        total, summed = 0.0, 0.0
        for score, see, value in zip(scores, seen, values):
            weight = jnp.where(see, jnp.exp(score - peak), 0.0)
            total = total + jnp.sum(weight, axis=1, keepdims=True)
            summed = summed + dot1(weight.astype(jnp.bfloat16), value)
        gate = gate_ref[:, h * HD : (h + 1) * HD].astype(jnp.float32)
        out_ref[:, h * HD : (h + 1) * HD] = (
            summed / total * jax.nn.sigmoid(gate)
        ).astype(jnp.bfloat16)


def whole_call(kernel, shapes, *arrays):
    space = pl.BlockSpec(memory_space=pltpu.VMEM)
    return pl.pallas_call(
        kernel,
        out_shape=shapes,
        in_specs=[space] * len(arrays),
        out_specs=jax.tree.map(lambda _: space, shapes),
        compiler_params=pltpu.CompilerParams(vmem_limit_bytes=48 * 2**20),
    )(*arrays)


def yarn_tables(positions, rotary):
    half = rotary // 2
    log_theta = math.log(ROPE_THETA)
    lower = max(
        math.floor(rotary * math.log(YARN_ANCHOR / (64.0 * math.pi)) / (2.0 * log_theta)), 0
    )
    upper = min(
        math.ceil(rotary * math.log(YARN_ANCHOR / (2.0 * math.pi)) / (2.0 * log_theta)), rotary - 1
    )
    spread = float(upper - lower)
    index = jnp.arange(half, dtype=jnp.float32)
    plain_frequency = jnp.exp(index * (-2.0 * log_theta / rotary))
    keep = 1.0 - jnp.clip((index - lower) / spread, 0.0, 1.0)
    frequency = plain_frequency * keep + plain_frequency / YARN_FACTOR * (1.0 - keep)
    angles = positions.astype(jnp.float32)[:, None] * frequency[None, :]
    attention_factor = 0.1 * math.log(YARN_FACTOR) + 1.0
    return (jnp.cos(angles) * attention_factor, jnp.sin(angles) * attention_factor)


def rotate(values, cosines, sines, rotary):
    half = rotary // 2
    first = values[..., :half]
    second = values[..., half:rotary]
    cosines = cosines[:, None, :]
    sines = sines[:, None, :]
    return jnp.concatenate(
        [first * cosines - second * sines, second * cosines + first * sines, values[..., rotary:]],
        axis=-1,
    )


def request_starts(req_len):
    order = jnp.arange(req_len.shape[0], dtype=jnp.int32)
    return jnp.sum(jnp.where(order[:, None] < order[None, :], req_len[:, None], 0), axis=0)


def row_layout(rows, req_len, req_prefix, req_offset):
    starts = request_starts(req_len)
    leading_found = (starts[None, :] <= rows[:, None]).astype(jnp.int32)
    segment = jnp.sum(leading_found, axis=1) - 1
    choose = (segment[:, None] == jnp.arange(req_len.shape[0], dtype=jnp.int32)[None, :]).astype(
        jnp.int32
    )
    first = jnp.sum(choose * starts[None, :], axis=1)
    prefix = jnp.sum(choose * req_prefix[None, :], axis=1)
    offset = jnp.sum(choose * req_offset[None, :], axis=1)
    return (segment, first, prefix, offset, offset + rows - first)


def product2(a, exact):
    rows = a.shape[0]
    both = dot1(jnp.concatenate(halves(a), axis=0), exact)
    return both[:rows] + both[rows:]


def product3(left, right):
    rows = left[0].shape[0]
    both = dot1(jnp.concatenate(left, axis=0), right[0])
    return both[:rows] + (both[rows:] + dot1(left[0], right[1]))


def turn(angle):
    quarter = jnp.floor(angle * (2.0 / math.pi) + 0.5)
    rest = angle - quarter * 1.5703125
    rest = rest - quarter * 4.837512969970703125e-4
    rest = rest - quarter * 7.54978995489188216e-8
    square = rest * rest
    sine = rest + rest * square * (
        (-1.9515295891e-4 * square + 8.3321608736e-3) * square - 1.6666654611e-1
    )
    cosine = (
        1.0
        - 0.5 * square
        + square
        * square
        * ((2.443315711809948e-5 * square - 1.388731625493765e-3) * square + 4.166664568298827e-2)
    )
    which = quarter.astype(jnp.int32) & 3
    odd = (which & 1) == 1
    cos_part = jnp.where(odd, sine, cosine)
    sin_part = jnp.where(odd, cosine, sine)
    cos_part = jnp.where((which == 1) | (which == 2), -cos_part, cos_part)
    sin_part = jnp.where(which >= 2, -sin_part, sin_part)
    return cos_part, sin_part


def lane_tables(position):
    half = ROT // 2
    log_theta = math.log(ROPE_THETA)
    lower = max(math.floor(ROT * math.log(YARN_ANCHOR / (64.0 * math.pi)) / (2.0 * log_theta)), 0)
    upper = min(
        math.ceil(ROT * math.log(YARN_ANCHOR / (2.0 * math.pi)) / (2.0 * log_theta)), ROT - 1
    )
    lane = lax.broadcasted_iota(jnp.int32, (1, 128), 1)
    index = (lane % half).astype(jnp.float32)
    plain = jnp.exp(index * (-2.0 * log_theta / ROT))
    keep = 1.0 - jnp.clip((index - lower) / float(upper - lower), 0.0, 1.0)
    frequency = plain * keep + plain / YARN_FACTOR * (1.0 - keep)
    cosine, sine = turn(position.astype(jnp.float32) * frequency)
    factor = 0.1 * math.log(YARN_FACTOR) + 1.0
    cosine = jnp.where(lane < ROT, cosine * factor, 1.0)
    sine = jnp.where(lane < half, -sine * factor, jnp.where(lane < ROT, sine * factor, 0.0))
    return cosine, sine


def roped(front, cosines, sines):
    lane = lax.broadcasted_iota(jnp.int32, front.shape, 1)
    swapped = jnp.where(
        lane < ROT // 2, pltpu.roll(front, 128 - ROT // 2, 1), pltpu.roll(front, ROT // 2, 1)
    )
    return front * cosines + swapped * sines


def fused_kernel(
    size, span,
    query_hbm, key_hbm, value_hbm, gate_hbm, logit_hbm, decay_hbm, gain_hbm, state_hbm,
    atq_hbm, atg_hbm, atk_hbm, atv_hbm, pk_hbm, pv_hbm,
    len_ref, prefix_ref, offset_ref, table_ref,
    dn_out_ref, at_out_ref,
    query_ref, key_ref, value_ref, gate_ref, logit_ref, decay_ref, gain_ref, atq_ref, atg_ref, raw_ref,
    states, cached, fresh,
    local_ref, reach_ref, map_ref, add_ref, held, leaving, bias_ref,
    load_sem, st_send, st_recv, ck_send, ck_recv, nk_send, nk_recv, sib_send, sib_recv,
    chain_send, chain_recv, fw_send,
):
    me = lax.axis_index("context")
    head_at = lax.axis_index("head")
    tokens = query_ref.shape[0]
    heads = local_ref.shape[0]
    share = VH // KH
    prefixes = states.shape[1]
    width = cached.shape[3]
    part = tokens // 2
    lane_half = lax.rem(head_at, 2)
    sibling = head_at + 1 - 2 * lane_half
    kv_head = lax.div(head_at, 2)

    barrier = pltpu.get_barrier_semaphore()
    for step in range(1, size):
        pl.semaphore_signal(
            barrier, inc=1, device_id={"context": lax.rem(me + step, size)}
        )
    pl.semaphore_signal(barrier, inc=1, device_id={"head": sibling})

    columns = pl.ds(pl.multiple_of(kv_head * HD, HD), HD)
    loads = [
        (state_hbm, states.at[me]),
        (atk_hbm.at[:, columns], raw_ref),
        (atv_hbm.at[pl.ds(0, part), columns], fresh.at[1, 0, 0]),
        (atv_hbm.at[pl.ds(part, part), columns], fresh.at[1, 0, 1]),
        (pk_hbm.at[0, :, columns], cached.at[0, me, 0]),
        (pk_hbm.at[1, :, columns], cached.at[0, me, 1]),
        (pv_hbm.at[0, :, columns], cached.at[1, me, 0]),
        (pv_hbm.at[1, :, columns], cached.at[1, me, 1]),
        (decay_hbm, decay_ref),
        (logit_hbm, logit_ref),
        (key_hbm, key_ref),
        (query_hbm, query_ref),
        (value_hbm, value_ref),
        (atq_hbm, atq_ref),
        (atg_hbm, atg_ref),
        (gate_hbm, gate_ref),
        (gain_hbm, gain_ref),
    ]
    loads = [
        pltpu.make_async_copy(source, target, load_sem.at[i])
        for i, (source, target) in enumerate(loads)
    ]
    for load in loads:
        load.start()

    groups = st_send.shape[2]
    group_heads = heads // groups

    def right_ok(s):
        return (me >= s) & (me < size - 1)

    def left_ok(s):
        return (me + s < size) & (me > 0)

    def st_copy(way, s, g, arriving):
        step = 1 if way == 0 else -1
        owner = lax.rem(me - step * (s + (1 if arriving else 0)) + 2 * size, size)
        ref = states.at[owner, :, pl.ds(g * group_heads, group_heads)]
        return pltpu.make_async_remote_copy(
            src_ref=ref, dst_ref=ref,
            send_sem=st_send.at[way, s, g], recv_sem=st_recv.at[way, s, g],
            device_id={"context": lax.rem(me + step + size, size)},
        )

    def state_start(s, g):
        for way, ok in ((0, right_ok), (1, left_ok)):

            @pl.when(ok(s)[0])
            def _(way=way):
                st_copy(way, s, g, False).start()

    def state_arrive(s, g):
        for way, ok in ((0, right_ok), (1, left_ok)):

            @pl.when(ok(s)[1])
            def _(way=way):
                st_copy(way, s, g, True).wait_recv()

    def ck_copy(step, arriving):
        owner = lax.rem(me - step + size, size) if arriving else me
        ref = cached.at[:, owner, lane_half]
        return pltpu.make_async_remote_copy(
            src_ref=ref, dst_ref=ref,
            send_sem=ck_send.at[step - 1], recv_sem=ck_recv.at[step - 1],
            device_id={"context": lax.rem(me + step, size)},
        )

    def nk_copy(step):
        return pltpu.make_async_remote_copy(
            src_ref=fresh.at[:, 0, lane_half], dst_ref=fresh.at[:, step, lane_half],
            send_sem=nk_send.at[step - 1], recv_sem=nk_recv.at[step - 1],
            device_id={"context": lax.rem(me + step, size)},
        )

    def sib_ck(step, arriving):
        owner = lax.rem(me - step + size, size)
        ref = cached.at[:, owner, 1 - lane_half if arriving else lane_half]
        return pltpu.make_async_remote_copy(
            src_ref=ref, dst_ref=ref,
            send_sem=sib_send.at[0, step - 1], recv_sem=sib_recv.at[0, step - 1],
            device_id={"head": sibling},
        )

    def sib_nk(step, arriving):
        ref = fresh.at[:, step, 1 - lane_half if arriving else lane_half]
        return pltpu.make_async_remote_copy(
            src_ref=ref, dst_ref=ref,
            send_sem=sib_send.at[1, step - 1], recv_sem=sib_recv.at[1, step - 1],
            device_id={"head": sibling},
        )

    def chain_copy(h):
        return pltpu.make_async_remote_copy(
            src_ref=leaving.at[h], dst_ref=held.at[h],
            send_sem=chain_send.at[h], recv_sem=chain_recv.at[h],
            device_id={"context": lax.rem(me + 1, size)},
        )

    def state_own(g):
        for way, ok in ((0, right_ok), (1, left_ok)):

            @pl.when(ok(0))
            def _(way=way):
                st_copy(way, 0, g, False).start()

    def state_forward(s, g):
        for way, ok in ((0, right_ok), (1, left_ok)):

            @pl.when(ok(s))
            def _(way=way):
                st_copy(way, s - 1, g, True).wait_recv()
                st_copy(way, s, g, False).start()

    def state_end(g):
        for way, end in ((0, size - 1), (1, 0)):

            @pl.when(me == end)
            def _(way=way):
                for s in range(size - 1):
                    st_copy(way, s, g, True).wait_recv()

    def kv_start(step):
        ck_copy(step, False).start()
        if step <= span:

            @pl.when(me + step < size)
            def _():
                nk_copy(step).start()

    def relayed(step):
        return (me + step == size - 1) & (step > 1)

    def ck_onward(owner):
        ref = cached.at[:, owner, lane_half]
        return pltpu.make_async_remote_copy(
            src_ref=ref, dst_ref=ref,
            send_sem=fw_send.at[0, owner], recv_sem=ck_recv.at[size - 2 - owner],
            device_id={"context": size - 1},
        )

    def nk_onward(owner):
        far = size - 1 - owner
        return pltpu.make_async_remote_copy(
            src_ref=fresh.at[:, far - 1, lane_half], dst_ref=fresh.at[:, far, lane_half],
            send_sem=fw_send.at[1, owner], recv_sem=nk_recv.at[far - 1],
            device_id={"context": size - 1},
        )

    def kv_onward(owner):
        @pl.when(me == size - 2)
        def _():
            near = size - 2 - owner
            ck_copy(near, True).wait_recv()
            ck_onward(owner).start()
            sib_ck(near, False).start()
            if near <= span:
                nk_copy(near).wait_recv()
                sib_nk(near, False).start()
            if near + 1 <= span:
                nk_onward(owner).start()

    def kv_side(rightward):
        for step in range(1, size):
            here = me + step < size if rightward else me + step >= size

            @pl.when(here & jnp.logical_not(relayed(step)))
            def _(step=step):
                kv_start(step)

    def kv_share():
        for step in range(1, size):

            @pl.when((me != size - 2) | (step > me))
            def _(step=step):
                ck_copy(step, True).wait_recv()
                sib_ck(step, False).start()
                if step <= span:

                    @pl.when(me >= step)
                    def _():
                        nk_copy(step).wait_recv()
                        sib_nk(step, False).start()

    def kv_arrive():
        for step in range(1, size):
            sib_ck(step, True).wait_recv()
            if step <= span:

                @pl.when(me >= step)
                def _(step=step):
                    sib_nk(step, True).wait_recv()

    loads[0].wait()
    pl.semaphore_wait(barrier, size)
    for g in range(groups):
        state_own(g)

    row_start = me * tokens
    last_row = row_start + tokens - 1
    requests = len_ref.shape[0]
    starts, total = [], jnp.int32(0)
    for r in range(requests):
        starts.append(total)
        total = total + len_ref[r]

    def layout(rows):
        seg = jnp.zeros_like(rows)
        for r in range(1, requests):
            seg = seg + (rows >= starts[r]).astype(jnp.int32)
        return seg

    rows = row_start + lax.broadcasted_iota(jnp.int32, (tokens, 1), 0)
    seg = layout(rows)
    first, prefix, offset = [jnp.zeros_like(rows)] * 3
    tail_first, tail_prefix, head_seg = jnp.int32(0), prefix_ref[0], jnp.int32(0)
    head_first = jnp.int32(0)
    for r in range(requests):
        first = jnp.where(seg == r, starts[r], first)
        prefix = jnp.where(seg == r, prefix_ref[r], prefix)
        offset = jnp.where(seg == r, offset_ref[r], offset)
        tail_first = jnp.where(starts[r] <= last_row, starts[r], tail_first)
        tail_prefix = jnp.where(starts[r] <= last_row, prefix_ref[r], tail_prefix)
        head_first = jnp.where(starts[r] <= row_start, starts[r], head_first)
        head_seg = jnp.where(starts[r] <= row_start, r, head_seg)
    restarts = tail_first >= row_start
    carried = (seg == head_seg) & (first < row_start)
    row_lane = lax.broadcasted_iota(jnp.int32, (1, tokens), 1)
    seg_row = layout(row_start + row_lane)
    cosines, sines = lane_tables(offset + rows - first)

    for load in loads[1:2]:
        load.wait()
    for j in range(2):
        piece = pl.ds(j * part, part)
        cut = slice(j * part, (j + 1) * part)
        fresh[0, 0, j, :, 0:128] = roped(
            raw_ref[piece, 0:128].astype(jnp.float32), cosines[cut], sines[cut]
        ).astype(jnp.bfloat16)
        fresh[0, 0, j, :, 128:HD] = raw_ref[piece, 128:HD]

    for load in loads[2:8]:
        load.wait()
    kv_side(True)

    for step in range(1, span + 1):

        @pl.when(me < step)
        def _(step=step):
            fresh[:, step] = jnp.zeros_like(fresh[:, step])

    @pl.when(me == 0)
    def _():
        held[...] = jnp.zeros_like(held)

    slots = size * 2
    lanes = lax.broadcasted_iota(jnp.int32, (1, slots * width), 1)
    slot, inside = lanes // width, lanes % width
    per_prefix = table_ref.shape[0] // prefixes
    code, place = jnp.zeros_like(lanes), jnp.zeros_like(lanes)
    for e in range(table_ref.shape[0]):
        here = slot == table_ref[e]
        code = jnp.where(here, e // per_prefix, code)
        place = jnp.where(here, e % per_prefix * width + inside, place)
    bias_ref[:, : slots * width] = jnp.where(
        (code == prefix) & (place < offset), 0.0, NEG_LARGE
    )
    for step in range(span + 1):
        key_row = row_start - step * tokens + row_lane
        seen = (layout(key_row) == seg) & (key_row <= rows) & (key_row >= 0)
        at = slots * width + step * tokens
        bias_ref[:, at : at + tokens] = jnp.where(seen, 0.0, NEG_LARGE)

    row = lax.broadcasted_iota(jnp.int32, (tokens, tokens), 0)
    col = lax.broadcasted_iota(jnp.int32, (tokens, tokens), 1)
    same = seg == seg_row
    causal = same & (row >= col)
    strict = same & (row > col)
    eye = row == col
    causal_f = causal.astype(jnp.float32)
    for load in loads[8:13]:
        load.wait()
    run_row = lax.dot_general(
        decay_ref[...], causal_f, (((1,), (1,)), ((), ())),
        precision=HIGH, preferred_element_type=jnp.float32,
    )
    beta_row = jax.nn.sigmoid(logit_ref[...])
    tail = seg_row == seg_row[:, tokens - 1 : tokens]
    end_row = jnp.where(
        tail, jnp.exp(jnp.where(tail, run_row[:, tokens - 1 : tokens] - run_row, 0.0)), 0.0
    )
    turned = jnp.concatenate(
        [run_row, beta_row, end_row, jnp.zeros((128 - 3 * heads, tokens), jnp.float32)], axis=0
    ).T
    run, beta = turned[:, :heads], turned[:, heads : 2 * heads]
    end = turned[:, 2 * heads : 3 * heads]
    start, start_row = jnp.exp(run), jnp.exp(run_row)
    keys, turned_keys, grams, mixes, scaled, inv_rows, inv_cols = [], [], [], [], [], [], []
    for g in range(heads // share):
        k = key_ref[:, g * DK : (g + 1) * DK]
        q = query_ref[:, g * DK : (g + 1) * DK]
        gram = dot1(k, k, ((1,), (1,)))
        cross = dot1(q, k, ((1,), (1,)))
        squares = jnp.where(eye, gram, 0.0)
        inv = lax.rsqrt(jnp.sum(squares, axis=1, keepdims=True) + 1e-06)
        inv_row = lax.rsqrt(jnp.sum(squares, axis=0, keepdims=True) + 1e-06)
        q_f = q.astype(jnp.float32)
        inv_q = lax.rsqrt(jnp.sum(q_f * q_f, axis=1, keepdims=True) + 1e-06) * DK ** (-0.5)
        keys.append(k)
        turned_keys.append(k.T)
        inv_rows.append(inv_row)
        inv_cols.append(inv)
        grams.append(gram * inv * inv_row)
        mixes.append(cross * inv_q * inv_row)
        scaled.append(q_f * inv_q)
    lowers, inverses, mixing = [], [], []
    for h in range(heads):
        gaps = run[:, h : h + 1] - run_row[h : h + 1, :]
        decay_mat = jnp.where(causal, jnp.exp(jnp.where(causal, gaps, 0.0)), 0.0)
        mixing.append(decay_mat * mixes[h // share])
        lower = jnp.where(strict, beta[:, h : h + 1] * grams[h // share] * decay_mat, 0.0)
        lowers.append(lower)
        inverses.append(
            jnp.where(eye, 1.0, 0.0) - jnp.where((row >> 1) == (col >> 1), lower, 0.0)
        )
    plan = {5: 0, 7: 1, 9: 2, 11: 3}
    ticks = [0]

    def tick():
        if ticks[0] in plan and size > 2:
            state_forward(1, plan[ticks[0]])
        ticks[0] += 1

    splits = [halves(lowers[h]) for h in range(heads)]
    parts = [halves(inverses[h]) for h in range(heads)]
    depth, level = 2, 1
    while depth < tokens:
        pair = ((row >> (level + 1)) == (col >> (level + 1))) & ((row >> level) > (col >> level))
        if depth < 16:
            picks = [(0, tokens)]
        else:
            picks = [(at, depth) for at in range(depth, tokens, 2 * depth)]

        def rows_of(x):
            cuts = [x[at : at + count] for at, count in picks]
            return cuts[0] if len(cuts) == 1 else jnp.concatenate(cuts, axis=0)

        def spread(x):
            if depth < 16:
                return x
            out = []
            for i in range(len(picks)):
                out.append(jnp.zeros((depth, tokens), x.dtype))
                out.append(x[i * depth : (i + 1) * depth])
            return jnp.concatenate(out, axis=0)

        mask = rows_of(pair.astype(jnp.float32)).astype(jnp.bfloat16)
        half = []
        for h in range(heads):
            left = [rows_of(s) * mask for s in splits[h]]
            half.append(product3(left, parts[h]))
        tick()
        for h in range(heads):
            left = [rows_of(p) for p in parts[h]]
            right = tuple(spread(p) for p in halves(half[h]))
            fixed = rows_of(inverses[h]) - product3(left, right)
            if depth < 16:
                inverses[h], parts[h] = fixed, halves(fixed)
            else:
                high, low = halves(fixed)
                whole_f, whole_high, whole_low = [], [], []
                for i, (at, count) in enumerate(picks):
                    cut = slice(i * count, (i + 1) * count)
                    for out, old, now in (
                        (whole_f, inverses[h], fixed),
                        (whole_high, parts[h][0], high),
                        (whole_low, parts[h][1], low),
                    ):
                        out.append(old[at - count : at])
                        out.append(now[cut])
                inverses[h] = jnp.concatenate(whole_f, axis=0)
                parts[h] = (
                    jnp.concatenate(whole_high, axis=0), jnp.concatenate(whole_low, axis=0)
                )
        tick()
        depth, level = depth * 2, level + 1
    weighted = [inverses[h] * beta_row[h : h + 1, :] for h in range(heads)]
    update = [product2(weighted[h], value_ref[:, h * DV : (h + 1) * DV]) for h in range(heads)]
    wy = [
        product2(weighted[h] * (start_row[h : h + 1, :] * inv_rows[h // share]), keys[h // share])
        for h in range(heads)
    ]
    tick()
    solved = [jnp.concatenate([update[h], wy[h]], axis=1) for h in range(heads)]
    carries = []
    for h in range(heads):
        high, low = halves(solved[h] * (end[:, h : h + 1] * inv_cols[h // share]))
        twice = jnp.concatenate([turned_keys[h // share]] * 2, axis=1)
        carries.append(dot1(twice, jnp.concatenate([high, low], axis=0)))
    tick()
    mixed = []
    for h in range(heads):
        mixed.append(product3(halves(mixing[h]), halves(solved[h])))
    tick()
    for h in range(heads):
        add_ref[h] = carries[h][:, :DV]
        map_ref[h] = (
            jnp.where(eye, start[tokens - 1 : tokens, h : h + 1], 0.0) - carries[h][:, DV:]
        ).astype(jnp.bfloat16)
        local_ref[h] = mixed[h][:, :DV]
        reach_ref[h] = (start[:, h : h + 1] * scaled[h // share] - mixed[h][:, DV:]).astype(
            jnp.bfloat16
        )
    for load in loads[13:]:
        load.wait()

    def attend():
        kv_arrive()
        old_keys = cached[0].reshape(-1, HD)
        old_values = cached[1].reshape(-1, HD)
        new_keys = fresh[0].reshape(-1, HD)
        new_values = fresh[1].reshape(-1, HD)
        old_bias, new_bias = bias_ref[:, : slots * width], bias_ref[:, slots * width :]
        for h in range(atq_ref.shape[1] // HD):
            front = atq_ref[:, h * HD : h * HD + 128].astype(jnp.float32)
            rear = atq_ref[:, h * HD + 128 : (h + 1) * HD].astype(jnp.float32)
            turned_front = roped(front, cosines, sines).astype(jnp.bfloat16).astype(jnp.float32)
            query = (
                jnp.concatenate([turned_front, rear], axis=1) * HD ** (-0.5)
            ).astype(jnp.bfloat16)
            old = dot1(query, old_keys, ((1,), (1,))) + old_bias
            new = dot1(query, new_keys, ((1,), (1,))) + new_bias
            peak = jnp.maximum(
                jnp.max(old, axis=1, keepdims=True), jnp.max(new, axis=1, keepdims=True)
            )
            old, new = jnp.exp(old - peak), jnp.exp(new - peak)
            whole = jnp.sum(old, axis=1, keepdims=True) + jnp.sum(new, axis=1, keepdims=True)
            summed = dot1(old.astype(jnp.bfloat16), old_values) + dot1(
                new.astype(jnp.bfloat16), new_values
            )
            gate = atg_ref[:, h * HD : (h + 1) * HD].astype(jnp.float32)
            at_out_ref[:, h * HD : (h + 1) * HD] = (
                summed / whole * jax.nn.sigmoid(gate)
            ).astype(jnp.bfloat16)

    def state_of(p, h):
        return jnp.concatenate([states[o, p, h] for o in range(size)], axis=0)

    def from_prefixes(these):
        own = [(prefix == p) & ~carried for p in range(prefixes)]
        for h in these:
            whole_states = [state_of(p, h) for p in range(prefixes)]
            base = whole_states[0]
            for p in range(1, prefixes):
                base = jnp.where(tail_prefix == p, whole_states[p], base)
            opened = dot1(map_ref[h], base, ((1,), (1,)))
            parts = dot1(reach_ref[h], jnp.concatenate(whole_states, axis=0), ((1,), (1,)))
            core = local_ref[h]
            for p in range(prefixes):
                core = core + jnp.where(own[p], parts[:, p * DV : (p + 1) * DV], 0.0)
            local_ref[h] = core
            add_ref[h] = add_ref[h] + jnp.where(restarts, opened, 0.0)

    for owner in range(size - 3, -1, -1):
        kv_onward(owner)
    for g in range(groups):
        for s in range(2, size - 1):
            state_forward(s, g)
    kv_side(False)
    @pl.when(me == size - 1)
    def _():
        kv_share()
        attend()

    for g in range(groups):
        these = range(g * group_heads, (g + 1) * group_heads)
        state_end(g)
        from_prefixes(these)

        @pl.when(me == 0)
        def _(these=these):
            for h in these:
                leaving[h] = add_ref[h].astype(jnp.bfloat16)
                chain_copy(h).start()


    for h in range(heads):

        @pl.when(me > 0)
        def _(h=h):
            chain_copy(h).wait_recv()

        @pl.when((me > 0) & (me < size - 1))
        def _(h=h):
            onward = dot1(map_ref[h], held[h])
            leaving[h] = (add_ref[h] + jnp.where(restarts, 0.0, onward)).astype(jnp.bfloat16)
            chain_copy(h).start()

        core = local_ref[h] + jnp.where(carried, dot1(reach_ref[h], held[h]), 0.0)
        normed = core * lax.rsqrt(jnp.mean(core * core, axis=1, keepdims=True) + 1e-06)
        gate = gate_ref[:, h * DV : (h + 1) * DV].astype(jnp.float32)
        dn_out_ref[:, h * DV : (h + 1) * DV] = (
            normed * gain_ref[...] * (gate * jax.nn.sigmoid(gate))
        ).astype(jnp.bfloat16)
        if h == heads - 2:

            @pl.when(me < size - 1)
            def _():
                kv_share()

    @pl.when(me < size - 1)
    def _():
        attend()

    for s in range(size - 1):
        for g in range(groups):
            for way, ok in ((0, right_ok), (1, left_ok)):

                @pl.when(ok(s))
                def _(way=way, s=s, g=g):
                    st_copy(way, s, g, False).wait_send()

    for step in range(1, size):
        sib_ck(step, False).wait_send()

        @pl.when(jnp.logical_not(relayed(step)))
        def _(step=step):
            ck_copy(step, False).wait_send()
            if step <= span:

                @pl.when(me + step < size)
                def _():
                    nk_copy(step).wait_send()

        if step <= span:

            @pl.when(me >= step)
            def _(step=step):
                sib_nk(step, False).wait_send()

    @pl.when(me == size - 2)
    def _():
        for owner in range(size - 2):
            ck_onward(owner).wait_send()
            if size - 1 - owner <= span:
                nk_onward(owner).wait_send()

    @pl.when(me < size - 1)
    def _():
        for h in range(heads):
            chain_copy(h).wait_send()


def hand_out_kernel(dn_ref, at_ref, dn_out_ref, at_out_ref, held, load_sem, store_sem):
    rows = dn_ref.shape[0] // 2
    loads, stores = [], []
    for i in range(2):
        cut = pl.ds(i * rows, rows)
        for j, (source, target) in enumerate(((dn_ref, dn_out_ref), (at_ref, at_out_ref))):
            loads.append(pltpu.make_async_copy(source.at[cut], held.at[j, cut], load_sem.at[i, j]))
            stores.append(pltpu.make_async_copy(held.at[j, cut], target.at[cut], store_sem.at[i, j]))
    for load in loads:
        load.start()
    for load, store in zip(loads, stores):
        load.wait()
        store.start()
    for store in stores:
        store.wait()


def hand_out(dn_out, at_out):
    far = pl.BlockSpec(memory_space=pl.ANY)
    return pl.pallas_call(
        hand_out_kernel,
        out_shape=[
            jax.ShapeDtypeStruct(dn_out.shape, dn_out.dtype),
            jax.ShapeDtypeStruct(at_out.shape, at_out.dtype),
        ],
        in_specs=[far, far],
        out_specs=[far, far],
        scratch_shapes=[
            pltpu.VMEM((2,) + dn_out.shape, dn_out.dtype),
            pltpu.SemaphoreType.DMA((2, 2)),
            pltpu.SemaphoreType.DMA((2, 2)),
        ],
        compiler_params=pltpu.CompilerParams(vmem_limit_bytes=60 * 2**20),
    )(dn_out, at_out)


def fits_fused(tokens, query_heads, prefix_state, prefix_key):
    size = lax.axis_size("context")
    return (
        tokens == 128
        and size <= 4
        and prefix_state.shape[2] % 16 == 0
        and prefix_key.shape[0] == 2
        and prefix_key.shape[1] % 16 == 0
        and HQ // KVH == 2 * query_heads
    )


def fused(
    dn_query, dn_key, dn_value, dn_gate, dn_beta_logit, dn_decay, dn_norm_gain,
    prefix_state, at_query, at_gate, at_key, at_value, prefix_key, prefix_value,
    req_len, req_prefix, req_offset, block_table,
):
    size = lax.axis_size("context")
    tokens = dn_query.shape[0]
    heads = dn_value.shape[1] // DV
    prefixes, _, state_rows, _ = prefix_state.shape
    width = prefix_key.shape[1]
    longest = size * tokens // 2
    span = min(size - 1, (longest - 1 + tokens - 1) // tokens)
    groups = 4
    bf16, f32 = jnp.bfloat16, jnp.float32
    far = pl.BlockSpec(memory_space=pl.ANY)
    near = pl.BlockSpec(memory_space=pltpu.VMEM)
    small = pl.BlockSpec(memory_space=pltpu.SMEM)
    keys_seen = size * 2 * width + (span + 1) * tokens
    dma = pltpu.SemaphoreType.DMA
    dn_out, at_out = pl.pallas_call(
        lambda *refs: fused_kernel(size, span, *refs),
        out_shape=[
            jax.ShapeDtypeStruct(dn_gate.shape, bf16),
            jax.ShapeDtypeStruct(at_query.shape, bf16),
        ],
        in_specs=[far] * 14 + [small] * 4,
        out_specs=[near, near],
        scratch_shapes=[
            pltpu.VMEM(dn_query.shape, bf16),
            pltpu.VMEM(dn_key.shape, bf16),
            pltpu.VMEM(dn_value.shape, bf16),
            pltpu.VMEM(dn_gate.shape, bf16),
            pltpu.VMEM((heads, tokens), f32),
            pltpu.VMEM((heads, tokens), f32),
            pltpu.VMEM((1, DV), f32),
            pltpu.VMEM(at_query.shape, bf16),
            pltpu.VMEM(at_gate.shape, bf16),
            pltpu.VMEM((tokens, HD), bf16),
            pltpu.VMEM((size, prefixes, heads, state_rows, DK), bf16),
            pltpu.VMEM((2, size, 2, width, HD), bf16),
            pltpu.VMEM((2, span + 1, 2, tokens // 2, HD), bf16),
            pltpu.VMEM((heads, tokens, DV), f32),
            pltpu.VMEM((heads, tokens, DK), bf16),
            pltpu.VMEM((heads, DK, DK), bf16),
            pltpu.VMEM((heads, DV, DK), f32),
            pltpu.VMEM((heads, DV, DK), bf16),
            pltpu.VMEM((heads, DV, DK), bf16),
            pltpu.VMEM((tokens, keys_seen), f32),
            dma((17,)),
            dma((2, size - 1, groups)),
            dma((2, size - 1, groups)),
            dma((size - 1,)),
            dma((size - 1,)),
            dma((span,)),
            dma((span,)),
            dma((2, size - 1)),
            dma((2, size - 1)),
            dma((heads,)),
            dma((heads,)),
            dma((2, size)),
        ],
        compiler_params=pltpu.CompilerParams(
            collective_id=2, has_side_effects=True, vmem_limit_bytes=60 * 2**20
        ),
    )(
        dn_query, dn_key, dn_value, dn_gate, dn_beta_logit.T, dn_decay.T, dn_norm_gain[None, :],
        prefix_state, at_query, at_gate, at_key, at_value, prefix_key, prefix_value,
        req_len, req_prefix, req_offset, block_table,
    )
    return hand_out(dn_out, at_out)


def shards(
    dn_query,
    dn_key,
    dn_value,
    dn_gate,
    dn_beta_logit,
    dn_decay,
    dn_norm_gain,
    prefix_state,
    at_query,
    at_gate,
    at_key,
    at_value,
    prefix_key,
    prefix_value,
    req_len,
    req_prefix,
    req_offset,
    block_table,
):
    tokens_here = dn_query.shape[0]
    value_heads = dn_value.shape[1] // DV
    query_heads = at_query.shape[1] // HD
    if fits_fused(tokens_here, query_heads, prefix_state, prefix_key):
        return fused(
            dn_query, dn_key, dn_value, dn_gate, dn_beta_logit, dn_decay, dn_norm_gain,
            prefix_state, at_query, at_gate, at_key, at_value, prefix_key, prefix_value,
            req_len, req_prefix, req_offset, block_table,
        )
    device = lax.axis_index("context")
    row_start = device * tokens_here
    rows = row_start + jnp.arange(tokens_here, dtype=jnp.int32)
    segment, first, prefix, offset, position = row_layout(rows, req_len, req_prefix, req_offset)
    size = lax.axis_size("context")
    query_heads_here = query_heads
    kv_head = lax.axis_index("head") * query_heads_here // (HQ // KVH)
    cosines, sines = yarn_tables(position, ROT)
    new_key = lax.dynamic_slice_in_dim(at_key, kv_head * HD, HD, 1).reshape(tokens_here, 1, HD)
    new_key = (
        rotate(new_key.astype(jnp.float32), cosines, sines, ROT)
        .reshape(tokens_here, HD)
        .astype(jnp.bfloat16)
    )
    new_value = lax.dynamic_slice_in_dim(at_value, kv_head * HD, HD, 1)
    cached_key = lax.dynamic_slice_in_dim(prefix_key, kv_head * HD, HD, 2)
    cached_value = lax.dynamic_slice_in_dim(prefix_value, kv_head * HD, HD, 2)
    states = jnp.stack([prefix_state] + from_others(prefix_state, "context", size, size))
    states = jnp.concatenate([states[::-1]] * 2)
    states = lax.dynamic_slice_in_dim(states, size - 1 - device, size, 0)
    states = jnp.moveaxis(states, 0, 2)
    states = states.reshape(states.shape[:2] + (-1, DK))
    slots_here = cached_key.shape[0]
    own_block = jnp.concatenate(
        [cached_key.reshape(-1, HD), new_key, cached_value.reshape(-1, HD), new_value]
    ).reshape(2, -1, HD)
    block_rows = own_block.shape[1]
    sharers = HQ // KVH // query_heads
    share = block_rows // sharers
    share_index = lax.axis_index("head") % sharers
    mine = lax.dynamic_slice_in_dim(own_block, share_index * share, share, 1)
    received = jnp.stack(from_others(mine, "context", size, size))
    siblings = from_others(received, "head", lax.axis_size("head"), sharers)
    cached_rows = cached_key.shape[0] * cached_key.shape[1]
    square = (value_heads, DK, DK)
    local_out, reach, map_half, carry_add = whole_call(
        local_kernel,
        [
            jax.ShapeDtypeStruct((value_heads, tokens_here, DV), jnp.float32),
            jax.ShapeDtypeStruct((value_heads, tokens_here, DK), jnp.bfloat16),
            jax.ShapeDtypeStruct(square, jnp.bfloat16),
            jax.ShapeDtypeStruct(square, jnp.float32),
        ],
        dn_query,
        dn_key,
        dn_value,
        dn_beta_logit,
        dn_beta_logit.T,
        dn_decay,
        dn_decay.T,
        segment[:, None],
        segment[None, :],
    )
    restarts = first[tokens_here - 1] >= row_start
    tail_prefix = prefix[tokens_here - 1]
    base = jnp.zeros(states.shape[1:], states.dtype)
    for owner in range(states.shape[0]):
        base = jnp.where(tail_prefix == owner, states[owner], base)
    fresh = jnp.einsum("hvj,hjk->hvk", base, map_half, preferred_element_type=jnp.float32)
    into_state = chain(
        jnp.where(restarts, 0, map_half).astype(jnp.bfloat16),
        carry_add + jnp.where(restarts, fresh, 0.0),
        size,
    )
    carried = (segment == segment[0]) & (first[0] < row_start)
    owner_ids = jnp.arange(states.shape[0], dtype=jnp.int32)
    select = (prefix[None, :] == owner_ids[:, None]) & ~carried[None, :]
    select = jnp.concatenate([select, carried[None, :]], axis=0)
    dn_out = whole_call(
        finish_kernel,
        jax.ShapeDtypeStruct((tokens_here, value_heads * DV), jnp.bfloat16),
        local_out,
        reach,
        states,
        into_state,
        select.astype(jnp.float32).T,
        dn_gate,
        dn_norm_gain[None, :],
    )
    blocks_per_prefix = block_table.shape[0] // prefix_state.shape[0]
    width = cached_key.shape[1]
    others = (device - 1 - jnp.arange(size - 1, dtype=jnp.int32)) % size
    origins = [jnp.full((block_rows,), device, jnp.int32)]
    parts = [jnp.arange(block_rows, dtype=jnp.int32)]
    for step in range(sharers):
        origins.append(jnp.repeat(others, share))
        parts.append(
            (share_index - step) % sharers * share
            + jnp.tile(jnp.arange(share, dtype=jnp.int32), size - 1)
        )
    origin, part = jnp.concatenate(origins), jnp.concatenate(parts)
    slot = origin * slots_here + part // width
    entry = jnp.sum(
        jnp.where(
            block_table[:, None] == slot[None, :],
            jnp.arange(block_table.shape[0], dtype=jnp.int32)[:, None],
            0,
        ),
        axis=0,
    )
    key_row = origin * tokens_here + part - cached_rows
    starts = request_starts(req_len)
    key_segment = jnp.sum((starts[:, None] <= key_row[None, :]).astype(jnp.int32), axis=0) - 1
    old = part < cached_rows
    prefixes = prefix_state.shape[0]
    code = jnp.where(old, entry // blocks_per_prefix, prefixes + key_segment)
    place = jnp.where(old, entry % blocks_per_prefix * width + part % width, key_row)
    ones = jnp.ones((tokens_here, 128 - ROT), jnp.float32)
    at_out = whole_call(
        attend_kernel,
        jax.ShapeDtypeStruct((tokens_here, query_heads * HD), jnp.bfloat16),
        at_query,
        jnp.concatenate([cosines, cosines, ones], axis=1),
        jnp.concatenate([-sines, sines, 0.0 * ones], axis=1),
        at_gate,
        jnp.stack([prefix, offset, prefixes + segment, rows], axis=1),
        code[None, :],
        place[None, :],
        own_block,
        received,
        *siblings,
    )
    return (dn_out, at_out)


def solution(mesh):
    placed = (
        P(("group", "context"), "head"),
        P(("group", "context"), "head"),
        P(("group", "context"), "head"),
        P(("group", "context"), "head"),
        P(("group", "context"), "head"),
        P(("group", "context"), "head"),
        P(),
        P("group", "head", "context", None),
        P(("group", "context"), "head"),
        P(("group", "context"), "head"),
        P(("group", "context"), None),
        P(("group", "context"), None),
        P(("group", "context"), None, None),
        P(("group", "context"), None, None),
        P("group"),
        P("group"),
        P("group"),
        P("group"),
    )
    return jax.shard_map(
        shards,
        mesh=mesh,
        in_specs=placed,
        out_specs=(P(("group", "context"), "head"), P(("group", "context"), "head")),
        check_vma=False,
    )
```

```python
import math

import jax
import jax.numpy as jnp
from jax import lax
from jax.experimental import pallas as pl
from jax.experimental.pallas import tpu as pltpu
from jax.sharding import PartitionSpec as P

VH = 32
KH = 16
DK = 128
DV = 128
HQ = 16
KVH = 2
HD = 256
ROT = 64


ROPE_THETA = 10000000.0
YARN_FACTOR = 4.0
YARN_ANCHOR = 262144.0
NEG_LARGE = -1e30
HIGH = lax.Precision.HIGHEST


def chain_kernel(size, map_ref, add_ref, into_ref, held, leaving, send_sem, recv_sem):
    me = lax.axis_index("context")
    heads = map_ref.shape[0]
    barrier = pltpu.get_barrier_semaphore()
    after, before = lax.rem(me + 1, size), lax.rem(me + size - 1, size)
    for neighbour in (before, after):
        pl.semaphore_signal(barrier, inc=1, device_id={"context": neighbour})
    pl.semaphore_wait(barrier, 2)

    def sent(h):
        return pltpu.make_async_remote_copy(
            src_ref=leaving.at[h],
            dst_ref=held.at[h],
            send_sem=send_sem.at[h],
            recv_sem=recv_sem.at[h],
            device_id={"context": after},
        )

    @pl.when(me == 0)
    def _():
        held[...] = jnp.zeros_like(held)

    for h in range(heads):

        @pl.when(me > 0)
        def _(h=h):
            sent(h).wait_recv()

        leaving[h] = (
            jnp.dot(held[h], map_ref[h], preferred_element_type=jnp.float32) + add_ref[h]
        ).astype(jnp.bfloat16)

        @pl.when(me < size - 1)
        def _(h=h):
            sent(h).start()

    into_ref[...] = held[...]

    @pl.when(me < size - 1)
    def _():
        for h in range(heads):
            sent(h).wait_send()


def chain(carry_map, carry_add, size):
    heads = carry_map.shape[0]
    return pl.pallas_call(
        lambda *refs: chain_kernel(size, *refs),
        out_shape=jax.ShapeDtypeStruct(carry_add.shape, jnp.bfloat16),
        in_specs=[pl.BlockSpec(memory_space=pltpu.VMEM)] * 2,
        out_specs=pl.BlockSpec(memory_space=pltpu.VMEM),
        scratch_shapes=[
            pltpu.VMEM(carry_add.shape, jnp.bfloat16),
            pltpu.VMEM(carry_add.shape, jnp.bfloat16),
            pltpu.SemaphoreType.DMA((heads,)),
            pltpu.SemaphoreType.DMA((heads,)),
        ],
        compiler_params=pltpu.CompilerParams(collective_id=1, has_side_effects=True),
    )(carry_map, carry_add)


def from_others(x, axis, size, span):
    return [
        lax.ppermute(
            x, axis, [(i, i // span * span + (i + step) % span) for i in range(size)]
        )
        for step in range(1, span)
    ]


def halves(x):
    high = x.astype(jnp.bfloat16)
    return high, (x - high.astype(jnp.float32)).astype(jnp.bfloat16)


def dot1(a, b, contract=((1,), (0,))):
    return lax.dot_general(a, b, (contract, ((), ())), preferred_element_type=jnp.float32)


def dot2(a, exact):
    high, low = halves(a)
    return dot1(high, exact) + dot1(low, exact)


def dot3(a, b):
    a_high, a_low = halves(a)
    b_high, b_low = halves(b)
    return dot1(a_high, b_high) + (dot1(a_high, b_low) + dot1(a_low, b_high))


def local_kernel(
    query_ref, key_ref, value_ref, logit_ref, logit_row_ref, decay_ref, decay_row_ref,
    seg_ref, seg_row_ref, local_ref, reach_ref, map_ref, add_ref,
):
    tokens = query_ref.shape[0]
    heads = local_ref.shape[0]
    share = VH // KH
    seg, seg_row = seg_ref[...], seg_row_ref[...]
    row = lax.broadcasted_iota(jnp.int32, (tokens, tokens), 0)
    col = lax.broadcasted_iota(jnp.int32, (tokens, tokens), 1)
    same = seg == seg_row
    causal = same & (row >= col)
    strict = same & (row > col)
    eye = row == col
    causal_f = causal.astype(jnp.float32)
    run = lax.dot_general(
        causal_f, decay_ref[...], (((1,), (0,)), ((), ())),
        precision=HIGH, preferred_element_type=jnp.float32,
    )
    run_row = lax.dot_general(
        decay_row_ref[...], causal_f, (((1,), (1,)), ((), ())),
        precision=HIGH, preferred_element_type=jnp.float32,
    )
    beta, beta_row = jax.nn.sigmoid(logit_ref[...]), jax.nn.sigmoid(logit_row_ref[...])
    start, start_row = jnp.exp(run), jnp.exp(run_row)
    tail = seg_row == seg_row[:, tokens - 1 : tokens]
    end_row = jnp.where(
        tail, jnp.exp(jnp.where(tail, run_row[:, tokens - 1 : tokens] - run_row, 0.0)), 0.0
    )
    keys, grams, mixes, scaled, inv_rows = [], [], [], [], []
    for g in range(heads // share):
        k = key_ref[:, g * DK : (g + 1) * DK]
        q = query_ref[:, g * DK : (g + 1) * DK]
        gram = dot1(k, k, ((1,), (1,)))
        cross = dot1(q, k, ((1,), (1,)))
        squares = jnp.where(eye, gram, 0.0)
        inv = lax.rsqrt(jnp.sum(squares, axis=1, keepdims=True) + 1e-06)
        inv_row = lax.rsqrt(jnp.sum(squares, axis=0, keepdims=True) + 1e-06)
        q_f = q.astype(jnp.float32)
        inv_q = lax.rsqrt(jnp.sum(q_f * q_f, axis=1, keepdims=True) + 1e-06) * DK ** (-0.5)
        keys.append(k)
        inv_rows.append(inv_row)
        grams.append(gram * inv * inv_row)
        mixes.append(cross * inv_q * inv_row)
        scaled.append(q_f * inv_q)
    lowers, inverses, mixing = [], [], []
    for h in range(heads):
        gaps = run[:, h : h + 1] - run_row[h : h + 1, :]
        decay_mat = jnp.where(causal, jnp.exp(jnp.where(causal, gaps, 0.0)), 0.0)
        mixing.append(decay_mat * mixes[h // share])
        lower = jnp.where(strict, beta[:, h : h + 1] * grams[h // share] * decay_mat, 0.0)
        lowers.append(lower)
        inverses.append(
            jnp.where(eye, 1.0, 0.0) - jnp.where(row // 2 == col // 2, lower, 0.0)
        )
    width = 2
    while width < tokens:
        pair = (row // (2 * width) == col // (2 * width)) & (row // width > col // width)
        half = [dot3(jnp.where(pair, lowers[h], 0.0), inverses[h]) for h in range(heads)]
        inverses = [inverses[h] - dot3(inverses[h], half[h]) for h in range(heads)]
        width *= 2
    for h in range(heads):
        g = h // share
        weighted = inverses[h] * beta_row[h : h + 1, :]
        update = dot2(weighted, value_ref[:, h * DV : (h + 1) * DV])
        wy = dot2(weighted * (start_row[h : h + 1, :] * inv_rows[g]), keys[g])
        solved = jnp.concatenate([update, wy], axis=1)
        mixed = dot3(mixing[h], solved)
        local_ref[h] = mixed[:, :DV]
        reach_ref[h] = (start[:, h : h + 1] * scaled[g] - mixed[:, DV:]).astype(jnp.bfloat16)
        turned = solved.T * (end_row[h : h + 1, :] * inv_rows[g])
        carry = dot2(turned, keys[g])
        add_ref[h] = carry[:DV]
        map_ref[h] = (
            jnp.where(eye, start[tokens - 1 : tokens, h : h + 1], 0.0) - carry[DV:]
        ).astype(jnp.bfloat16)


def finish_kernel(local_ref, reach_ref, states_ref, into_ref, select_ref, gate_ref, gain_ref, out_ref):
    owners = states_ref.shape[0]
    select = select_ref[...] > 0.5
    for h in range(local_ref.shape[0]):
        core = local_ref[h]
        reach = reach_ref[h]
        for owner in range(owners + 1):
            state = states_ref[owner, h] if owner < owners else into_ref[h]
            part = dot1(reach, state, ((1,), (1,)))
            core = core + jnp.where(select[:, owner : owner + 1], part, 0.0)
        normed = core * lax.rsqrt(jnp.mean(core * core, axis=1, keepdims=True) + 1e-06)
        gate = gate_ref[:, h * DV : (h + 1) * DV].astype(jnp.float32)
        out_ref[:, h * DV : (h + 1) * DV] = (
            normed * gain_ref[...] * (gate * jax.nn.sigmoid(gate))
        ).astype(jnp.bfloat16)


def attend_kernel(
    query_ref, cos_ref, sin_ref, gate_ref, row_ref, code_ref, place_ref, own_ref, *rest
):
    pieces, out_ref = [own_ref] + list(rest[:-1]), rest[-1]
    tokens = query_ref.shape[0]
    cosines, sines = cos_ref[...], sin_ref[...]
    lane = lax.broadcasted_iota(jnp.int32, (tokens, 128), 1)
    old_code, limit = row_ref[:, 0:1], row_ref[:, 1:2]
    new_code, own_row = row_ref[:, 2:3], row_ref[:, 3:4]
    keys, values, seen, at = [], [], [], 0
    for ref in pieces:
        if len(ref.shape) == 3:
            keys.append(ref[0])
            values.append(ref[1])
        else:
            keys.append(ref[:, 0].reshape(-1, HD))
            values.append(ref[:, 1].reshape(-1, HD))
        count = keys[-1].shape[0]
        code, place = code_ref[:, at : at + count], place_ref[:, at : at + count]
        at += count
        seen.append(
            ((code == old_code) & (place < limit)) | ((code == new_code) & (place <= own_row))
        )
    for h in range(query_ref.shape[1] // HD):
        front = query_ref[:, h * HD : h * HD + 128].astype(jnp.float32)
        swapped = jnp.where(
            lane < ROT // 2, pltpu.roll(front, 128 - ROT // 2, 1), pltpu.roll(front, ROT // 2, 1)
        )
        query = jnp.concatenate(
            [
                (front * cosines + swapped * sines).astype(jnp.bfloat16),
                query_ref[:, h * HD + 128 : (h + 1) * HD],
            ],
            axis=1,
        )
        scores = [
            jnp.where(see, dot1(query, key, ((1,), (1,))) * HD ** (-0.5), NEG_LARGE)
            for see, key in zip(seen, keys)
        ]
        peak = jnp.max(scores[0], axis=1, keepdims=True)
        for score in scores[1:]:
            peak = jnp.maximum(peak, jnp.max(score, axis=1, keepdims=True))
        total, summed = 0.0, 0.0
        for score, see, value in zip(scores, seen, values):
            weight = jnp.where(see, jnp.exp(score - peak), 0.0)
            total = total + jnp.sum(weight, axis=1, keepdims=True)
            summed = summed + dot1(weight.astype(jnp.bfloat16), value)
        gate = gate_ref[:, h * HD : (h + 1) * HD].astype(jnp.float32)
        out_ref[:, h * HD : (h + 1) * HD] = (
            summed / total * jax.nn.sigmoid(gate)
        ).astype(jnp.bfloat16)


def whole_call(kernel, shapes, *arrays):
    space = pl.BlockSpec(memory_space=pltpu.VMEM)
    return pl.pallas_call(
        kernel,
        out_shape=shapes,
        in_specs=[space] * len(arrays),
        out_specs=jax.tree.map(lambda _: space, shapes),
        compiler_params=pltpu.CompilerParams(vmem_limit_bytes=48 * 2**20),
    )(*arrays)


def yarn_tables(positions, rotary):
    half = rotary // 2
    log_theta = math.log(ROPE_THETA)
    lower = max(
        math.floor(rotary * math.log(YARN_ANCHOR / (64.0 * math.pi)) / (2.0 * log_theta)), 0
    )
    upper = min(
        math.ceil(rotary * math.log(YARN_ANCHOR / (2.0 * math.pi)) / (2.0 * log_theta)), rotary - 1
    )
    spread = float(upper - lower)
    index = jnp.arange(half, dtype=jnp.float32)
    plain_frequency = jnp.exp(index * (-2.0 * log_theta / rotary))
    keep = 1.0 - jnp.clip((index - lower) / spread, 0.0, 1.0)
    frequency = plain_frequency * keep + plain_frequency / YARN_FACTOR * (1.0 - keep)
    angles = positions.astype(jnp.float32)[:, None] * frequency[None, :]
    attention_factor = 0.1 * math.log(YARN_FACTOR) + 1.0
    return (jnp.cos(angles) * attention_factor, jnp.sin(angles) * attention_factor)


def rotate(values, cosines, sines, rotary):
    half = rotary // 2
    first = values[..., :half]
    second = values[..., half:rotary]
    cosines = cosines[:, None, :]
    sines = sines[:, None, :]
    return jnp.concatenate(
        [first * cosines - second * sines, second * cosines + first * sines, values[..., rotary:]],
        axis=-1,
    )


def request_starts(req_len):
    order = jnp.arange(req_len.shape[0], dtype=jnp.int32)
    return jnp.sum(jnp.where(order[:, None] < order[None, :], req_len[:, None], 0), axis=0)


def row_layout(rows, req_len, req_prefix, req_offset):
    starts = request_starts(req_len)
    leading_found = (starts[None, :] <= rows[:, None]).astype(jnp.int32)
    segment = jnp.sum(leading_found, axis=1) - 1
    choose = (segment[:, None] == jnp.arange(req_len.shape[0], dtype=jnp.int32)[None, :]).astype(
        jnp.int32
    )
    first = jnp.sum(choose * starts[None, :], axis=1)
    prefix = jnp.sum(choose * req_prefix[None, :], axis=1)
    offset = jnp.sum(choose * req_offset[None, :], axis=1)
    return (segment, first, prefix, offset, offset + rows - first)


def product2(a, exact):
    rows = a.shape[0]
    both = dot1(jnp.concatenate(halves(a), axis=0), exact)
    return both[:rows] + both[rows:]


def product3(left, right):
    rows = left[0].shape[0]
    both = dot1(jnp.concatenate(left, axis=0), right[0])
    return both[:rows] + (both[rows:] + dot1(left[0], right[1]))


def turn(angle):
    quarter = jnp.floor(angle * (2.0 / math.pi) + 0.5)
    rest = angle - quarter * 1.5703125
    rest = rest - quarter * 4.837512969970703125e-4
    rest = rest - quarter * 7.54978995489188216e-8
    square = rest * rest
    sine = rest + rest * square * (
        (-1.9515295891e-4 * square + 8.3321608736e-3) * square - 1.6666654611e-1
    )
    cosine = (
        1.0
        - 0.5 * square
        + square
        * square
        * ((2.443315711809948e-5 * square - 1.388731625493765e-3) * square + 4.166664568298827e-2)
    )
    which = quarter.astype(jnp.int32) & 3
    odd = (which & 1) == 1
    cos_part = jnp.where(odd, sine, cosine)
    sin_part = jnp.where(odd, cosine, sine)
    cos_part = jnp.where((which == 1) | (which == 2), -cos_part, cos_part)
    sin_part = jnp.where(which >= 2, -sin_part, sin_part)
    return cos_part, sin_part


def lane_tables(position):
    half = ROT // 2
    log_theta = math.log(ROPE_THETA)
    lower = max(math.floor(ROT * math.log(YARN_ANCHOR / (64.0 * math.pi)) / (2.0 * log_theta)), 0)
    upper = min(
        math.ceil(ROT * math.log(YARN_ANCHOR / (2.0 * math.pi)) / (2.0 * log_theta)), ROT - 1
    )
    lane = lax.broadcasted_iota(jnp.int32, (1, 128), 1)
    index = (lane % half).astype(jnp.float32)
    plain = jnp.exp(index * (-2.0 * log_theta / ROT))
    keep = 1.0 - jnp.clip((index - lower) / float(upper - lower), 0.0, 1.0)
    frequency = plain * keep + plain / YARN_FACTOR * (1.0 - keep)
    cosine, sine = turn(position.astype(jnp.float32) * frequency)
    factor = 0.1 * math.log(YARN_FACTOR) + 1.0
    cosine = jnp.where(lane < ROT, cosine * factor, 1.0)
    sine = jnp.where(lane < half, -sine * factor, jnp.where(lane < ROT, sine * factor, 0.0))
    return cosine, sine


def roped(front, cosines, sines):
    lane = lax.broadcasted_iota(jnp.int32, front.shape, 1)
    swapped = jnp.where(
        lane < ROT // 2, pltpu.roll(front, 128 - ROT // 2, 1), pltpu.roll(front, ROT // 2, 1)
    )
    return front * cosines + swapped * sines


def fused_kernel(
    size, span,
    query_hbm, key_hbm, value_hbm, gate_hbm, logit_hbm, decay_hbm, gain_hbm, state_hbm,
    atq_hbm, atg_hbm, atk_hbm, atv_hbm, pk_hbm, pv_hbm,
    len_ref, prefix_ref, offset_ref, table_ref,
    dn_out_ref, at_out_ref,
    query_ref, key_ref, value_ref, gate_ref, logit_ref, decay_ref, gain_ref, atq_ref, atg_ref, raw_ref,
    states, cached, fresh,
    local_ref, reach_ref, map_ref, add_ref, held, leaving, bias_ref,
    load_sem, st_send, st_recv, ck_send, ck_recv, nk_send, nk_recv, sib_send, sib_recv,
    chain_send, chain_recv, fw_send,
):
    me = lax.axis_index("context")
    head_at = lax.axis_index("head")
    tokens = query_ref.shape[0]
    heads = local_ref.shape[0]
    share = VH // KH
    prefixes = states.shape[1]
    width = cached.shape[3]
    part = tokens // 2
    lane_half = lax.rem(head_at, 2)
    sibling = head_at + 1 - 2 * lane_half
    kv_head = lax.div(head_at, 2)

    barrier = pltpu.get_barrier_semaphore()
    for step in range(1, size):
        pl.semaphore_signal(
            barrier, inc=1, device_id={"context": lax.rem(me + step, size)}
        )
    pl.semaphore_signal(barrier, inc=1, device_id={"head": sibling})

    columns = pl.ds(pl.multiple_of(kv_head * HD, HD), HD)
    loads = [
        (state_hbm, states.at[me]),
        (atk_hbm.at[:, columns], raw_ref),
        (atv_hbm.at[pl.ds(0, part), columns], fresh.at[1, 0, 0]),
        (atv_hbm.at[pl.ds(part, part), columns], fresh.at[1, 0, 1]),
        (pk_hbm.at[0, :, columns], cached.at[0, me, 0]),
        (pk_hbm.at[1, :, columns], cached.at[0, me, 1]),
        (pv_hbm.at[0, :, columns], cached.at[1, me, 0]),
        (pv_hbm.at[1, :, columns], cached.at[1, me, 1]),
        (decay_hbm, decay_ref),
        (logit_hbm, logit_ref),
        (key_hbm, key_ref),
        (query_hbm, query_ref),
        (value_hbm, value_ref),
        (atq_hbm, atq_ref),
        (atg_hbm, atg_ref),
        (gate_hbm, gate_ref),
        (gain_hbm, gain_ref),
    ]
    loads = [
        pltpu.make_async_copy(source, target, load_sem.at[i])
        for i, (source, target) in enumerate(loads)
    ]
    for load in loads:
        load.start()

    groups = st_send.shape[2]
    group_heads = heads // groups

    def right_ok(s):
        return (me >= s) & (me < size - 1)

    def left_ok(s):
        return (me + s < size) & (me > 0)

    def st_copy(way, s, g, arriving):
        step = 1 if way == 0 else -1
        owner = lax.rem(me - step * (s + (1 if arriving else 0)) + 2 * size, size)
        ref = states.at[owner, :, pl.ds(g * group_heads, group_heads)]
        return pltpu.make_async_remote_copy(
            src_ref=ref, dst_ref=ref,
            send_sem=st_send.at[way, s, g], recv_sem=st_recv.at[way, s, g],
            device_id={"context": lax.rem(me + step + size, size)},
        )

    def state_start(s, g):
        for way, ok in ((0, right_ok), (1, left_ok)):

            @pl.when(ok(s)[0])
            def _(way=way):
                st_copy(way, s, g, False).start()

    def state_arrive(s, g):
        for way, ok in ((0, right_ok), (1, left_ok)):

            @pl.when(ok(s)[1])
            def _(way=way):
                st_copy(way, s, g, True).wait_recv()

    def ck_copy(step, arriving):
        owner = lax.rem(me - step + size, size) if arriving else me
        ref = cached.at[:, owner, lane_half]
        return pltpu.make_async_remote_copy(
            src_ref=ref, dst_ref=ref,
            send_sem=ck_send.at[step - 1], recv_sem=ck_recv.at[step - 1],
            device_id={"context": lax.rem(me + step, size)},
        )

    def nk_copy(step):
        return pltpu.make_async_remote_copy(
            src_ref=fresh.at[:, 0, lane_half], dst_ref=fresh.at[:, step, lane_half],
            send_sem=nk_send.at[step - 1], recv_sem=nk_recv.at[step - 1],
            device_id={"context": lax.rem(me + step, size)},
        )

    def sib_ck(step, arriving):
        owner = lax.rem(me - step + size, size)
        ref = cached.at[:, owner, 1 - lane_half if arriving else lane_half]
        return pltpu.make_async_remote_copy(
            src_ref=ref, dst_ref=ref,
            send_sem=sib_send.at[0, step - 1], recv_sem=sib_recv.at[0, step - 1],
            device_id={"head": sibling},
        )

    def sib_nk(step, arriving):
        ref = fresh.at[:, step, 1 - lane_half if arriving else lane_half]
        return pltpu.make_async_remote_copy(
            src_ref=ref, dst_ref=ref,
            send_sem=sib_send.at[1, step - 1], recv_sem=sib_recv.at[1, step - 1],
            device_id={"head": sibling},
        )

    def chain_copy(h):
        return pltpu.make_async_remote_copy(
            src_ref=leaving.at[h], dst_ref=held.at[h],
            send_sem=chain_send.at[h], recv_sem=chain_recv.at[h],
            device_id={"context": lax.rem(me + 1, size)},
        )

    def state_own(g):
        for way, ok in ((0, right_ok), (1, left_ok)):

            @pl.when(ok(0))
            def _(way=way):
                st_copy(way, 0, g, False).start()

    def state_forward(s, g):
        for way, ok in ((0, right_ok), (1, left_ok)):

            @pl.when(ok(s))
            def _(way=way):
                st_copy(way, s - 1, g, True).wait_recv()
                st_copy(way, s, g, False).start()

    def state_end(g):
        for way, end in ((0, size - 1), (1, 0)):

            @pl.when(me == end)
            def _(way=way):
                for s in range(size - 1):
                    st_copy(way, s, g, True).wait_recv()

    def kv_start(step):
        ck_copy(step, False).start()
        if step <= span:

            @pl.when(me + step < size)
            def _():
                nk_copy(step).start()

    def relayed(step):
        return (me + step == size - 1) & (step > 1)

    def ck_onward(owner):
        ref = cached.at[:, owner, lane_half]
        return pltpu.make_async_remote_copy(
            src_ref=ref, dst_ref=ref,
            send_sem=fw_send.at[0, owner], recv_sem=ck_recv.at[size - 2 - owner],
            device_id={"context": size - 1},
        )

    def nk_onward(owner):
        far = size - 1 - owner
        return pltpu.make_async_remote_copy(
            src_ref=fresh.at[:, far - 1, lane_half], dst_ref=fresh.at[:, far, lane_half],
            send_sem=fw_send.at[1, owner], recv_sem=nk_recv.at[far - 1],
            device_id={"context": size - 1},
        )

    def kv_onward(owner):
        @pl.when(me == size - 2)
        def _():
            near = size - 2 - owner
            ck_copy(near, True).wait_recv()
            ck_onward(owner).start()
            sib_ck(near, False).start()
            if near <= span:
                nk_copy(near).wait_recv()
                sib_nk(near, False).start()
            if near + 1 <= span:
                nk_onward(owner).start()

    def kv_side(rightward):
        for step in range(1, size):
            here = me + step < size if rightward else me + step >= size

            @pl.when(here & jnp.logical_not(relayed(step)))
            def _(step=step):
                kv_start(step)

    def kv_share():
        for step in range(1, size):

            @pl.when((me != size - 2) | (step > me))
            def _(step=step):
                ck_copy(step, True).wait_recv()
                sib_ck(step, False).start()
                if step <= span:

                    @pl.when(me >= step)
                    def _():
                        nk_copy(step).wait_recv()
                        sib_nk(step, False).start()

    def kv_arrive():
        for step in range(1, size):
            sib_ck(step, True).wait_recv()
            if step <= span:

                @pl.when(me >= step)
                def _(step=step):
                    sib_nk(step, True).wait_recv()

    loads[0].wait()
    pl.semaphore_wait(barrier, size)
    for g in range(groups):
        state_own(g)

    row_start = me * tokens
    last_row = row_start + tokens - 1
    requests = len_ref.shape[0]
    starts, total = [], jnp.int32(0)
    for r in range(requests):
        starts.append(total)
        total = total + len_ref[r]

    def layout(rows):
        seg = jnp.zeros_like(rows)
        for r in range(1, requests):
            seg = seg + (rows >= starts[r]).astype(jnp.int32)
        return seg

    rows = row_start + lax.broadcasted_iota(jnp.int32, (tokens, 1), 0)
    seg = layout(rows)
    first, prefix, offset = [jnp.zeros_like(rows)] * 3
    tail_first, tail_prefix, head_seg = jnp.int32(0), prefix_ref[0], jnp.int32(0)
    head_first = jnp.int32(0)
    for r in range(requests):
        first = jnp.where(seg == r, starts[r], first)
        prefix = jnp.where(seg == r, prefix_ref[r], prefix)
        offset = jnp.where(seg == r, offset_ref[r], offset)
        tail_first = jnp.where(starts[r] <= last_row, starts[r], tail_first)
        tail_prefix = jnp.where(starts[r] <= last_row, prefix_ref[r], tail_prefix)
        head_first = jnp.where(starts[r] <= row_start, starts[r], head_first)
        head_seg = jnp.where(starts[r] <= row_start, r, head_seg)
    restarts = tail_first >= row_start
    carried = (seg == head_seg) & (first < row_start)
    row_lane = lax.broadcasted_iota(jnp.int32, (1, tokens), 1)
    seg_row = layout(row_start + row_lane)
    cosines, sines = lane_tables(offset + rows - first)

    for load in loads[1:2]:
        load.wait()
    for j in range(2):
        piece = pl.ds(j * part, part)
        cut = slice(j * part, (j + 1) * part)
        fresh[0, 0, j, :, 0:128] = roped(
            raw_ref[piece, 0:128].astype(jnp.float32), cosines[cut], sines[cut]
        ).astype(jnp.bfloat16)
        fresh[0, 0, j, :, 128:HD] = raw_ref[piece, 128:HD]

    for load in loads[2:8]:
        load.wait()
    kv_side(True)

    for step in range(1, span + 1):

        @pl.when(me < step)
        def _(step=step):
            fresh[:, step] = jnp.zeros_like(fresh[:, step])

    @pl.when(me == 0)
    def _():
        held[...] = jnp.zeros_like(held)

    slots = size * 2
    lanes = lax.broadcasted_iota(jnp.int32, (1, slots * width), 1)
    slot, inside = lanes // width, lanes % width
    per_prefix = table_ref.shape[0] // prefixes
    code, place = jnp.zeros_like(lanes), jnp.zeros_like(lanes)
    for e in range(table_ref.shape[0]):
        here = slot == table_ref[e]
        code = jnp.where(here, e // per_prefix, code)
        place = jnp.where(here, e % per_prefix * width + inside, place)
    bias_ref[:, : slots * width] = jnp.where(
        (code == prefix) & (place < offset), 0.0, NEG_LARGE
    )
    for step in range(span + 1):
        key_row = row_start - step * tokens + row_lane
        seen = (layout(key_row) == seg) & (key_row <= rows) & (key_row >= 0)
        at = slots * width + step * tokens
        bias_ref[:, at : at + tokens] = jnp.where(seen, 0.0, NEG_LARGE)

    row = lax.broadcasted_iota(jnp.int32, (tokens, tokens), 0)
    col = lax.broadcasted_iota(jnp.int32, (tokens, tokens), 1)
    same = seg == seg_row
    causal = same & (row >= col)
    strict = same & (row > col)
    eye = row == col
    causal_f = causal.astype(jnp.float32)
    for load in loads[8:13]:
        load.wait()
    run_row = lax.dot_general(
        decay_ref[...], causal_f, (((1,), (1,)), ((), ())),
        precision=HIGH, preferred_element_type=jnp.float32,
    )
    beta_row = jax.nn.sigmoid(logit_ref[...])
    tail = seg_row == seg_row[:, tokens - 1 : tokens]
    end_row = jnp.where(
        tail, jnp.exp(jnp.where(tail, run_row[:, tokens - 1 : tokens] - run_row, 0.0)), 0.0
    )
    turned = jnp.concatenate(
        [run_row, beta_row, end_row, jnp.zeros((128 - 3 * heads, tokens), jnp.float32)], axis=0
    ).T
    run, beta = turned[:, :heads], turned[:, heads : 2 * heads]
    end = turned[:, 2 * heads : 3 * heads]
    start, start_row = jnp.exp(run), jnp.exp(run_row)
    keys, turned_keys, grams, mixes, scaled, inv_rows, inv_cols = [], [], [], [], [], [], []
    for g in range(heads // share):
        k = key_ref[:, g * DK : (g + 1) * DK]
        q = query_ref[:, g * DK : (g + 1) * DK]
        gram = dot1(k, k, ((1,), (1,)))
        cross = dot1(q, k, ((1,), (1,)))
        squares = jnp.where(eye, gram, 0.0)
        inv = lax.rsqrt(jnp.sum(squares, axis=1, keepdims=True) + 1e-06)
        inv_row = lax.rsqrt(jnp.sum(squares, axis=0, keepdims=True) + 1e-06)
        q_f = q.astype(jnp.float32)
        inv_q = lax.rsqrt(jnp.sum(q_f * q_f, axis=1, keepdims=True) + 1e-06) * DK ** (-0.5)
        keys.append(k)
        turned_keys.append(k.T)
        inv_rows.append(inv_row)
        inv_cols.append(inv)
        grams.append(gram * inv * inv_row)
        mixes.append(cross * inv_q * inv_row)
        scaled.append(q_f * inv_q)
    lowers, inverses, mixing = [], [], []
    for h in range(heads):
        gaps = run[:, h : h + 1] - run_row[h : h + 1, :]
        decay_mat = jnp.where(causal, jnp.exp(jnp.where(causal, gaps, 0.0)), 0.0)
        mixing.append(decay_mat * mixes[h // share])
        lower = jnp.where(strict, beta[:, h : h + 1] * grams[h // share] * decay_mat, 0.0)
        lowers.append(lower)
        inverses.append(
            jnp.where(eye, 1.0, 0.0) - jnp.where((row >> 1) == (col >> 1), lower, 0.0)
        )
    plan = {5: 0, 7: 1, 9: 2, 11: 3}
    ticks = [0]

    def tick():
        if ticks[0] in plan and size > 2:
            state_forward(1, plan[ticks[0]])
        ticks[0] += 1

    splits = [halves(lowers[h]) for h in range(heads)]
    parts = [halves(inverses[h]) for h in range(heads)]
    depth, level = 2, 1
    while depth < tokens:
        pair = ((row >> (level + 1)) == (col >> (level + 1))) & ((row >> level) > (col >> level))
        if depth < 16:
            picks = [(0, tokens)]
        else:
            picks = [(at, depth) for at in range(depth, tokens, 2 * depth)]

        def rows_of(x):
            cuts = [x[at : at + count] for at, count in picks]
            return cuts[0] if len(cuts) == 1 else jnp.concatenate(cuts, axis=0)

        def spread(x):
            if depth < 16:
                return x
            out = []
            for i in range(len(picks)):
                out.append(jnp.zeros((depth, tokens), x.dtype))
                out.append(x[i * depth : (i + 1) * depth])
            return jnp.concatenate(out, axis=0)

        mask = rows_of(pair.astype(jnp.float32)).astype(jnp.bfloat16)
        half = []
        for h in range(heads):
            left = [rows_of(s) * mask for s in splits[h]]
            half.append(product3(left, parts[h]))
        tick()
        for h in range(heads):
            left = [rows_of(p) for p in parts[h]]
            right = tuple(spread(p) for p in halves(half[h]))
            fixed = rows_of(inverses[h]) - product3(left, right)
            if depth < 16:
                inverses[h], parts[h] = fixed, halves(fixed)
            else:
                high, low = halves(fixed)
                whole_f, whole_high, whole_low = [], [], []
                for i, (at, count) in enumerate(picks):
                    cut = slice(i * count, (i + 1) * count)
                    for out, old, now in (
                        (whole_f, inverses[h], fixed),
                        (whole_high, parts[h][0], high),
                        (whole_low, parts[h][1], low),
                    ):
                        out.append(old[at - count : at])
                        out.append(now[cut])
                inverses[h] = jnp.concatenate(whole_f, axis=0)
                parts[h] = (
                    jnp.concatenate(whole_high, axis=0), jnp.concatenate(whole_low, axis=0)
                )
        tick()
        depth, level = depth * 2, level + 1
    weighted = [inverses[h] * beta_row[h : h + 1, :] for h in range(heads)]
    update = [product2(weighted[h], value_ref[:, h * DV : (h + 1) * DV]) for h in range(heads)]
    wy = [
        product2(weighted[h] * (start_row[h : h + 1, :] * inv_rows[h // share]), keys[h // share])
        for h in range(heads)
    ]
    tick()
    solved = [jnp.concatenate([update[h], wy[h]], axis=1) for h in range(heads)]
    carries = []
    for h in range(heads):
        high, low = halves(solved[h] * (end[:, h : h + 1] * inv_cols[h // share]))
        twice = jnp.concatenate([turned_keys[h // share]] * 2, axis=1)
        carries.append(dot1(twice, jnp.concatenate([high, low], axis=0)))
    tick()
    mixed = []
    for h in range(heads):
        mixed.append(product3(halves(mixing[h]), halves(solved[h])))
    tick()
    for h in range(heads):
        add_ref[h] = carries[h][:, :DV]
        map_ref[h] = (
            jnp.where(eye, start[tokens - 1 : tokens, h : h + 1], 0.0) - carries[h][:, DV:]
        ).astype(jnp.bfloat16)
        local_ref[h] = mixed[h][:, :DV]
        reach_ref[h] = (start[:, h : h + 1] * scaled[h // share] - mixed[h][:, DV:]).astype(
            jnp.bfloat16
        )
    for load in loads[13:]:
        load.wait()

    query_heads = atq_ref.shape[1] // HD
    for h in range(query_heads):
        cut = slice(h * HD, h * HD + 128)
        front = roped(atq_ref[:, cut].astype(jnp.float32), cosines, sines)
        front = front.astype(jnp.bfloat16).astype(jnp.float32)
        rear = atq_ref[:, h * HD + 128 : (h + 1) * HD].astype(jnp.float32)
        atq_ref[:, h * HD : (h + 1) * HD] = (
            jnp.concatenate([front, rear], axis=1) * HD ** (-0.5)
        ).astype(jnp.bfloat16)

    def attend():
        kv_arrive()
        old_keys = cached[0].reshape(-1, HD)
        old_values = cached[1].reshape(-1, HD)
        new_keys = fresh[0].reshape(-1, HD)
        new_values = fresh[1].reshape(-1, HD)
        old_bias, new_bias = bias_ref[:, : slots * width], bias_ref[:, slots * width :]
        for pair in range(0, query_heads, 4):
            these = range(pair, min(pair + 4, query_heads))
            queries = [atq_ref[:, h * HD : (h + 1) * HD] for h in these]
            old = [dot1(query, old_keys, ((1,), (1,))) + old_bias for query in queries]
            new = [dot1(query, new_keys, ((1,), (1,))) + new_bias for query in queries]
            peaks = [
                jnp.maximum(jnp.max(o, axis=1, keepdims=True), jnp.max(n, axis=1, keepdims=True))
                for o, n in zip(old, new)
            ]
            old = [jnp.exp(o - peak) for o, peak in zip(old, peaks)]
            new = [jnp.exp(n - peak) for n, peak in zip(new, peaks)]
            wholes = [
                jnp.sum(o, axis=1, keepdims=True) + jnp.sum(n, axis=1, keepdims=True)
                for o, n in zip(old, new)
            ]
            summed = [
                dot1(o.astype(jnp.bfloat16), old_values) + dot1(n.astype(jnp.bfloat16), new_values)
                for o, n in zip(old, new)
            ]
            for i, h in enumerate(these):
                gate = atg_ref[:, h * HD : (h + 1) * HD].astype(jnp.float32)
                at_out_ref[:, h * HD : (h + 1) * HD] = (
                    summed[i] / wholes[i] * jax.nn.sigmoid(gate)
                ).astype(jnp.bfloat16)

    def state_of(p, h):
        return jnp.concatenate([states[o, p, h] for o in range(size)], axis=0)

    def from_prefixes(these):
        own = [(prefix == p) & ~carried for p in range(prefixes)]
        for h in these:
            whole_states = [state_of(p, h) for p in range(prefixes)]
            base = whole_states[0]
            for p in range(1, prefixes):
                base = jnp.where(tail_prefix == p, whole_states[p], base)
            opened = dot1(map_ref[h], base, ((1,), (1,)))
            parts = dot1(reach_ref[h], jnp.concatenate(whole_states, axis=0), ((1,), (1,)))
            core = local_ref[h]
            for p in range(prefixes):
                core = core + jnp.where(own[p], parts[:, p * DV : (p + 1) * DV], 0.0)
            local_ref[h] = core
            add_ref[h] = add_ref[h] + jnp.where(restarts, opened, 0.0)

    for owner in range(size - 3, -1, -1):
        kv_onward(owner)
    for g in range(groups):
        for s in range(2, size - 1):
            state_forward(s, g)
    kv_side(False)
    @pl.when(me == size - 1)
    def _():
        kv_share()
        attend()

    for g in range(groups):
        these = range(g * group_heads, (g + 1) * group_heads)
        state_end(g)
        from_prefixes(these)

        @pl.when(me == 0)
        def _(these=these):
            for h in these:
                leaving[h] = add_ref[h].astype(jnp.bfloat16)
                chain_copy(h).start()


    for h in range(heads):

        @pl.when(me > 0)
        def _(h=h):
            chain_copy(h).wait_recv()

        @pl.when((me > 0) & (me < size - 1))
        def _(h=h):
            onward = dot1(map_ref[h], held[h])
            leaving[h] = (add_ref[h] + jnp.where(restarts, 0.0, onward)).astype(jnp.bfloat16)
            chain_copy(h).start()

        core = local_ref[h] + jnp.where(carried, dot1(reach_ref[h], held[h]), 0.0)
        normed = core * lax.rsqrt(jnp.mean(core * core, axis=1, keepdims=True) + 1e-06)
        gate = gate_ref[:, h * DV : (h + 1) * DV].astype(jnp.float32)
        dn_out_ref[:, h * DV : (h + 1) * DV] = (
            normed * gain_ref[...] * (gate * jax.nn.sigmoid(gate))
        ).astype(jnp.bfloat16)
        if h == heads - 2:

            @pl.when(me < size - 1)
            def _():
                kv_share()

    @pl.when(me < size - 1)
    def _():
        attend()

    for s in range(size - 1):
        for g in range(groups):
            for way, ok in ((0, right_ok), (1, left_ok)):

                @pl.when(ok(s))
                def _(way=way, s=s, g=g):
                    st_copy(way, s, g, False).wait_send()

    for step in range(1, size):
        sib_ck(step, False).wait_send()

        @pl.when(jnp.logical_not(relayed(step)))
        def _(step=step):
            ck_copy(step, False).wait_send()
            if step <= span:

                @pl.when(me + step < size)
                def _():
                    nk_copy(step).wait_send()

        if step <= span:

            @pl.when(me >= step)
            def _(step=step):
                sib_nk(step, False).wait_send()

    @pl.when(me == size - 2)
    def _():
        for owner in range(size - 2):
            ck_onward(owner).wait_send()
            if size - 1 - owner <= span:
                nk_onward(owner).wait_send()

    @pl.when(me < size - 1)
    def _():
        for h in range(heads):
            chain_copy(h).wait_send()


def hand_out_kernel(dn_ref, at_ref, dn_out_ref, at_out_ref, held, load_sem, store_sem):
    rows = dn_ref.shape[0] // 2
    loads, stores = [], []
    for i in range(2):
        cut = pl.ds(i * rows, rows)
        for j, (source, target) in enumerate(((dn_ref, dn_out_ref), (at_ref, at_out_ref))):
            loads.append(pltpu.make_async_copy(source.at[cut], held.at[j, cut], load_sem.at[i, j]))
            stores.append(pltpu.make_async_copy(held.at[j, cut], target.at[cut], store_sem.at[i, j]))
    for load in loads:
        load.start()
    for load, store in zip(loads, stores):
        load.wait()
        store.start()
    for store in stores:
        store.wait()


def hand_out(dn_out, at_out):
    far = pl.BlockSpec(memory_space=pl.ANY)
    return pl.pallas_call(
        hand_out_kernel,
        out_shape=[
            jax.ShapeDtypeStruct(dn_out.shape, dn_out.dtype),
            jax.ShapeDtypeStruct(at_out.shape, at_out.dtype),
        ],
        in_specs=[far, far],
        out_specs=[far, far],
        scratch_shapes=[
            pltpu.VMEM((2,) + dn_out.shape, dn_out.dtype),
            pltpu.SemaphoreType.DMA((2, 2)),
            pltpu.SemaphoreType.DMA((2, 2)),
        ],
        compiler_params=pltpu.CompilerParams(vmem_limit_bytes=60 * 2**20),
    )(dn_out, at_out)


def fits_fused(tokens, query_heads, prefix_state, prefix_key):
    size = lax.axis_size("context")
    return (
        tokens == 128
        and size <= 4
        and prefix_state.shape[2] % 16 == 0
        and prefix_key.shape[0] == 2
        and prefix_key.shape[1] % 16 == 0
        and HQ // KVH == 2 * query_heads
    )


def fused(
    dn_query, dn_key, dn_value, dn_gate, dn_beta_logit, dn_decay, dn_norm_gain,
    prefix_state, at_query, at_gate, at_key, at_value, prefix_key, prefix_value,
    req_len, req_prefix, req_offset, block_table,
):
    size = lax.axis_size("context")
    tokens = dn_query.shape[0]
    heads = dn_value.shape[1] // DV
    prefixes, _, state_rows, _ = prefix_state.shape
    width = prefix_key.shape[1]
    longest = size * tokens // 2
    span = min(size - 1, (longest - 1 + tokens - 1) // tokens)
    groups = 4
    bf16, f32 = jnp.bfloat16, jnp.float32
    far = pl.BlockSpec(memory_space=pl.ANY)
    near = pl.BlockSpec(memory_space=pltpu.VMEM)
    small = pl.BlockSpec(memory_space=pltpu.SMEM)
    keys_seen = size * 2 * width + (span + 1) * tokens
    dma = pltpu.SemaphoreType.DMA
    dn_out, at_out = pl.pallas_call(
        lambda *refs: fused_kernel(size, span, *refs),
        out_shape=[
            jax.ShapeDtypeStruct(dn_gate.shape, bf16),
            jax.ShapeDtypeStruct(at_query.shape, bf16),
        ],
        in_specs=[far] * 14 + [small] * 4,
        out_specs=[near, near],
        scratch_shapes=[
            pltpu.VMEM(dn_query.shape, bf16),
            pltpu.VMEM(dn_key.shape, bf16),
            pltpu.VMEM(dn_value.shape, bf16),
            pltpu.VMEM(dn_gate.shape, bf16),
            pltpu.VMEM((heads, tokens), f32),
            pltpu.VMEM((heads, tokens), f32),
            pltpu.VMEM((1, DV), f32),
            pltpu.VMEM(at_query.shape, bf16),
            pltpu.VMEM(at_gate.shape, bf16),
            pltpu.VMEM((tokens, HD), bf16),
            pltpu.VMEM((size, prefixes, heads, state_rows, DK), bf16),
            pltpu.VMEM((2, size, 2, width, HD), bf16),
            pltpu.VMEM((2, span + 1, 2, tokens // 2, HD), bf16),
            pltpu.VMEM((heads, tokens, DV), f32),
            pltpu.VMEM((heads, tokens, DK), bf16),
            pltpu.VMEM((heads, DK, DK), bf16),
            pltpu.VMEM((heads, DV, DK), f32),
            pltpu.VMEM((heads, DV, DK), bf16),
            pltpu.VMEM((heads, DV, DK), bf16),
            pltpu.VMEM((tokens, keys_seen), f32),
            dma((17,)),
            dma((2, size - 1, groups)),
            dma((2, size - 1, groups)),
            dma((size - 1,)),
            dma((size - 1,)),
            dma((span,)),
            dma((span,)),
            dma((2, size - 1)),
            dma((2, size - 1)),
            dma((heads,)),
            dma((heads,)),
            dma((2, size)),
        ],
        compiler_params=pltpu.CompilerParams(
            collective_id=2, has_side_effects=True, vmem_limit_bytes=60 * 2**20
        ),
    )(
        dn_query, dn_key, dn_value, dn_gate, dn_beta_logit.T, dn_decay.T, dn_norm_gain[None, :],
        prefix_state, at_query, at_gate, at_key, at_value, prefix_key, prefix_value,
        req_len, req_prefix, req_offset, block_table,
    )
    return hand_out(dn_out, at_out)


def shards(
    dn_query,
    dn_key,
    dn_value,
    dn_gate,
    dn_beta_logit,
    dn_decay,
    dn_norm_gain,
    prefix_state,
    at_query,
    at_gate,
    at_key,
    at_value,
    prefix_key,
    prefix_value,
    req_len,
    req_prefix,
    req_offset,
    block_table,
):
    tokens_here = dn_query.shape[0]
    value_heads = dn_value.shape[1] // DV
    query_heads = at_query.shape[1] // HD
    if fits_fused(tokens_here, query_heads, prefix_state, prefix_key):
        return fused(
            dn_query, dn_key, dn_value, dn_gate, dn_beta_logit, dn_decay, dn_norm_gain,
            prefix_state, at_query, at_gate, at_key, at_value, prefix_key, prefix_value,
            req_len, req_prefix, req_offset, block_table,
        )
    device = lax.axis_index("context")
    row_start = device * tokens_here
    rows = row_start + jnp.arange(tokens_here, dtype=jnp.int32)
    segment, first, prefix, offset, position = row_layout(rows, req_len, req_prefix, req_offset)
    size = lax.axis_size("context")
    query_heads_here = query_heads
    kv_head = lax.axis_index("head") * query_heads_here // (HQ // KVH)
    cosines, sines = yarn_tables(position, ROT)
    new_key = lax.dynamic_slice_in_dim(at_key, kv_head * HD, HD, 1).reshape(tokens_here, 1, HD)
    new_key = (
        rotate(new_key.astype(jnp.float32), cosines, sines, ROT)
        .reshape(tokens_here, HD)
        .astype(jnp.bfloat16)
    )
    new_value = lax.dynamic_slice_in_dim(at_value, kv_head * HD, HD, 1)
    cached_key = lax.dynamic_slice_in_dim(prefix_key, kv_head * HD, HD, 2)
    cached_value = lax.dynamic_slice_in_dim(prefix_value, kv_head * HD, HD, 2)
    states = jnp.stack([prefix_state] + from_others(prefix_state, "context", size, size))
    states = jnp.concatenate([states[::-1]] * 2)
    states = lax.dynamic_slice_in_dim(states, size - 1 - device, size, 0)
    states = jnp.moveaxis(states, 0, 2)
    states = states.reshape(states.shape[:2] + (-1, DK))
    slots_here = cached_key.shape[0]
    own_block = jnp.concatenate(
        [cached_key.reshape(-1, HD), new_key, cached_value.reshape(-1, HD), new_value]
    ).reshape(2, -1, HD)
    block_rows = own_block.shape[1]
    sharers = HQ // KVH // query_heads
    share = block_rows // sharers
    share_index = lax.axis_index("head") % sharers
    mine = lax.dynamic_slice_in_dim(own_block, share_index * share, share, 1)
    received = jnp.stack(from_others(mine, "context", size, size))
    siblings = from_others(received, "head", lax.axis_size("head"), sharers)
    cached_rows = cached_key.shape[0] * cached_key.shape[1]
    square = (value_heads, DK, DK)
    local_out, reach, map_half, carry_add = whole_call(
        local_kernel,
        [
            jax.ShapeDtypeStruct((value_heads, tokens_here, DV), jnp.float32),
            jax.ShapeDtypeStruct((value_heads, tokens_here, DK), jnp.bfloat16),
            jax.ShapeDtypeStruct(square, jnp.bfloat16),
            jax.ShapeDtypeStruct(square, jnp.float32),
        ],
        dn_query,
        dn_key,
        dn_value,
        dn_beta_logit,
        dn_beta_logit.T,
        dn_decay,
        dn_decay.T,
        segment[:, None],
        segment[None, :],
    )
    restarts = first[tokens_here - 1] >= row_start
    tail_prefix = prefix[tokens_here - 1]
    base = jnp.zeros(states.shape[1:], states.dtype)
    for owner in range(states.shape[0]):
        base = jnp.where(tail_prefix == owner, states[owner], base)
    fresh = jnp.einsum("hvj,hjk->hvk", base, map_half, preferred_element_type=jnp.float32)
    into_state = chain(
        jnp.where(restarts, 0, map_half).astype(jnp.bfloat16),
        carry_add + jnp.where(restarts, fresh, 0.0),
        size,
    )
    carried = (segment == segment[0]) & (first[0] < row_start)
    owner_ids = jnp.arange(states.shape[0], dtype=jnp.int32)
    select = (prefix[None, :] == owner_ids[:, None]) & ~carried[None, :]
    select = jnp.concatenate([select, carried[None, :]], axis=0)
    dn_out = whole_call(
        finish_kernel,
        jax.ShapeDtypeStruct((tokens_here, value_heads * DV), jnp.bfloat16),
        local_out,
        reach,
        states,
        into_state,
        select.astype(jnp.float32).T,
        dn_gate,
        dn_norm_gain[None, :],
    )
    blocks_per_prefix = block_table.shape[0] // prefix_state.shape[0]
    width = cached_key.shape[1]
    others = (device - 1 - jnp.arange(size - 1, dtype=jnp.int32)) % size
    origins = [jnp.full((block_rows,), device, jnp.int32)]
    parts = [jnp.arange(block_rows, dtype=jnp.int32)]
    for step in range(sharers):
        origins.append(jnp.repeat(others, share))
        parts.append(
            (share_index - step) % sharers * share
            + jnp.tile(jnp.arange(share, dtype=jnp.int32), size - 1)
        )
    origin, part = jnp.concatenate(origins), jnp.concatenate(parts)
    slot = origin * slots_here + part // width
    entry = jnp.sum(
        jnp.where(
            block_table[:, None] == slot[None, :],
            jnp.arange(block_table.shape[0], dtype=jnp.int32)[:, None],
            0,
        ),
        axis=0,
    )
    key_row = origin * tokens_here + part - cached_rows
    starts = request_starts(req_len)
    key_segment = jnp.sum((starts[:, None] <= key_row[None, :]).astype(jnp.int32), axis=0) - 1
    old = part < cached_rows
    prefixes = prefix_state.shape[0]
    code = jnp.where(old, entry // blocks_per_prefix, prefixes + key_segment)
    place = jnp.where(old, entry % blocks_per_prefix * width + part % width, key_row)
    ones = jnp.ones((tokens_here, 128 - ROT), jnp.float32)
    at_out = whole_call(
        attend_kernel,
        jax.ShapeDtypeStruct((tokens_here, query_heads * HD), jnp.bfloat16),
        at_query,
        jnp.concatenate([cosines, cosines, ones], axis=1),
        jnp.concatenate([-sines, sines, 0.0 * ones], axis=1),
        at_gate,
        jnp.stack([prefix, offset, prefixes + segment, rows], axis=1),
        code[None, :],
        place[None, :],
        own_block,
        received,
        *siblings,
    )
    return (dn_out, at_out)


def solution(mesh):
    placed = (
        P(("group", "context"), "head"),
        P(("group", "context"), "head"),
        P(("group", "context"), "head"),
        P(("group", "context"), "head"),
        P(("group", "context"), "head"),
        P(("group", "context"), "head"),
        P(),
        P("group", "head", "context", None),
        P(("group", "context"), "head"),
        P(("group", "context"), "head"),
        P(("group", "context"), None),
        P(("group", "context"), None),
        P(("group", "context"), None, None),
        P(("group", "context"), None, None),
        P("group"),
        P("group"),
        P("group"),
        P("group"),
    )
    return jax.shard_map(
        shards,
        mesh=mesh,
        in_specs=placed,
        out_specs=(P(("group", "context"), "head"), P(("group", "context"), "head")),
        check_vma=False,
    )
```

```python
import math

import jax
import jax.numpy as jnp
from jax import lax
from jax.experimental import pallas as pl
from jax.experimental.pallas import tpu as pltpu
from jax.sharding import PartitionSpec as P

VH = 32
KH = 16
DK = 128
DV = 128
HQ = 16
KVH = 2
HD = 256
ROT = 64


ROPE_THETA = 10000000.0
YARN_FACTOR = 4.0
YARN_ANCHOR = 262144.0
NEG_LARGE = -1e30
HIGH = lax.Precision.HIGHEST


def chain_kernel(size, map_ref, add_ref, into_ref, held, leaving, send_sem, recv_sem):
    me = lax.axis_index("context")
    heads = map_ref.shape[0]
    barrier = pltpu.get_barrier_semaphore()
    after, before = lax.rem(me + 1, size), lax.rem(me + size - 1, size)
    for neighbour in (before, after):
        pl.semaphore_signal(barrier, inc=1, device_id={"context": neighbour})
    pl.semaphore_wait(barrier, 2)

    def sent(h):
        return pltpu.make_async_remote_copy(
            src_ref=leaving.at[h],
            dst_ref=held.at[h],
            send_sem=send_sem.at[h],
            recv_sem=recv_sem.at[h],
            device_id={"context": after},
        )

    @pl.when(me == 0)
    def _():
        held[...] = jnp.zeros_like(held)

    for h in range(heads):

        @pl.when(me > 0)
        def _(h=h):
            sent(h).wait_recv()

        leaving[h] = (
            jnp.dot(held[h], map_ref[h], preferred_element_type=jnp.float32) + add_ref[h]
        ).astype(jnp.bfloat16)

        @pl.when(me < size - 1)
        def _(h=h):
            sent(h).start()

    into_ref[...] = held[...]

    @pl.when(me < size - 1)
    def _():
        for h in range(heads):
            sent(h).wait_send()


def chain(carry_map, carry_add, size):
    heads = carry_map.shape[0]
    return pl.pallas_call(
        lambda *refs: chain_kernel(size, *refs),
        out_shape=jax.ShapeDtypeStruct(carry_add.shape, jnp.bfloat16),
        in_specs=[pl.BlockSpec(memory_space=pltpu.VMEM)] * 2,
        out_specs=pl.BlockSpec(memory_space=pltpu.VMEM),
        scratch_shapes=[
            pltpu.VMEM(carry_add.shape, jnp.bfloat16),
            pltpu.VMEM(carry_add.shape, jnp.bfloat16),
            pltpu.SemaphoreType.DMA((heads,)),
            pltpu.SemaphoreType.DMA((heads,)),
        ],
        compiler_params=pltpu.CompilerParams(collective_id=1, has_side_effects=True),
    )(carry_map, carry_add)


def from_others(x, axis, size, span):
    return [
        lax.ppermute(
            x, axis, [(i, i // span * span + (i + step) % span) for i in range(size)]
        )
        for step in range(1, span)
    ]


def halves(x):
    high = x.astype(jnp.bfloat16)
    return high, (x - high.astype(jnp.float32)).astype(jnp.bfloat16)


def dot1(a, b, contract=((1,), (0,))):
    return lax.dot_general(a, b, (contract, ((), ())), preferred_element_type=jnp.float32)


def dot2(a, exact):
    high, low = halves(a)
    return dot1(high, exact) + dot1(low, exact)


def dot3(a, b):
    a_high, a_low = halves(a)
    b_high, b_low = halves(b)
    return dot1(a_high, b_high) + (dot1(a_high, b_low) + dot1(a_low, b_high))


def local_kernel(
    query_ref, key_ref, value_ref, logit_ref, logit_row_ref, decay_ref, decay_row_ref,
    seg_ref, seg_row_ref, local_ref, reach_ref, map_ref, add_ref,
):
    tokens = query_ref.shape[0]
    heads = local_ref.shape[0]
    share = VH // KH
    seg, seg_row = seg_ref[...], seg_row_ref[...]
    row = lax.broadcasted_iota(jnp.int32, (tokens, tokens), 0)
    col = lax.broadcasted_iota(jnp.int32, (tokens, tokens), 1)
    same = seg == seg_row
    causal = same & (row >= col)
    strict = same & (row > col)
    eye = row == col
    causal_f = causal.astype(jnp.float32)
    run = lax.dot_general(
        causal_f, decay_ref[...], (((1,), (0,)), ((), ())),
        precision=HIGH, preferred_element_type=jnp.float32,
    )
    run_row = lax.dot_general(
        decay_row_ref[...], causal_f, (((1,), (1,)), ((), ())),
        precision=HIGH, preferred_element_type=jnp.float32,
    )
    beta, beta_row = jax.nn.sigmoid(logit_ref[...]), jax.nn.sigmoid(logit_row_ref[...])
    start, start_row = jnp.exp(run), jnp.exp(run_row)
    tail = seg_row == seg_row[:, tokens - 1 : tokens]
    end_row = jnp.where(
        tail, jnp.exp(jnp.where(tail, run_row[:, tokens - 1 : tokens] - run_row, 0.0)), 0.0
    )
    keys, grams, mixes, scaled, inv_rows = [], [], [], [], []
    for g in range(heads // share):
        k = key_ref[:, g * DK : (g + 1) * DK]
        q = query_ref[:, g * DK : (g + 1) * DK]
        gram = dot1(k, k, ((1,), (1,)))
        cross = dot1(q, k, ((1,), (1,)))
        squares = jnp.where(eye, gram, 0.0)
        inv = lax.rsqrt(jnp.sum(squares, axis=1, keepdims=True) + 1e-06)
        inv_row = lax.rsqrt(jnp.sum(squares, axis=0, keepdims=True) + 1e-06)
        q_f = q.astype(jnp.float32)
        inv_q = lax.rsqrt(jnp.sum(q_f * q_f, axis=1, keepdims=True) + 1e-06) * DK ** (-0.5)
        keys.append(k)
        inv_rows.append(inv_row)
        grams.append(gram * inv * inv_row)
        mixes.append(cross * inv_q * inv_row)
        scaled.append(q_f * inv_q)
    lowers, inverses, mixing = [], [], []
    for h in range(heads):
        gaps = run[:, h : h + 1] - run_row[h : h + 1, :]
        decay_mat = jnp.where(causal, jnp.exp(jnp.where(causal, gaps, 0.0)), 0.0)
        mixing.append(decay_mat * mixes[h // share])
        lower = jnp.where(strict, beta[:, h : h + 1] * grams[h // share] * decay_mat, 0.0)
        lowers.append(lower)
        inverses.append(
            jnp.where(eye, 1.0, 0.0) - jnp.where(row // 2 == col // 2, lower, 0.0)
        )
    width = 2
    while width < tokens:
        pair = (row // (2 * width) == col // (2 * width)) & (row // width > col // width)
        half = [dot3(jnp.where(pair, lowers[h], 0.0), inverses[h]) for h in range(heads)]
        inverses = [inverses[h] - dot3(inverses[h], half[h]) for h in range(heads)]
        width *= 2
    for h in range(heads):
        g = h // share
        weighted = inverses[h] * beta_row[h : h + 1, :]
        update = dot2(weighted, value_ref[:, h * DV : (h + 1) * DV])
        wy = dot2(weighted * (start_row[h : h + 1, :] * inv_rows[g]), keys[g])
        solved = jnp.concatenate([update, wy], axis=1)
        mixed = dot3(mixing[h], solved)
        local_ref[h] = mixed[:, :DV]
        reach_ref[h] = (start[:, h : h + 1] * scaled[g] - mixed[:, DV:]).astype(jnp.bfloat16)
        turned = solved.T * (end_row[h : h + 1, :] * inv_rows[g])
        carry = dot2(turned, keys[g])
        add_ref[h] = carry[:DV]
        map_ref[h] = (
            jnp.where(eye, start[tokens - 1 : tokens, h : h + 1], 0.0) - carry[DV:]
        ).astype(jnp.bfloat16)


def finish_kernel(local_ref, reach_ref, states_ref, into_ref, select_ref, gate_ref, gain_ref, out_ref):
    owners = states_ref.shape[0]
    select = select_ref[...] > 0.5
    for h in range(local_ref.shape[0]):
        core = local_ref[h]
        reach = reach_ref[h]
        for owner in range(owners + 1):
            state = states_ref[owner, h] if owner < owners else into_ref[h]
            part = dot1(reach, state, ((1,), (1,)))
            core = core + jnp.where(select[:, owner : owner + 1], part, 0.0)
        normed = core * lax.rsqrt(jnp.mean(core * core, axis=1, keepdims=True) + 1e-06)
        gate = gate_ref[:, h * DV : (h + 1) * DV].astype(jnp.float32)
        out_ref[:, h * DV : (h + 1) * DV] = (
            normed * gain_ref[...] * (gate * jax.nn.sigmoid(gate))
        ).astype(jnp.bfloat16)


def attend_kernel(
    query_ref, cos_ref, sin_ref, gate_ref, row_ref, code_ref, place_ref, own_ref, *rest
):
    pieces, out_ref = [own_ref] + list(rest[:-1]), rest[-1]
    tokens = query_ref.shape[0]
    cosines, sines = cos_ref[...], sin_ref[...]
    lane = lax.broadcasted_iota(jnp.int32, (tokens, 128), 1)
    old_code, limit = row_ref[:, 0:1], row_ref[:, 1:2]
    new_code, own_row = row_ref[:, 2:3], row_ref[:, 3:4]
    keys, values, seen, at = [], [], [], 0
    for ref in pieces:
        if len(ref.shape) == 3:
            keys.append(ref[0])
            values.append(ref[1])
        else:
            keys.append(ref[:, 0].reshape(-1, HD))
            values.append(ref[:, 1].reshape(-1, HD))
        count = keys[-1].shape[0]
        code, place = code_ref[:, at : at + count], place_ref[:, at : at + count]
        at += count
        seen.append(
            ((code == old_code) & (place < limit)) | ((code == new_code) & (place <= own_row))
        )
    for h in range(query_ref.shape[1] // HD):
        front = query_ref[:, h * HD : h * HD + 128].astype(jnp.float32)
        swapped = jnp.where(
            lane < ROT // 2, pltpu.roll(front, 128 - ROT // 2, 1), pltpu.roll(front, ROT // 2, 1)
        )
        query = jnp.concatenate(
            [
                (front * cosines + swapped * sines).astype(jnp.bfloat16),
                query_ref[:, h * HD + 128 : (h + 1) * HD],
            ],
            axis=1,
        )
        scores = [
            jnp.where(see, dot1(query, key, ((1,), (1,))) * HD ** (-0.5), NEG_LARGE)
            for see, key in zip(seen, keys)
        ]
        peak = jnp.max(scores[0], axis=1, keepdims=True)
        for score in scores[1:]:
            peak = jnp.maximum(peak, jnp.max(score, axis=1, keepdims=True))
        total, summed = 0.0, 0.0
        for score, see, value in zip(scores, seen, values):
            weight = jnp.where(see, jnp.exp(score - peak), 0.0)
            total = total + jnp.sum(weight, axis=1, keepdims=True)
            summed = summed + dot1(weight.astype(jnp.bfloat16), value)
        gate = gate_ref[:, h * HD : (h + 1) * HD].astype(jnp.float32)
        out_ref[:, h * HD : (h + 1) * HD] = (
            summed / total * jax.nn.sigmoid(gate)
        ).astype(jnp.bfloat16)


def whole_call(kernel, shapes, *arrays):
    space = pl.BlockSpec(memory_space=pltpu.VMEM)
    return pl.pallas_call(
        kernel,
        out_shape=shapes,
        in_specs=[space] * len(arrays),
        out_specs=jax.tree.map(lambda _: space, shapes),
        compiler_params=pltpu.CompilerParams(vmem_limit_bytes=48 * 2**20),
    )(*arrays)


def yarn_tables(positions, rotary):
    half = rotary // 2
    log_theta = math.log(ROPE_THETA)
    lower = max(
        math.floor(rotary * math.log(YARN_ANCHOR / (64.0 * math.pi)) / (2.0 * log_theta)), 0
    )
    upper = min(
        math.ceil(rotary * math.log(YARN_ANCHOR / (2.0 * math.pi)) / (2.0 * log_theta)), rotary - 1
    )
    spread = float(upper - lower)
    index = jnp.arange(half, dtype=jnp.float32)
    plain_frequency = jnp.exp(index * (-2.0 * log_theta / rotary))
    keep = 1.0 - jnp.clip((index - lower) / spread, 0.0, 1.0)
    frequency = plain_frequency * keep + plain_frequency / YARN_FACTOR * (1.0 - keep)
    angles = positions.astype(jnp.float32)[:, None] * frequency[None, :]
    attention_factor = 0.1 * math.log(YARN_FACTOR) + 1.0
    return (jnp.cos(angles) * attention_factor, jnp.sin(angles) * attention_factor)


def rotate(values, cosines, sines, rotary):
    half = rotary // 2
    first = values[..., :half]
    second = values[..., half:rotary]
    cosines = cosines[:, None, :]
    sines = sines[:, None, :]
    return jnp.concatenate(
        [first * cosines - second * sines, second * cosines + first * sines, values[..., rotary:]],
        axis=-1,
    )


def request_starts(req_len):
    order = jnp.arange(req_len.shape[0], dtype=jnp.int32)
    return jnp.sum(jnp.where(order[:, None] < order[None, :], req_len[:, None], 0), axis=0)


def row_layout(rows, req_len, req_prefix, req_offset):
    starts = request_starts(req_len)
    leading_found = (starts[None, :] <= rows[:, None]).astype(jnp.int32)
    segment = jnp.sum(leading_found, axis=1) - 1
    choose = (segment[:, None] == jnp.arange(req_len.shape[0], dtype=jnp.int32)[None, :]).astype(
        jnp.int32
    )
    first = jnp.sum(choose * starts[None, :], axis=1)
    prefix = jnp.sum(choose * req_prefix[None, :], axis=1)
    offset = jnp.sum(choose * req_offset[None, :], axis=1)
    return (segment, first, prefix, offset, offset + rows - first)


def product2(a, exact):
    rows = a.shape[0]
    both = dot1(jnp.concatenate(halves(a), axis=0), exact)
    return both[:rows] + both[rows:]


def product3(left, right):
    rows = left[0].shape[0]
    both = dot1(jnp.concatenate(left, axis=0), right[0])
    return both[:rows] + (both[rows:] + dot1(left[0], right[1]))


def turn(angle):
    quarter = jnp.floor(angle * (2.0 / math.pi) + 0.5)
    rest = angle - quarter * 1.5703125
    rest = rest - quarter * 4.837512969970703125e-4
    rest = rest - quarter * 7.54978995489188216e-8
    square = rest * rest
    sine = rest + rest * square * (
        (-1.9515295891e-4 * square + 8.3321608736e-3) * square - 1.6666654611e-1
    )
    cosine = (
        1.0
        - 0.5 * square
        + square
        * square
        * ((2.443315711809948e-5 * square - 1.388731625493765e-3) * square + 4.166664568298827e-2)
    )
    which = quarter.astype(jnp.int32) & 3
    odd = (which & 1) == 1
    cos_part = jnp.where(odd, sine, cosine)
    sin_part = jnp.where(odd, cosine, sine)
    cos_part = jnp.where((which == 1) | (which == 2), -cos_part, cos_part)
    sin_part = jnp.where(which >= 2, -sin_part, sin_part)
    return cos_part, sin_part


def lane_tables(position):
    half = ROT // 2
    log_theta = math.log(ROPE_THETA)
    lower = max(math.floor(ROT * math.log(YARN_ANCHOR / (64.0 * math.pi)) / (2.0 * log_theta)), 0)
    upper = min(
        math.ceil(ROT * math.log(YARN_ANCHOR / (2.0 * math.pi)) / (2.0 * log_theta)), ROT - 1
    )
    lane = lax.broadcasted_iota(jnp.int32, (1, 128), 1)
    index = (lane % half).astype(jnp.float32)
    plain = jnp.exp(index * (-2.0 * log_theta / ROT))
    keep = 1.0 - jnp.clip((index - lower) / float(upper - lower), 0.0, 1.0)
    frequency = plain * keep + plain / YARN_FACTOR * (1.0 - keep)
    cosine, sine = turn(position.astype(jnp.float32) * frequency)
    factor = 0.1 * math.log(YARN_FACTOR) + 1.0
    cosine = jnp.where(lane < ROT, cosine * factor, 1.0)
    sine = jnp.where(lane < half, -sine * factor, jnp.where(lane < ROT, sine * factor, 0.0))
    return cosine, sine


def roped(front, cosines, sines):
    lane = lax.broadcasted_iota(jnp.int32, front.shape, 1)
    swapped = jnp.where(
        lane < ROT // 2, pltpu.roll(front, 128 - ROT // 2, 1), pltpu.roll(front, ROT // 2, 1)
    )
    return front * cosines + swapped * sines


def fused_kernel(
    size, span,
    query_hbm, key_hbm, value_hbm, gate_hbm, logit_hbm, decay_hbm, gain_hbm, state_hbm,
    atq_hbm, atg_hbm, atk_hbm, atv_hbm, pk_hbm, pv_hbm,
    len_ref, prefix_ref, offset_ref, table_ref,
    dn_out_ref, at_out_ref,
    query_ref, key_ref, value_ref, gate_ref, logit_ref, decay_ref, gain_ref, atq_ref, atg_ref, raw_ref,
    states, cached, fresh,
    local_ref, reach_ref, map_ref, add_ref, held, leaving, bias_ref,
    load_sem, st_send, st_recv, ck_send, ck_recv, nk_send, nk_recv, sib_send, sib_recv,
    chain_send, chain_recv, fw_send, factor_ref,
):
    me = lax.axis_index("context")
    head_at = lax.axis_index("head")
    tokens = query_ref.shape[0]
    heads = local_ref.shape[0]
    share = VH // KH
    prefixes = states.shape[1]
    width = cached.shape[3]
    part = tokens // 2
    lane_half = lax.rem(head_at, 2)
    sibling = head_at + 1 - 2 * lane_half
    kv_head = lax.div(head_at, 2)

    barrier = pltpu.get_barrier_semaphore()
    for step in range(1, size):
        pl.semaphore_signal(
            barrier, inc=1, device_id={"context": lax.rem(me + step, size)}
        )
    pl.semaphore_signal(barrier, inc=1, device_id={"head": sibling})

    columns = pl.ds(pl.multiple_of(kv_head * HD, HD), HD)
    loads = [
        (state_hbm, states.at[me]),
        (atk_hbm.at[:, columns], raw_ref),
        (atv_hbm.at[pl.ds(0, part), columns], fresh.at[1, 0, 0]),
        (atv_hbm.at[pl.ds(part, part), columns], fresh.at[1, 0, 1]),
        (pk_hbm.at[0, :, columns], cached.at[0, me, 0]),
        (pk_hbm.at[1, :, columns], cached.at[0, me, 1]),
        (pv_hbm.at[0, :, columns], cached.at[1, me, 0]),
        (pv_hbm.at[1, :, columns], cached.at[1, me, 1]),
        (decay_hbm, decay_ref),
        (logit_hbm, logit_ref),
        (key_hbm, key_ref),
        (query_hbm, query_ref),
        (value_hbm, value_ref),
        (atq_hbm, atq_ref),
        (atg_hbm, atg_ref),
        (gate_hbm, gate_ref),
        (gain_hbm, gain_ref),
    ]
    loads = [
        pltpu.make_async_copy(source, target, load_sem.at[i])
        for i, (source, target) in enumerate(loads)
    ]
    for load in loads:
        load.start()

    groups = st_send.shape[2]
    group_heads = heads // groups

    def right_ok(s):
        return (me >= s) & (me < size - 1)

    def left_ok(s):
        return (me + s < size) & (me > 0)

    def st_copy(way, s, g, arriving):
        step = 1 if way == 0 else -1
        owner = lax.rem(me - step * (s + (1 if arriving else 0)) + 2 * size, size)
        ref = states.at[owner, :, pl.ds(g * group_heads, group_heads)]
        return pltpu.make_async_remote_copy(
            src_ref=ref, dst_ref=ref,
            send_sem=st_send.at[way, s, g], recv_sem=st_recv.at[way, s, g],
            device_id={"context": lax.rem(me + step + size, size)},
        )

    def state_start(s, g):
        for way, ok in ((0, right_ok), (1, left_ok)):

            @pl.when(ok(s)[0])
            def _(way=way):
                st_copy(way, s, g, False).start()

    def state_arrive(s, g):
        for way, ok in ((0, right_ok), (1, left_ok)):

            @pl.when(ok(s)[1])
            def _(way=way):
                st_copy(way, s, g, True).wait_recv()

    def ck_copy(step, arriving):
        owner = lax.rem(me - step + size, size) if arriving else me
        ref = cached.at[:, owner, lane_half]
        return pltpu.make_async_remote_copy(
            src_ref=ref, dst_ref=ref,
            send_sem=ck_send.at[step - 1], recv_sem=ck_recv.at[step - 1],
            device_id={"context": lax.rem(me + step, size)},
        )

    def nk_copy(step):
        return pltpu.make_async_remote_copy(
            src_ref=fresh.at[:, 0, lane_half], dst_ref=fresh.at[:, step, lane_half],
            send_sem=nk_send.at[step - 1], recv_sem=nk_recv.at[step - 1],
            device_id={"context": lax.rem(me + step, size)},
        )

    def sib_ck(step, arriving):
        owner = lax.rem(me - step + size, size)
        ref = cached.at[:, owner, 1 - lane_half if arriving else lane_half]
        return pltpu.make_async_remote_copy(
            src_ref=ref, dst_ref=ref,
            send_sem=sib_send.at[0, step - 1], recv_sem=sib_recv.at[0, step - 1],
            device_id={"head": sibling},
        )

    def sib_nk(step, arriving):
        ref = fresh.at[:, step, 1 - lane_half if arriving else lane_half]
        return pltpu.make_async_remote_copy(
            src_ref=ref, dst_ref=ref,
            send_sem=sib_send.at[1, step - 1], recv_sem=sib_recv.at[1, step - 1],
            device_id={"head": sibling},
        )

    def chain_copy(h):
        return pltpu.make_async_remote_copy(
            src_ref=leaving.at[h], dst_ref=held.at[h],
            send_sem=chain_send.at[h], recv_sem=chain_recv.at[h],
            device_id={"context": lax.rem(me + 1, size)},
        )

    def state_own(g):
        for way, ok in ((0, right_ok), (1, left_ok)):

            @pl.when(ok(0))
            def _(way=way):
                st_copy(way, 0, g, False).start()

    def state_forward(s, g):
        for way, ok in ((0, right_ok), (1, left_ok)):

            @pl.when(ok(s))
            def _(way=way):
                st_copy(way, s - 1, g, True).wait_recv()
                st_copy(way, s, g, False).start()

    def state_end(g):
        for way, end in ((0, size - 1), (1, 0)):

            @pl.when(me == end)
            def _(way=way):
                for s in range(size - 1):
                    st_copy(way, s, g, True).wait_recv()

    def kv_start(step):
        ck_copy(step, False).start()
        if step <= span:

            @pl.when(me + step < size)
            def _():
                nk_copy(step).start()

    def relayed(step):
        return (me + step == size - 1) & (step > 1)

    def ck_onward(owner):
        ref = cached.at[:, owner, lane_half]
        return pltpu.make_async_remote_copy(
            src_ref=ref, dst_ref=ref,
            send_sem=fw_send.at[0, owner], recv_sem=ck_recv.at[size - 2 - owner],
            device_id={"context": size - 1},
        )

    def nk_onward(owner):
        far = size - 1 - owner
        return pltpu.make_async_remote_copy(
            src_ref=fresh.at[:, far - 1, lane_half], dst_ref=fresh.at[:, far, lane_half],
            send_sem=fw_send.at[1, owner], recv_sem=nk_recv.at[far - 1],
            device_id={"context": size - 1},
        )

    def kv_onward(owner):
        @pl.when(me == size - 2)
        def _():
            near = size - 2 - owner
            ck_copy(near, True).wait_recv()
            ck_onward(owner).start()
            sib_ck(near, False).start()
            if near <= span:
                nk_copy(near).wait_recv()
                sib_nk(near, False).start()
            if near + 1 <= span:
                nk_onward(owner).start()

    def kv_side(rightward):
        for step in range(1, size):
            here = me + step < size if rightward else me + step >= size

            @pl.when(here & jnp.logical_not(relayed(step)))
            def _(step=step):
                kv_start(step)

    def kv_share():
        for step in range(1, size):

            @pl.when((me != size - 2) | (step > me))
            def _(step=step):
                ck_copy(step, True).wait_recv()
                sib_ck(step, False).start()
                if step <= span:

                    @pl.when(me >= step)
                    def _():
                        nk_copy(step).wait_recv()
                        sib_nk(step, False).start()

    def kv_arrive():
        for step in range(1, size):
            sib_ck(step, True).wait_recv()
            if step <= span:

                @pl.when(me >= step)
                def _(step=step):
                    sib_nk(step, True).wait_recv()

    loads[0].wait()
    pl.semaphore_wait(barrier, size)
    for g in range(groups):
        state_own(g)

    row_start = me * tokens
    last_row = row_start + tokens - 1
    requests = len_ref.shape[0]
    starts, total = [], jnp.int32(0)
    for r in range(requests):
        starts.append(total)
        total = total + len_ref[r]

    def layout(rows):
        seg = jnp.zeros_like(rows)
        for r in range(1, requests):
            seg = seg + (rows >= starts[r]).astype(jnp.int32)
        return seg

    rows = row_start + lax.broadcasted_iota(jnp.int32, (tokens, 1), 0)
    seg = layout(rows)
    first, prefix, offset = [jnp.zeros_like(rows)] * 3
    tail_first, tail_prefix, head_seg = jnp.int32(0), prefix_ref[0], jnp.int32(0)
    head_first = jnp.int32(0)
    for r in range(requests):
        first = jnp.where(seg == r, starts[r], first)
        prefix = jnp.where(seg == r, prefix_ref[r], prefix)
        offset = jnp.where(seg == r, offset_ref[r], offset)
        tail_first = jnp.where(starts[r] <= last_row, starts[r], tail_first)
        tail_prefix = jnp.where(starts[r] <= last_row, prefix_ref[r], tail_prefix)
        head_first = jnp.where(starts[r] <= row_start, starts[r], head_first)
        head_seg = jnp.where(starts[r] <= row_start, r, head_seg)
    restarts = tail_first >= row_start
    carried = (seg == head_seg) & (first < row_start)
    row_lane = lax.broadcasted_iota(jnp.int32, (1, tokens), 1)
    seg_row = layout(row_start + row_lane)
    cosines, sines = lane_tables(offset + rows - first)

    for load in loads[1:2]:
        load.wait()
    for j in range(2):
        piece = pl.ds(j * part, part)
        cut = slice(j * part, (j + 1) * part)
        fresh[0, 0, j, :, 0:128] = roped(
            raw_ref[piece, 0:128].astype(jnp.float32), cosines[cut], sines[cut]
        ).astype(jnp.bfloat16)
        fresh[0, 0, j, :, 128:HD] = raw_ref[piece, 128:HD]

    for load in loads[2:8]:
        load.wait()
    kv_side(True)

    for step in range(1, span + 1):

        @pl.when(me < step)
        def _(step=step):
            fresh[:, step] = jnp.zeros_like(fresh[:, step])

    @pl.when(me == 0)
    def _():
        held[...] = jnp.zeros_like(held)

    slots = size * 2
    lanes = lax.broadcasted_iota(jnp.int32, (1, slots * width), 1)
    slot, inside = lanes // width, lanes % width
    per_prefix = table_ref.shape[0] // prefixes
    code, place = jnp.zeros_like(lanes), jnp.zeros_like(lanes)
    for e in range(table_ref.shape[0]):
        here = slot == table_ref[e]
        code = jnp.where(here, e // per_prefix, code)
        place = jnp.where(here, e % per_prefix * width + inside, place)
    bias_ref[:, : slots * width] = jnp.where(
        (code == prefix) & (place < offset), 0.0, NEG_LARGE
    )
    for step in range(span + 1):
        key_row = row_start - step * tokens + row_lane
        seen = (layout(key_row) == seg) & (key_row <= rows) & (key_row >= 0)
        at = slots * width + step * tokens
        bias_ref[:, at : at + tokens] = jnp.where(seen, 0.0, NEG_LARGE)

    row = lax.broadcasted_iota(jnp.int32, (tokens, tokens), 0)
    col = lax.broadcasted_iota(jnp.int32, (tokens, tokens), 1)
    same = seg == seg_row
    causal = same & (row >= col)
    strict = same & (row > col)
    eye = row == col
    causal_f = causal.astype(jnp.float32)
    for load in loads[8:13]:
        load.wait()
    run_row = lax.dot_general(
        decay_ref[...], causal_f, (((1,), (1,)), ((), ())),
        precision=HIGH, preferred_element_type=jnp.float32,
    )
    beta_row = jax.nn.sigmoid(logit_ref[...])
    tail = seg_row == seg_row[:, tokens - 1 : tokens]
    end_row = jnp.where(
        tail, jnp.exp(jnp.where(tail, run_row[:, tokens - 1 : tokens] - run_row, 0.0)), 0.0
    )
    turned = jnp.concatenate(
        [run_row, beta_row, end_row, jnp.zeros((128 - 3 * heads, tokens), jnp.float32)], axis=0
    ).T
    run, beta = turned[:, :heads], turned[:, heads : 2 * heads]
    end = turned[:, 2 * heads : 3 * heads]
    start, start_row = jnp.exp(run), jnp.exp(run_row)
    keys, turned_keys, grams, mixes, scaled, inv_rows, inv_cols = [], [], [], [], [], [], []
    for g in range(heads // share):
        k = key_ref[:, g * DK : (g + 1) * DK]
        q = query_ref[:, g * DK : (g + 1) * DK]
        gram = dot1(k, k, ((1,), (1,)))
        cross = dot1(q, k, ((1,), (1,)))
        squares = jnp.where(eye, gram, 0.0)
        inv = lax.rsqrt(jnp.sum(squares, axis=1, keepdims=True) + 1e-06)
        inv_row = lax.rsqrt(jnp.sum(squares, axis=0, keepdims=True) + 1e-06)
        q_f = q.astype(jnp.float32)
        inv_q = lax.rsqrt(jnp.sum(q_f * q_f, axis=1, keepdims=True) + 1e-06) * DK ** (-0.5)
        keys.append(k)
        turned_keys.append(k.T)
        inv_rows.append(inv_row)
        inv_cols.append(inv)
        grams.append(gram * inv * inv_row)
        mixes.append(cross * inv_q * inv_row)
        scaled.append(q_f * inv_q)
    lowers, inverses, mixing = [], [], []
    for h in range(heads):
        gaps = run[:, h : h + 1] - run_row[h : h + 1, :]
        decay_mat = jnp.where(causal, jnp.exp(jnp.where(causal, gaps, 0.0)), 0.0)
        mixing.append(decay_mat * mixes[h // share])
        lower = jnp.where(strict, beta[:, h : h + 1] * grams[h // share] * decay_mat, 0.0)
        lowers.append(lower)
        inverses.append(
            jnp.where(eye, 1.0, 0.0) - jnp.where((row >> 1) == (col >> 1), lower, 0.0)
        )
    plan = {5: 0, 7: 1, 9: 2, 11: 3}
    ticks = [0]

    def tick():
        if ticks[0] in plan and size > 2:
            state_forward(1, plan[ticks[0]])
        ticks[0] += 1

    splits = [halves(lowers[h]) for h in range(heads)]
    parts = [halves(inverses[h]) for h in range(heads)]
    depth, level = 2, 1
    while depth < tokens:
        pair = ((row >> (level + 1)) == (col >> (level + 1))) & ((row >> level) > (col >> level))
        if depth < 16:
            picks = [(0, tokens)]
        else:
            picks = [(at, depth) for at in range(depth, tokens, 2 * depth)]

        def rows_of(x):
            cuts = [x[at : at + count] for at, count in picks]
            return cuts[0] if len(cuts) == 1 else jnp.concatenate(cuts, axis=0)

        def spread(x):
            if depth < 16:
                return x
            out = []
            for i in range(len(picks)):
                out.append(jnp.zeros((depth, tokens), x.dtype))
                out.append(x[i * depth : (i + 1) * depth])
            return jnp.concatenate(out, axis=0)

        mask = rows_of(pair.astype(jnp.float32)).astype(jnp.bfloat16)
        half = []
        for h in range(heads):
            left = [rows_of(s) * mask for s in splits[h]]
            half.append(product3(left, parts[h]))
        tick()
        for h in range(heads):
            left = [rows_of(p) for p in parts[h]]
            right = tuple(spread(p) for p in halves(half[h]))
            fixed = rows_of(inverses[h]) - product3(left, right)
            if depth < 16:
                inverses[h], parts[h] = fixed, halves(fixed)
            else:
                high, low = halves(fixed)
                whole_f, whole_high, whole_low = [], [], []
                for i, (at, count) in enumerate(picks):
                    cut = slice(i * count, (i + 1) * count)
                    for out, old, now in (
                        (whole_f, inverses[h], fixed),
                        (whole_high, parts[h][0], high),
                        (whole_low, parts[h][1], low),
                    ):
                        out.append(old[at - count : at])
                        out.append(now[cut])
                inverses[h] = jnp.concatenate(whole_f, axis=0)
                parts[h] = (
                    jnp.concatenate(whole_high, axis=0), jnp.concatenate(whole_low, axis=0)
                )
        tick()
        depth, level = depth * 2, level + 1
    weighted = [inverses[h] * beta_row[h : h + 1, :] for h in range(heads)]
    update = [product2(weighted[h], value_ref[:, h * DV : (h + 1) * DV]) for h in range(heads)]
    wy = [
        product2(weighted[h] * (start_row[h : h + 1, :] * inv_rows[h // share]), keys[h // share])
        for h in range(heads)
    ]
    tick()
    solved = [jnp.concatenate([update[h], wy[h]], axis=1) for h in range(heads)]
    carries = []
    for h in range(heads):
        high, low = halves(solved[h] * (end[:, h : h + 1] * inv_cols[h // share]))
        twice = jnp.concatenate([turned_keys[h // share]] * 2, axis=1)
        carries.append(dot1(twice, jnp.concatenate([high, low], axis=0)))
    tick()
    mixed = []
    for h in range(heads):
        mixed.append(product3(halves(mixing[h]), halves(solved[h])))
    tick()
    for h in range(heads):
        add_ref[h] = carries[h][:, :DV]
        map_ref[h] = (
            jnp.where(eye, start[tokens - 1 : tokens, h : h + 1], 0.0) - carries[h][:, DV:]
        ).astype(jnp.bfloat16)
        local_ref[h] = mixed[h][:, :DV]
        reach_ref[h] = (start[:, h : h + 1] * scaled[h // share] - mixed[h][:, DV:]).astype(
            jnp.bfloat16
        )
    for load in loads[13:]:
        load.wait()

    query_heads = atq_ref.shape[1] // HD
    for h in range(query_heads):
        cut = slice(h * HD, h * HD + 128)
        front = roped(atq_ref[:, cut].astype(jnp.float32), cosines, sines)
        front = front.astype(jnp.bfloat16).astype(jnp.float32)
        rear = atq_ref[:, h * HD + 128 : (h + 1) * HD].astype(jnp.float32)
        atq_ref[:, h * HD : (h + 1) * HD] = (
            jnp.concatenate([front, rear], axis=1) * HD ** (-0.5)
        ).astype(jnp.bfloat16)

    def attend():
        kv_arrive()
        old_keys = cached[0].reshape(-1, HD)
        old_values = cached[1].reshape(-1, HD)
        new_keys = fresh[0].reshape(-1, HD)
        new_values = fresh[1].reshape(-1, HD)
        old_bias, new_bias = bias_ref[:, : slots * width], bias_ref[:, slots * width :]
        for pair in range(0, query_heads, 4):
            these = range(pair, min(pair + 4, query_heads))
            queries = [atq_ref[:, h * HD : (h + 1) * HD] for h in these]
            old = [dot1(query, old_keys, ((1,), (1,))) + old_bias for query in queries]
            new = [dot1(query, new_keys, ((1,), (1,))) + new_bias for query in queries]
            peaks = [
                jnp.maximum(jnp.max(o, axis=1, keepdims=True), jnp.max(n, axis=1, keepdims=True))
                for o, n in zip(old, new)
            ]
            old = [jnp.exp(o - peak) for o, peak in zip(old, peaks)]
            new = [jnp.exp(n - peak) for n, peak in zip(new, peaks)]
            wholes = [
                jnp.sum(o, axis=1, keepdims=True) + jnp.sum(n, axis=1, keepdims=True)
                for o, n in zip(old, new)
            ]
            summed = [
                dot1(o.astype(jnp.bfloat16), old_values) + dot1(n.astype(jnp.bfloat16), new_values)
                for o, n in zip(old, new)
            ]
            for i, h in enumerate(these):
                gate = atg_ref[:, h * HD : (h + 1) * HD].astype(jnp.float32)
                at_out_ref[:, h * HD : (h + 1) * HD] = (
                    summed[i] / wholes[i] * jax.nn.sigmoid(gate)
                ).astype(jnp.bfloat16)

    def state_of(p, h):
        return jnp.concatenate([states[o, p, h] for o in range(size)], axis=0)

    def from_prefixes(these):
        own = [(prefix == p) & ~carried for p in range(prefixes)]
        for h in these:
            whole_states = [state_of(p, h) for p in range(prefixes)]
            base = whole_states[0]
            for p in range(1, prefixes):
                base = jnp.where(tail_prefix == p, whole_states[p], base)
            opened = dot1(map_ref[h], base, ((1,), (1,)))
            parts = dot1(reach_ref[h], jnp.concatenate(whole_states, axis=0), ((1,), (1,)))
            core = local_ref[h]
            for p in range(prefixes):
                core = core + jnp.where(own[p], parts[:, p * DV : (p + 1) * DV], 0.0)
            local_ref[h] = core
            gate = gate_ref[:, h * DV : (h + 1) * DV].astype(jnp.float32)
            factor_ref[h] = gain_ref[...] * (gate * jax.nn.sigmoid(gate))
            add_ref[h] = add_ref[h] + jnp.where(restarts, opened, 0.0)

    for owner in range(size - 3, -1, -1):
        kv_onward(owner)
    for g in range(groups):
        for s in range(2, size - 1):
            state_forward(s, g)
    kv_side(False)
    @pl.when(me == size - 1)
    def _():
        kv_share()
        attend()

    for g in range(groups):
        these = range(g * group_heads, (g + 1) * group_heads)
        state_end(g)
        from_prefixes(these)

        @pl.when(me == 0)
        def _(these=these):
            for h in these:
                leaving[h] = add_ref[h].astype(jnp.bfloat16)
                chain_copy(h).start()


    for h in range(heads):

        @pl.when(me > 0)
        def _(h=h):
            chain_copy(h).wait_recv()

        @pl.when((me > 0) & (me < size - 1))
        def _(h=h):
            onward = dot1(map_ref[h], held[h])
            leaving[h] = (add_ref[h] + jnp.where(restarts, 0.0, onward)).astype(jnp.bfloat16)
            chain_copy(h).start()

        core = local_ref[h] + jnp.where(carried, dot1(reach_ref[h], held[h]), 0.0)
        normed = core * lax.rsqrt(jnp.mean(core * core, axis=1, keepdims=True) + 1e-06)
        dn_out_ref[:, h * DV : (h + 1) * DV] = (normed * factor_ref[h]).astype(jnp.bfloat16)
        if h == heads - 2:

            @pl.when(me < size - 1)
            def _():
                kv_share()

    @pl.when(me < size - 1)
    def _():
        attend()

    for s in range(size - 1):
        for g in range(groups):
            for way, ok in ((0, right_ok), (1, left_ok)):

                @pl.when(ok(s))
                def _(way=way, s=s, g=g):
                    st_copy(way, s, g, False).wait_send()

    for step in range(1, size):
        sib_ck(step, False).wait_send()

        @pl.when(jnp.logical_not(relayed(step)))
        def _(step=step):
            ck_copy(step, False).wait_send()
            if step <= span:

                @pl.when(me + step < size)
                def _():
                    nk_copy(step).wait_send()

        if step <= span:

            @pl.when(me >= step)
            def _(step=step):
                sib_nk(step, False).wait_send()

    @pl.when(me == size - 2)
    def _():
        for owner in range(size - 2):
            ck_onward(owner).wait_send()
            if size - 1 - owner <= span:
                nk_onward(owner).wait_send()

    @pl.when(me < size - 1)
    def _():
        for h in range(heads):
            chain_copy(h).wait_send()


def hand_out_kernel(dn_ref, at_ref, dn_out_ref, at_out_ref, held, load_sem, store_sem):
    rows = dn_ref.shape[0] // 2
    loads, stores = [], []
    for i in range(2):
        cut = pl.ds(i * rows, rows)
        for j, (source, target) in enumerate(((dn_ref, dn_out_ref), (at_ref, at_out_ref))):
            loads.append(pltpu.make_async_copy(source.at[cut], held.at[j, cut], load_sem.at[i, j]))
            stores.append(pltpu.make_async_copy(held.at[j, cut], target.at[cut], store_sem.at[i, j]))
    for load in loads:
        load.start()
    for load, store in zip(loads, stores):
        load.wait()
        store.start()
    for store in stores:
        store.wait()


def hand_out(dn_out, at_out):
    far = pl.BlockSpec(memory_space=pl.ANY)
    return pl.pallas_call(
        hand_out_kernel,
        out_shape=[
            jax.ShapeDtypeStruct(dn_out.shape, dn_out.dtype),
            jax.ShapeDtypeStruct(at_out.shape, at_out.dtype),
        ],
        in_specs=[far, far],
        out_specs=[far, far],
        scratch_shapes=[
            pltpu.VMEM((2,) + dn_out.shape, dn_out.dtype),
            pltpu.SemaphoreType.DMA((2, 2)),
            pltpu.SemaphoreType.DMA((2, 2)),
        ],
        compiler_params=pltpu.CompilerParams(vmem_limit_bytes=60 * 2**20),
    )(dn_out, at_out)


def fits_fused(tokens, query_heads, prefix_state, prefix_key):
    size = lax.axis_size("context")
    return (
        tokens == 128
        and size <= 4
        and prefix_state.shape[2] % 16 == 0
        and prefix_key.shape[0] == 2
        and prefix_key.shape[1] % 16 == 0
        and HQ // KVH == 2 * query_heads
    )


def fused(
    dn_query, dn_key, dn_value, dn_gate, dn_beta_logit, dn_decay, dn_norm_gain,
    prefix_state, at_query, at_gate, at_key, at_value, prefix_key, prefix_value,
    req_len, req_prefix, req_offset, block_table,
):
    size = lax.axis_size("context")
    tokens = dn_query.shape[0]
    heads = dn_value.shape[1] // DV
    prefixes, _, state_rows, _ = prefix_state.shape
    width = prefix_key.shape[1]
    longest = size * tokens // 2
    span = min(size - 1, (longest - 1 + tokens - 1) // tokens)
    groups = 4
    bf16, f32 = jnp.bfloat16, jnp.float32
    far = pl.BlockSpec(memory_space=pl.ANY)
    near = pl.BlockSpec(memory_space=pltpu.VMEM)
    small = pl.BlockSpec(memory_space=pltpu.SMEM)
    keys_seen = size * 2 * width + (span + 1) * tokens
    dma = pltpu.SemaphoreType.DMA
    dn_out, at_out = pl.pallas_call(
        lambda *refs: fused_kernel(size, span, *refs),
        out_shape=[
            jax.ShapeDtypeStruct(dn_gate.shape, bf16),
            jax.ShapeDtypeStruct(at_query.shape, bf16),
        ],
        in_specs=[far] * 14 + [small] * 4,
        out_specs=[near, near],
        scratch_shapes=[
            pltpu.VMEM(dn_query.shape, bf16),
            pltpu.VMEM(dn_key.shape, bf16),
            pltpu.VMEM(dn_value.shape, bf16),
            pltpu.VMEM(dn_gate.shape, bf16),
            pltpu.VMEM((heads, tokens), f32),
            pltpu.VMEM((heads, tokens), f32),
            pltpu.VMEM((1, DV), f32),
            pltpu.VMEM(at_query.shape, bf16),
            pltpu.VMEM(at_gate.shape, bf16),
            pltpu.VMEM((tokens, HD), bf16),
            pltpu.VMEM((size, prefixes, heads, state_rows, DK), bf16),
            pltpu.VMEM((2, size, 2, width, HD), bf16),
            pltpu.VMEM((2, span + 1, 2, tokens // 2, HD), bf16),
            pltpu.VMEM((heads, tokens, DV), f32),
            pltpu.VMEM((heads, tokens, DK), bf16),
            pltpu.VMEM((heads, DK, DK), bf16),
            pltpu.VMEM((heads, DV, DK), f32),
            pltpu.VMEM((heads, DV, DK), bf16),
            pltpu.VMEM((heads, DV, DK), bf16),
            pltpu.VMEM((tokens, keys_seen), f32),
            dma((17,)),
            dma((2, size - 1, groups)),
            dma((2, size - 1, groups)),
            dma((size - 1,)),
            dma((size - 1,)),
            dma((span,)),
            dma((span,)),
            dma((2, size - 1)),
            dma((2, size - 1)),
            dma((heads,)),
            dma((heads,)),
            dma((2, size)),
            pltpu.VMEM((heads, tokens, DV), f32),
        ],
        compiler_params=pltpu.CompilerParams(
            collective_id=2, has_side_effects=True, vmem_limit_bytes=60 * 2**20
        ),
    )(
        dn_query, dn_key, dn_value, dn_gate, dn_beta_logit.T, dn_decay.T, dn_norm_gain[None, :],
        prefix_state, at_query, at_gate, at_key, at_value, prefix_key, prefix_value,
        req_len, req_prefix, req_offset, block_table,
    )
    return hand_out(dn_out, at_out)


def shards(
    dn_query,
    dn_key,
    dn_value,
    dn_gate,
    dn_beta_logit,
    dn_decay,
    dn_norm_gain,
    prefix_state,
    at_query,
    at_gate,
    at_key,
    at_value,
    prefix_key,
    prefix_value,
    req_len,
    req_prefix,
    req_offset,
    block_table,
):
    tokens_here = dn_query.shape[0]
    value_heads = dn_value.shape[1] // DV
    query_heads = at_query.shape[1] // HD
    if fits_fused(tokens_here, query_heads, prefix_state, prefix_key):
        return fused(
            dn_query, dn_key, dn_value, dn_gate, dn_beta_logit, dn_decay, dn_norm_gain,
            prefix_state, at_query, at_gate, at_key, at_value, prefix_key, prefix_value,
            req_len, req_prefix, req_offset, block_table,
        )
    device = lax.axis_index("context")
    row_start = device * tokens_here
    rows = row_start + jnp.arange(tokens_here, dtype=jnp.int32)
    segment, first, prefix, offset, position = row_layout(rows, req_len, req_prefix, req_offset)
    size = lax.axis_size("context")
    query_heads_here = query_heads
    kv_head = lax.axis_index("head") * query_heads_here // (HQ // KVH)
    cosines, sines = yarn_tables(position, ROT)
    new_key = lax.dynamic_slice_in_dim(at_key, kv_head * HD, HD, 1).reshape(tokens_here, 1, HD)
    new_key = (
        rotate(new_key.astype(jnp.float32), cosines, sines, ROT)
        .reshape(tokens_here, HD)
        .astype(jnp.bfloat16)
    )
    new_value = lax.dynamic_slice_in_dim(at_value, kv_head * HD, HD, 1)
    cached_key = lax.dynamic_slice_in_dim(prefix_key, kv_head * HD, HD, 2)
    cached_value = lax.dynamic_slice_in_dim(prefix_value, kv_head * HD, HD, 2)
    states = jnp.stack([prefix_state] + from_others(prefix_state, "context", size, size))
    states = jnp.concatenate([states[::-1]] * 2)
    states = lax.dynamic_slice_in_dim(states, size - 1 - device, size, 0)
    states = jnp.moveaxis(states, 0, 2)
    states = states.reshape(states.shape[:2] + (-1, DK))
    slots_here = cached_key.shape[0]
    own_block = jnp.concatenate(
        [cached_key.reshape(-1, HD), new_key, cached_value.reshape(-1, HD), new_value]
    ).reshape(2, -1, HD)
    block_rows = own_block.shape[1]
    sharers = HQ // KVH // query_heads
    share = block_rows // sharers
    share_index = lax.axis_index("head") % sharers
    mine = lax.dynamic_slice_in_dim(own_block, share_index * share, share, 1)
    received = jnp.stack(from_others(mine, "context", size, size))
    siblings = from_others(received, "head", lax.axis_size("head"), sharers)
    cached_rows = cached_key.shape[0] * cached_key.shape[1]
    square = (value_heads, DK, DK)
    local_out, reach, map_half, carry_add = whole_call(
        local_kernel,
        [
            jax.ShapeDtypeStruct((value_heads, tokens_here, DV), jnp.float32),
            jax.ShapeDtypeStruct((value_heads, tokens_here, DK), jnp.bfloat16),
            jax.ShapeDtypeStruct(square, jnp.bfloat16),
            jax.ShapeDtypeStruct(square, jnp.float32),
        ],
        dn_query,
        dn_key,
        dn_value,
        dn_beta_logit,
        dn_beta_logit.T,
        dn_decay,
        dn_decay.T,
        segment[:, None],
        segment[None, :],
    )
    restarts = first[tokens_here - 1] >= row_start
    tail_prefix = prefix[tokens_here - 1]
    base = jnp.zeros(states.shape[1:], states.dtype)
    for owner in range(states.shape[0]):
        base = jnp.where(tail_prefix == owner, states[owner], base)
    fresh = jnp.einsum("hvj,hjk->hvk", base, map_half, preferred_element_type=jnp.float32)
    into_state = chain(
        jnp.where(restarts, 0, map_half).astype(jnp.bfloat16),
        carry_add + jnp.where(restarts, fresh, 0.0),
        size,
    )
    carried = (segment == segment[0]) & (first[0] < row_start)
    owner_ids = jnp.arange(states.shape[0], dtype=jnp.int32)
    select = (prefix[None, :] == owner_ids[:, None]) & ~carried[None, :]
    select = jnp.concatenate([select, carried[None, :]], axis=0)
    dn_out = whole_call(
        finish_kernel,
        jax.ShapeDtypeStruct((tokens_here, value_heads * DV), jnp.bfloat16),
        local_out,
        reach,
        states,
        into_state,
        select.astype(jnp.float32).T,
        dn_gate,
        dn_norm_gain[None, :],
    )
    blocks_per_prefix = block_table.shape[0] // prefix_state.shape[0]
    width = cached_key.shape[1]
    others = (device - 1 - jnp.arange(size - 1, dtype=jnp.int32)) % size
    origins = [jnp.full((block_rows,), device, jnp.int32)]
    parts = [jnp.arange(block_rows, dtype=jnp.int32)]
    for step in range(sharers):
        origins.append(jnp.repeat(others, share))
        parts.append(
            (share_index - step) % sharers * share
            + jnp.tile(jnp.arange(share, dtype=jnp.int32), size - 1)
        )
    origin, part = jnp.concatenate(origins), jnp.concatenate(parts)
    slot = origin * slots_here + part // width
    entry = jnp.sum(
        jnp.where(
            block_table[:, None] == slot[None, :],
            jnp.arange(block_table.shape[0], dtype=jnp.int32)[:, None],
            0,
        ),
        axis=0,
    )
    key_row = origin * tokens_here + part - cached_rows
    starts = request_starts(req_len)
    key_segment = jnp.sum((starts[:, None] <= key_row[None, :]).astype(jnp.int32), axis=0) - 1
    old = part < cached_rows
    prefixes = prefix_state.shape[0]
    code = jnp.where(old, entry // blocks_per_prefix, prefixes + key_segment)
    place = jnp.where(old, entry % blocks_per_prefix * width + part % width, key_row)
    ones = jnp.ones((tokens_here, 128 - ROT), jnp.float32)
    at_out = whole_call(
        attend_kernel,
        jax.ShapeDtypeStruct((tokens_here, query_heads * HD), jnp.bfloat16),
        at_query,
        jnp.concatenate([cosines, cosines, ones], axis=1),
        jnp.concatenate([-sines, sines, 0.0 * ones], axis=1),
        at_gate,
        jnp.stack([prefix, offset, prefixes + segment, rows], axis=1),
        code[None, :],
        place[None, :],
        own_block,
        received,
        *siblings,
    )
    return (dn_out, at_out)


def solution(mesh):
    placed = (
        P(("group", "context"), "head"),
        P(("group", "context"), "head"),
        P(("group", "context"), "head"),
        P(("group", "context"), "head"),
        P(("group", "context"), "head"),
        P(("group", "context"), "head"),
        P(),
        P("group", "head", "context", None),
        P(("group", "context"), "head"),
        P(("group", "context"), "head"),
        P(("group", "context"), None),
        P(("group", "context"), None),
        P(("group", "context"), None, None),
        P(("group", "context"), None, None),
        P("group"),
        P("group"),
        P("group"),
        P("group"),
    )
    return jax.shard_map(
        shards,
        mesh=mesh,
        in_specs=placed,
        out_specs=(P(("group", "context"), "head"), P(("group", "context"), "head")),
        check_vma=False,
    )
```
